32 devices in a mesh: groups: 2 (over x), seq: 8 (over z, y), pipe: 2 (over core).
Axes of the slice: x: 2, y: 2, z: 4, core: 2. Of those that a mesh axis runs over, the one named last changes fastest.
Arguments:
- tokens: bfloat16 [2, 2048, 1440], P('pipe', ('groups', 'seq')), parts along dimension 1, may hold values from -6 to 6
- routes: int32 [2, 2048, 4], P('pipe', ('groups', 'seq')), parts along dimension 1, may hold values from 0 to 15, all different within a row; in each aligned block of 128 rows (0 to 127, 128 to 255, ..., all dimensions but the last counted through in order) at most 48 rows name the same one
- route_weights: float32 [2, 2048, 4], P('pipe', ('groups', 'seq')), parts along dimension 1, may hold values from 0.1 to 1
- moe_gain: float32 [1440], replicated, may hold values from 0.5 to 1.5
- gate_up: bfloat16 [32, 1440, 1440], P('seq'), may hold values from -0.15625 to 0.15625
- down_proj: bfloat16 [32, 720, 1440], P('seq'), may hold values from -0.15625 to 0.15625
- attn_gain: float32 [1440], replicated, may hold values from 0.5 to 1.5
- qkv_proj: bfloat16 [1440, 2560], P('seq'), may hold values from -0.15625 to 0.15625
- head_sink_logits: float32 [32], replicated, may hold values from 3 to 6
- out_proj: bfloat16 [2048, 1440], P('seq'), may hold values from -0.125 to 0.125
Outputs:
- layer_output: bfloat16 [2, 2048, 1440], P('pipe', ('groups', 'seq')), parts along dimension 1
The draws below stay inside these ranges and needn't reach their ends.
There are 2 independent parts, one for each index of `groups`. The reference program is written for one: setup_inputs(seed, part) draws one part's arguments, and reference() takes and returns one part's arrays. A program takes and returns all parts, laid end to end along the dimension named above; an argument that names none is the same for every part. Nothing has to cross between parts.
Inputs may be any that keep to these rules, and one draw needn't show every extreme that they name: `routes`: within the 128 positions of one micro-batch on one index of seq, a token names each of its 4 experts once, and each expert is named by at most 48 tokens; one expert is named by exactly 48 of them.
All inputs are finite; a program needn't handle non-finite values.
Results may differ from the reference program's by a relative error of at most 0.0085.
Values may be sent and summed in bfloat16 or wider, within the bound.
A program may use at most 128 MiB of HBM per device.

```python
import math
import jax
import jax.numpy as jnp
import numpy as np
from jax import lax

D = 1440
E = 16
H = 1440
TOP = 4
QUERY_HEADS = 32
KEY_VALUE_HEADS = 4
HEAD_SIZE = 64
WINDOW_SPAN = 128
TOK_DEV = 128
HALF = 720
SLABS = 32
CAP = 48
MB = 2
TOKENS = 1024
QKV = 2560
N_SEQ = 8


def shard_levels(stream_key, extent, shards, least, top_value):
    def one(position, shards_of):
        steps = jax.random.uniform(jax.random.fold_in(jax.random.fold_in(stream_key, 6), position), (shards_of,), jnp.float32, least / len(shards), top_value / len(shards))
        return jnp.repeat(jnp.exp(steps), extent[position] // shards_of).reshape((-1,) + (1,) * (len(extent) - position - 1))

    loudness = one(*shards[0])
    for cut in shards[1:]:
        loudness = loudness * one(*cut)
    return loudness


def deal_out(key, own, number, rows, amount, top, most, lean):
    sequence = jax.random.permutation(key, amount)
    packed, usual = load_shares(amount, rows * top, most, lean, True), load_shares(amount, rows * top, most, lean, False)
    places = jnp.arange(amount)

    def named(sizes, rotation):
        used = int((sizes > 0).sum())
        fixed = max(1, used // 4)
        moved = fixed + (places - fixed + rotation * (used - fixed)) % max(1, amount - fixed)
        return jnp.zeros((amount,), jnp.int32).at[sequence[jnp.where(places < fixed, places, moved)]].set(jnp.asarray(sizes, jnp.int32))

    sizes = jnp.where(number % 4 == 0, named(packed, number // 4), named(usual, number - number // 4 - 1))
    mixed = jax.random.permutation(jax.random.fold_in(own, 3), amount)
    source_of, sink = mixed[0:amount // 2 * 2:2], mixed[1:amount // 2 * 2:2]
    slack = jnp.minimum(sizes[source_of] - 1, most - sizes[sink]) // 2
    slack = jnp.where((source_of == sequence[0]) | (sink == sequence[0]) | (sizes[sink] == 0), 0, jnp.maximum(slack, 0))
    moved = jax.random.randint(jax.random.fold_in(own, 4), (amount // 2,), 0, 1 << 20) % (slack + 1)
    sizes = sizes.at[source_of].add(-moved).at[sink].add(moved)
    items = jnp.searchsorted(jnp.cumsum(sizes), jnp.arange(rows * top), side="right").astype(jnp.int32)
    grid = items.reshape(top, rows).T
    grid = grid[jax.random.permutation(jax.random.fold_in(own, 1), rows)]
    rotation = jax.random.randint(jax.random.fold_in(own, 2), (rows, 1), 0, top)
    return jnp.take_along_axis(grid, (jnp.arange(top)[None, :] + rotation) % top, axis=1)


def load_shares(amount, total, bound, slope, full):
    loads = [(1 << 20) // math.isqrt(grade ** slope) + 1 for grade in range(1, amount + 1)]
    largest = bound if full else min(bound, max(-(-total // amount), total * loads[0] // sum(loads)))
    least = 1 if total - largest >= amount - 1 else 0
    counts, spare = [largest] + [least] * (amount - 1), total - largest - least * (amount - 1)
    while spare > 0:
        free = [i for i in range(1, amount) if counts[i] < largest] or [i for i in range(1, amount) if counts[i] < bound]
        pool, remaining = sum([loads[i] for i in free]), spare
        for i in free:
            addition = min(bound - counts[i], max(1, remaining * loads[i] // pool), spare)
            counts[i] = counts[i] + addition
            spare = spare - addition
    return np.array(counts)


def centred(rng, dims, width, most, shards=(), kind=jnp.bfloat16):
    loudness = shard_levels(rng, dims, shards, -0.22, 0.18) if shards else 1.0
    entries = jax.random.normal(rng, dims, jnp.float32) * width * loudness
    return jnp.minimum(jnp.maximum(entries, -most), most).astype(kind)


def setup_inputs(seed: int = 0, part: int = 0) -> dict:
    keys = jax.random.split(jax.random.key(seed), 11)
    own_keys = jax.random.split(jax.random.fold_in(keys[10], part), 11)
    tokens = centred(own_keys[0], (MB, TOKENS, D), 1.0, 6.0, ((0, 2), (1, 8)))
    routes_keys = jax.random.split(jax.random.fold_in(own_keys[1], 1), MB * TOKENS // TOK_DEV)
    routes_turns = jax.random.permutation(jax.random.fold_in(own_keys[1], 3), MB * TOKENS // TOK_DEV)
    routes = jax.vmap(lambda own, number: deal_out(jax.random.fold_in(own_keys[1], 2), own, number, TOK_DEV, E, TOP, CAP, 2))(routes_keys, routes_turns).reshape((MB, TOKENS, TOP))
    route_weights = jnp.clip(0.1 + 0.9 * jax.random.uniform(own_keys[2], (MB, TOKENS, TOP), jnp.float32) ** shard_levels(own_keys[2], (MB, TOKENS, TOP), ((0, 2), (1, 8)), -0.2, 0.2), 0.1, 1.0)
    moe_gain = jnp.clip(1.0 + 0.1 * jax.random.normal(keys[3], (D,), jnp.float32), 0.5, 1.5)
    gate_up = centred(keys[4], (SLABS, D, 2 * HALF), D ** -0.5, 0.15625, ((0, 8),))
    down_proj = centred(keys[5], (SLABS, HALF, D), H ** -0.5, 0.15625, ((0, 8),))
    attn_gain = jnp.clip(1.0 + 0.1 * jax.random.normal(keys[6], (D,), jnp.float32), 0.5, 1.5)
    qkv_proj = centred(keys[7], (D, QKV), D ** -0.5, 0.15625, ((0, 8),))
    head_sink_logits = jnp.clip(jax.random.uniform(keys[8], (QUERY_HEADS,), jnp.float32, 3.0, 6.0), 3.0, 6.0)
    out_proj = centred(keys[9], (QUERY_HEADS * HEAD_SIZE, D), (QUERY_HEADS * HEAD_SIZE) ** -0.5, 0.125, ((0, 8),))
    return {"tokens": tokens, "routes": routes, "route_weights": route_weights, "moe_gain": moe_gain, "gate_up": gate_up, "down_proj": down_proj, "attn_gain": attn_gain, "qkv_proj": qkv_proj, "head_sink_logits": head_sink_logits, "out_proj": out_proj}


eps = 1e-05

def rms_scale(value_matrix, gain):
    widened = value_matrix.astype(jnp.float32)
    mean_square = lax.optimization_barrier(jnp.mean(widened * widened, axis=-1, keepdims=True))
    return (widened * lax.rsqrt(mean_square + eps) * gain).astype(jnp.bfloat16)

def slot_positions(route_rows):
    flat = route_rows.reshape(-1).astype(jnp.int32)
    onehot = (flat[:, None] == jnp.arange(E, dtype=jnp.int32)[None, :]).astype(jnp.int32)
    earlier = jnp.cumsum(onehot, axis=0) - onehot
    return (flat * CAP + lax.optimization_barrier(jnp.sum(earlier * onehot, axis=1))).astype(jnp.int32)

def expert_apply(items):
    rows, pair_gate_up, pair_down = items
    gate_matrix = jnp.concatenate([pair_gate_up[0][:, :HALF], pair_gate_up[1][:, :HALF]], axis=1)
    up_matrix = jnp.concatenate([pair_gate_up[0][:, HALF:], pair_gate_up[1][:, HALF:]], axis=1)
    down_matrix = jnp.concatenate([pair_down[0], pair_down[1]], axis=0)
    gate = jnp.dot(rows, gate_matrix, preferred_element_type=jnp.float32)
    upper = jnp.dot(rows, up_matrix, preferred_element_type=jnp.float32)
    hidden = (gate * jax.nn.sigmoid(1.702 * gate) * (upper + 1.0)).astype(jnp.bfloat16)
    return jnp.dot(hidden, down_matrix, preferred_element_type=jnp.float32).astype(jnp.bfloat16)

def dispatch_block(items):
    rows, route_rows = items
    positions = slot_positions(route_rows)
    source = jnp.repeat(rows, TOP, axis=0)
    table = jnp.zeros((E * CAP, D), jnp.bfloat16).at[positions].set(source)
    return (table, positions)

def pick_rows(results, positions):
    return results[positions]

def moe_block(tokens_mb, routes_mb, weights_mb, moe_gain, gate_up, down_proj):
    normed = rms_scale(tokens_mb, moe_gain)
    blocks = normed.reshape(N_SEQ, TOK_DEV, D)
    route_blocks = routes_mb.reshape(N_SEQ, TOK_DEV, TOP)
    tables, positions = lax.map(dispatch_block, (blocks, route_blocks))
    per_expert = tables.reshape(N_SEQ, E, CAP, D).transpose(1, 0, 2, 3).reshape(E, N_SEQ * CAP, D)
    results = lax.map(expert_apply, (per_expert, gate_up.reshape(E, 2, D, 2 * HALF), down_proj.reshape(E, 2, HALF, D)))
    results = results.reshape(E, N_SEQ, CAP, D).transpose(1, 0, 2, 3).reshape(N_SEQ, E * CAP, D)
    picked = jax.vmap(pick_rows)(results, positions)
    picked = picked.reshape(TOKENS, TOP, D).astype(jnp.float32)
    summed = tokens_mb.astype(jnp.float32) + lax.optimization_barrier(jnp.sum(picked * weights_mb[:, :, None], axis=1))
    return summed.astype(jnp.bfloat16)

def attention_all(hidden_all, attn_gain, qkv_proj, head_sink_logits, out_proj):
    length = hidden_all.shape[0]
    query_groups = QUERY_HEADS // KEY_VALUE_HEADS
    normed = rms_scale(hidden_all, attn_gain)
    packed_heads = lax.optimization_barrier(jnp.dot(normed, qkv_proj, preferred_element_type=jnp.float32).astype(jnp.bfloat16)).astype(jnp.float32)
    query_matrix = packed_heads[:, :QUERY_HEADS * HEAD_SIZE]
    key_matrix = packed_heads[:, QUERY_HEADS * HEAD_SIZE:(QUERY_HEADS + KEY_VALUE_HEADS) * HEAD_SIZE]
    value_matrix = packed_heads[:, (QUERY_HEADS + KEY_VALUE_HEADS) * HEAD_SIZE:]
    padding_rows = jnp.zeros((WINDOW_SPAN, KEY_VALUE_HEADS * HEAD_SIZE), jnp.float32)
    keys_extended = jnp.concatenate([padding_rows, key_matrix], axis=0)
    values_extended = jnp.concatenate([padding_rows, value_matrix], axis=0)
    scale = float(HEAD_SIZE) ** (-0.5)
    sink_mass_total = jnp.exp(head_sink_logits).reshape(KEY_VALUE_HEADS, query_groups, 1, 1)

    def one_block(index):
        start_position = (index * WINDOW_SPAN).astype(jnp.int32)
        rows_of_queries = lax.dynamic_slice_in_dim(query_matrix, start_position, WINDOW_SPAN, 0).reshape(WINDOW_SPAN, KEY_VALUE_HEADS, query_groups, HEAD_SIZE)
        rows_of_keys = lax.dynamic_slice_in_dim(keys_extended, start_position, 2 * WINDOW_SPAN, 0).reshape(2 * WINDOW_SPAN, KEY_VALUE_HEADS, HEAD_SIZE)
        rows_of_values = lax.dynamic_slice_in_dim(values_extended, start_position, 2 * WINDOW_SPAN, 0).reshape(2 * WINDOW_SPAN, KEY_VALUE_HEADS, HEAD_SIZE)
        scores = jnp.einsum('qhgd,khd->hgqk', rows_of_queries, rows_of_keys) * scale
        query_pos = start_position + jnp.arange(WINDOW_SPAN, dtype=jnp.int32)
        key_pos = start_position - WINDOW_SPAN + jnp.arange(2 * WINDOW_SPAN, dtype=jnp.int32)
        distance = query_pos[:, None] - key_pos[None, :]
        allowed = (distance >= 0) & (distance < WINDOW_SPAN) & (key_pos[None, :] >= 0)
        weights = jnp.where(allowed, jnp.exp(scores), 0.0)
        total = lax.optimization_barrier(jnp.sum(weights, axis=-1, keepdims=True)) + sink_mass_total
        probs = lax.optimization_barrier((weights / total).astype(jnp.bfloat16)).astype(jnp.float32)
        mixed = jnp.einsum('hgqk,khd->qhgd', probs, rows_of_values)
        return mixed.reshape(WINDOW_SPAN, QUERY_HEADS * HEAD_SIZE).astype(jnp.bfloat16)
    attended = lax.map(one_block, jnp.arange(length // WINDOW_SPAN, dtype=jnp.int32)).reshape(length, QUERY_HEADS * HEAD_SIZE)
    projected = jnp.dot(attended, out_proj, preferred_element_type=jnp.float32)
    return (hidden_all.astype(jnp.float32) + projected).astype(jnp.bfloat16)

def reference(tokens, routes, route_weights, moe_gain, gate_up, down_proj, attn_gain, qkv_proj, head_sink_logits, out_proj):
    sections = []
    for index in range(MB):
        sections.append(moe_block(tokens[index], routes[index], route_weights[index], moe_gain, gate_up, down_proj))
    whole = jnp.stack(sections).reshape(MB * TOKENS, D)
    result = attention_all(whole, attn_gain, qkv_proj, head_sink_logits, out_proj)
    return result.reshape(MB, TOKENS, D)
```

```python
import functools

import jax
import jax.numpy as jnp
from jax import lax
from jax.experimental import pallas as pl
from jax.experimental.pallas import tpu as pltpu
from jax.sharding import PartitionSpec as P

MESH = pl.DeviceIdType.MESH
E = 16
TOP = 4
QUERY_HEADS = 32
KEY_VALUE_HEADS = 4
HEAD_SIZE = 64
WINDOW_SPAN = 128
HALF = 720
CAP = 48


eps = 1e-05


def from_partner(value, axis, distance):
    return lax.ppermute(value, axis, [(i, i ^ 1 << distance) for i in range(lax.axis_size(axis))])


def shifted(value, axis, steps):
    count = lax.axis_size(axis)
    pairs = [(source, (source + steps) % count) for source in range(count)]
    return lax.ppermute(value, axis, pairs)


def passed_along(value, axis, steps):
    count = lax.axis_size(axis)
    first, last = (max(0, -steps), min(count, count - steps))
    return lax.ppermute(value, axis, [(source, source + steps) for source in range(first, last)])


def rms_scale(value_matrix, gain):
    widened = value_matrix.astype(jnp.float32)
    mean_square = jnp.mean(widened * widened, axis=-1, keepdims=True)
    return (widened * lax.rsqrt(mean_square + eps) * gain).astype(jnp.bfloat16)


def slot_positions(route_rows):
    flat = route_rows.reshape(-1)
    onehot = (flat[:, None] == jnp.arange(E, dtype=jnp.int32)[None, :]).astype(jnp.int32)
    earlier = jnp.cumsum(onehot, axis=0) - onehot
    return flat * CAP + jnp.sum(earlier * onehot, axis=1)


def expert_layer(local, route_rows, route_scale, moe_gain, gate_up, down_proj):
    tok_count, width = local.shape
    seq_count = lax.axis_size("seq")
    per_device = gate_up.shape[0]
    normed = rms_scale(local, moe_gain)
    positions = slot_positions(route_rows)
    select = (positions[None, :] == jnp.arange(E * CAP, dtype=jnp.int32)[:, None]).astype(
        jnp.bfloat16
    )
    repeated = jnp.repeat(normed, TOP, axis=0)
    table = jnp.dot(select, repeated, preferred_element_type=jnp.float32).astype(jnp.bfloat16)
    by_expert = table.reshape(E, CAP, width)
    first = lax.axis_index("seq") % 2 == 0
    outgoing = jnp.repeat(by_expert, 2, axis=0).reshape(seq_count, per_device, CAP, width)
    received = lax.all_to_all(outgoing, "seq", split_axis=0, concat_axis=0, tiled=True)
    projected = jnp.einsum("spcd,pdh->spch", received, gate_up, preferred_element_type=jnp.float32)
    gate_part = projected[..., :HALF]
    up_part = projected[..., HALF:]
    hidden = (gate_part * jax.nn.sigmoid(1.702 * gate_part) * (up_part + 1.0)).astype(jnp.bfloat16)
    partial_value = jnp.einsum(
        "spch,phd->spcd", hidden, down_proj, preferred_element_type=jnp.float32
    )
    if per_device >= 2:
        finished = (
            partial_value.reshape(seq_count, per_device // 2, 2, CAP, width)
            .sum(axis=2)
            .astype(jnp.bfloat16)
        )
    else:
        lower_rows = partial_value[:, :, : CAP // 2]
        upper_rows = partial_value[:, :, CAP // 2 :]
        kept = jnp.where(first, lower_rows, upper_rows)
        given = jnp.where(first, upper_rows, lower_rows)
        partner_part = from_partner(given.astype(jnp.bfloat16), "seq", 0).astype(given.dtype)
        finished = (kept + partner_part).astype(jnp.bfloat16)
    summed = lax.all_to_all(finished, "seq", split_axis=0, concat_axis=0, tiled=True).reshape(
        E * CAP, width
    )
    picked = lax.dot_general(
        select, summed, (((0,), (0,)), ((), ())), preferred_element_type=jnp.float32
    )
    weighted = jnp.sum(picked.reshape(tok_count, TOP, width) * route_scale[:, :, None], axis=1)
    return (local.astype(jnp.float32) + weighted).astype(jnp.bfloat16)


def attend(query_matrix, keys_extended, values_extended, head_sink_logits, halo_valid):
    tok_count = query_matrix.shape[0]
    query_groups = QUERY_HEADS // KEY_VALUE_HEADS
    attention_block = min(tok_count, 512)
    scale = float(HEAD_SIZE) ** (-0.5)
    sink_mass_total = jnp.exp(head_sink_logits).reshape(KEY_VALUE_HEADS, query_groups, 1, 1)
    block_queries = query_matrix.reshape(attention_block, KEY_VALUE_HEADS, query_groups, HEAD_SIZE)
    block_keys = keys_extended.reshape(attention_block + WINDOW_SPAN, KEY_VALUE_HEADS, HEAD_SIZE)
    block_values = values_extended.reshape(
        attention_block + WINDOW_SPAN, KEY_VALUE_HEADS, HEAD_SIZE
    )
    scores = (
        jnp.einsum("qhgd,khd->hgqk", block_queries, block_keys, preferred_element_type=jnp.float32)
        * scale
    )
    query_pos = jnp.arange(attention_block, dtype=jnp.int32)[:, None] + WINDOW_SPAN
    key_pos = jnp.arange(attention_block + WINDOW_SPAN, dtype=jnp.int32)[None, :]
    distance = query_pos - key_pos
    allowed = (
        (distance >= 0) & (distance < WINDOW_SPAN) & ((key_pos + 0 >= WINDOW_SPAN) | halo_valid)
    )
    weights = jnp.where(allowed, jnp.exp(scores), 0.0)
    probs = (weights / (jnp.sum(weights, axis=-1, keepdims=True) + sink_mass_total)).astype(
        jnp.bfloat16
    )
    mixed = jnp.einsum("hgqk,khd->qhgd", probs, block_values, preferred_element_type=jnp.float32)
    outputs = mixed.reshape(attention_block, QUERY_HEADS * HEAD_SIZE).astype(jnp.bfloat16)
    return outputs


def body(
    tokens,
    routes,
    route_weights,
    moe_gain,
    gate_up,
    down_proj,
    attn_gain,
    qkv_proj,
    head_sink_logits,
    out_proj,
):
    hidden = expert_layer(tokens[0], routes[0], route_weights[0], moe_gain, gate_up, down_proj)
    tok_count, width = hidden.shape
    normed = rms_scale(hidden, attn_gain)
    seq_index = lax.axis_index("seq")
    pipe_index = lax.axis_index("pipe")
    halo_valid = (seq_index > 0) | (pipe_index > 0)
    query_width = QUERY_HEADS * HEAD_SIZE
    width_of_pair = KEY_VALUE_HEADS * HEAD_SIZE
    columns = normed
    packed_heads = jnp.dot(
        columns,
        lax.all_gather(qkv_proj, "seq", axis=0, tiled=True),
        preferred_element_type=jnp.float32,
    ).astype(jnp.bfloat16)
    from_left = shifted(packed_heads[tok_count - WINDOW_SPAN :, query_width:], "seq", 1)
    from_section = passed_along(from_left, "pipe", 1)
    halo_pairs = jnp.where(seq_index == 0, from_section, from_left)
    query_matrix = packed_heads[:, :query_width]
    pairs_ext = jnp.concatenate([halo_pairs, packed_heads[:, query_width:]], axis=0)
    keys_extended = pairs_ext[:, :width_of_pair]
    values_extended = pairs_ext[:, width_of_pair:]
    attended = attend(query_matrix, keys_extended, values_extended, head_sink_logits, halo_valid)
    columns = attended
    projected = jnp.dot(
        columns,
        lax.all_gather(out_proj, "seq", axis=0, tiled=True),
        preferred_element_type=jnp.float32,
    )
    return (hidden.astype(jnp.float32) + projected).astype(jnp.bfloat16)[None]


def ring_place(index, count, folded):
    if not folded:
        return index
    line, side = index // 2, index % 2
    return line + side * (count - 1 - 2 * line)

def ring_index(place, count, folded):
    if not folded:
        return place
    side = place // (count // 2)
    line = place + side * (count - 1 - 2 * place)
    return 2 * line + side


def copy_to(src, dst, send, recv, **device):
    return pltpu.make_async_remote_copy(src_ref=src, dst_ref=dst, send_sem=send, recv_sem=recv,
        device_id=device, device_id_type=MESH)


def dot(a, b, dims=((1,), (0,))):
    return lax.dot_general(a, b, (dims, ((), ())), preferred_element_type=jnp.float32)


def layer_kernel(
    tok_t_ref, tok_ref, routes_ref, weights_ref, gain_ref, attn_gain_ref, sink_ref,
    gate_up_ref, down_ref, qkv_ref, out_t_ref,
    out_ref,
    blocks, picked, combine, gu, dn, proj, act, done, parts, held, wq, wo,
    both, kv, halo, queries, mixed, given, back,
    gu_sem, dn_sem, wq_sem, wo_sem, ag_s, ag_r, rs_s, rs_r, q_s, q_r, qx_s, qx_r,
    o_s, o_r, ox_s, ox_r, pair_s, pair_r, halo_s, halo_r,
):
    count = lax.axis_size("seq")
    steps = count // 2
    me = lax.axis_index("seq")
    core = lax.axis_index("pipe")
    group = lax.axis_index("groups")
    width, tok_count = tok_t_ref.shape
    own = picked.shape[0]
    slots = own * CAP
    place = ring_place(me, count, True)
    at = lambda offset: ring_index(lax.rem(place + offset + count, count), count, True)
    peers = (at(1), at(-1))
    following, preceding = lax.rem(me + 1, count), lax.rem(me + count - 1, count)
    other_core, other_group = 1 - core, 1 - group
    sends = []

    def launch(copy):
        copy.start()
        sends.append((None, copy))
        return copy

    qw, kw = queries.shape[2], kv.shape[2] // 2
    all_q = QUERY_HEADS * HEAD_SIZE
    all_k = KEY_VALUE_HEADS * HEAD_SIZE
    wo_slot = lax.rem(me, steps)
    holds = lambda origin: lax.div(origin, steps) == core
    wo_copy = pltpu.make_async_copy(out_t_ref, wo.at[wo_slot], wo_sem.at[0])

    @pl.when(holds(me))
    def _():
        wo_copy.start()

    wq_copies = []
    for i, (source, goal, size) in enumerate((
        (all_q + core * kw, 0, kw), (all_q + all_k + core * kw, kw, kw), (core * qw, 2 * kw, qw))):
        wq_copies.append(pltpu.make_async_copy(
            qkv_ref.at[:, pl.ds(pl.multiple_of(source, 128), size)],
            wq.at[me, :, pl.ds(goal, size)], wq_sem.at[i]))
    for copy in wq_copies:
        copy.start()
    gu_copies = [pltpu.make_async_copy(gate_up_ref.at[j], gu.at[j], gu_sem.at[j]) for j in range(2 * own)]
    dn_copies = [pltpu.make_async_copy(down_ref.at[j], dn.at[j], dn_sem.at[j]) for j in range(2 * own)]
    for copy in gu_copies + dn_copies:
        copy.start()

    tall = tok_t_ref[...].astype(jnp.float32)
    scale = lax.rsqrt(jnp.sum(tall * tall, axis=0, keepdims=True) / width + eps)
    for i in range(0, width, 128):
        size = min(128, width - i)
        blocks[me, i : i + size, :] = (
            tok_t_ref[i : i + size, :].astype(jnp.float32) * scale * gain_ref[:size, i // 128 : i // 128 + 1]
        ).astype(jnp.bfloat16)
    expert_row = lax.broadcasted_iota(jnp.int32, (E, tok_count), 0)
    dense = jnp.zeros((E, tok_count), jnp.float32)
    for j in range(TOP):
        dense = dense + jnp.where(expert_row == routes_ref[j : j + 1, :], weights_ref[j : j + 1, :], 0.0)
    blocks[me, width : width + E, :] = dense.astype(jnp.bfloat16)

    barrier = pltpu.get_barrier_semaphore()
    for device in ({"seq": peers[0]}, {"seq": peers[1]}, {"seq": following}, {"seq": preceding},
                   {"pipe": other_core}, {"groups": other_group}):
        pl.semaphore_signal(barrier, inc=1, device_id=device, device_id_type=MESH)
    pl.semaphore_wait(barrier, 6)

    rows_all = blocks.shape[1]
    cut = (rows_all // 2 + 15) // 16 * 16
    pieces = (pl.ds(0, cut), pl.ds(cut, rows_all - cut))
    ag = {}

    def ag_send(way, step, piece):
        origin = at(-step if way == 0 else step)
        ref = blocks.at[origin, pieces[piece]]
        ag[way, step, piece] = launch(copy_to(ref, ref, ag_s.at[way, step, piece], ag_r.at[way, step, piece], seq=peers[way]))

    qcols = wq.shape[2] // 2
    qcut = (qcols // 2 + 127) // 128 * 128
    q = {}
    qx = {}

    def q_part(way, step):
        base = pl.multiple_of(group * qcols, 128)
        if step < steps - 1:
            return pl.ds(base, qcols)
        return pl.ds(base, qcut) if way == 0 else pl.ds(base + qcut, qcols - qcut)

    def q_send(way, step):
        ref = wq.at[at(-step if way == 0 else step), :, q_part(way, step)]
        q[way, step] = launch(copy_to(ref, ref, q_s.at[way, step], q_r.at[way, step], seq=peers[way]))

    def q_cross(way, step):
        q[way, step].wait_recv()
        ref = wq.at[at(-step - 1 if way == 0 else step + 1), :, q_part(way, step)]
        qx[way, step] = launch(copy_to(ref, ref, qx_s.at[way, step], qx_r.at[way, step], groups=other_group))

    def q_begin():
        for copy in wq_copies:
            copy.wait()
        for way in (0, 1):
            q_send(way, 0)

    def q_step(step):
        for way in (0, 1):
            q_cross(way, step - 1)
            if step < steps:
                q_send(way, step)

    orows = wo.shape[1] // 2
    ocut = (orows // 2 + 15) // 16 * 16
    o_sends = []

    def o_part(way, step):
        base = pl.multiple_of(group * orows, 16)
        if step < steps - 1:
            return pl.ds(base, orows)
        return pl.ds(base, ocut) if way == 0 else pl.ds(pl.multiple_of(base + ocut, 16), orows - ocut)

    def o_copy(way, step):
        origin = at(-step if way == 0 else step)
        ref = wo.at[lax.rem(origin, steps), o_part(way, step)]
        return holds(origin), copy_to(ref, ref, o_s.at[way, step], o_r.at[way, step], seq=peers[way])

    def o_landed(way, step):
        origin = at(-step - 1 if way == 0 else step + 1)
        ref = wo.at[lax.rem(origin, steps), o_part(way, step)]
        return (holds(origin), copy_to(ref, ref, o_s.at[way, step], o_r.at[way, step], seq=peers[way]),
                copy_to(ref, ref, ox_s.at[way, step], ox_r.at[way, step], groups=other_group))

    def o_begin():
        @pl.when(holds(me))
        def _():
            wo_copy.wait()
        for way in (0, 1):
            cond, copy = o_copy(way, 0)

            @pl.when(cond)
            def _():
                copy.start()
            o_sends.append((cond, copy))

    def o_step(step):
        for way in (0, 1):
            cond, arrived, crossing = o_landed(way, step - 1)

            @pl.when(cond)
            def _():
                arrived.wait_recv()
                crossing.start()
            o_sends.append((cond, crossing))
            if step < steps:
                onward, copy = o_copy(way, step)

                @pl.when(onward)
                def _():
                    copy.start()
                o_sends.append((onward, copy))

    lane_tok = lax.broadcasted_iota(jnp.int32, (tok_count, tok_count), 1)
    row_tok = lax.broadcasted_iota(jnp.int32, (tok_count, tok_count), 0)
    before = jnp.where(row_tok < lane_tok, 1.0, 0.0).astype(jnp.bfloat16)
    slot_row = lax.broadcasted_iota(jnp.int32, (tok_count, tok_count), 0).astype(jnp.float32)

    def process(n):
        table = blocks[n, width : width + E, :].astype(jnp.float32)
        present = table > 0.0
        earlier = dot(jnp.where(present, 1.0, 0.0).astype(jnp.bfloat16), before)
        slot = jnp.where(present, earlier, -1.0)
        comb = jnp.zeros((tok_count, tok_count), jnp.float32)
        for e in range(own):
            mine = expert_row == me * own + e
            slot_e = jnp.sum(jnp.where(mine, slot, 0.0), axis=0, keepdims=True)
            scale_e = jnp.sum(jnp.where(mine, table, 0.0), axis=0, keepdims=True)
            hit = (slot_row == slot_e + float(e * CAP)) & (slot_e >= 0.0)
            comb = jnp.where(hit, scale_e, comb)
        combine[n] = comb.T.astype(jnp.bfloat16)
        select = jnp.where(comb > 0.0, 1.0, 0.0).astype(jnp.bfloat16)[:slots]
        rows = dot(select, blocks[n, :width, :], ((1,), (1,))).astype(jnp.bfloat16)
        for e in range(own):
            picked[e, n] = rows[e * CAP : (e + 1) * CAP]

    for piece in (0, 1):
        for way in (0, 1):
            ag_send(way, 0, piece ^ way)
    o_begin()
    process(me)
    for step in range(1, steps):
        for piece in (0, 1):
            for way in (0, 1):
                ag[way, step - 1, piece ^ way].wait_recv()
                if step < steps - 1 or piece == 0:
                    ag_send(way, step, piece ^ way)
        o_step(step)
        process(at(-step))
        process(at(step))
    ag[0, steps - 1, 0].wait_recv()
    ag[1, steps - 1, 1].wait_recv()
    process(at(steps))
    o_step(steps)

    q_begin()
    pos = {0: 1, 1: 2, 2: 3, 3: 4}
    half = dn.shape[1]
    chunk = CAP
    for e in range(own):
        for j in (2 * e, 2 * e + 1):
            gu_copies[j].wait()
            x = picked[e].reshape(count * CAP, width)
            proj[...] = dot(x, gu[j])

            @pl.loop(0, count)
            def _(i):
                r = pl.ds(pl.multiple_of(i * chunk, 16), chunk)
                gate = proj[r, :half]
                up = proj[r, half:]
                act[j % 2, r, :] = (gate * jax.nn.sigmoid(1.702 * gate) * (up + 1.0)).astype(jnp.bfloat16)

            if j < steps:
                q_step(j + 1)
        dn_copies[2 * e].wait()
        dn_copies[2 * e + 1].wait()
        result = dot(act[0], dn[2 * e]) + dot(act[1], dn[2 * e + 1])
        done[:, e * CAP : (e + 1) * CAP, :] = result.astype(jnp.bfloat16).reshape(count, CAP, width)
    for step in range(2 * own + 1, steps + 1):
        q_step(step)

    def part(n):
        parts[n] = dot(combine[n][:, :slots], done[n]).astype(jnp.bfloat16)

    hrows = tok_count // 2
    lanes = [pl.ds(0, hrows), pl.ds(hrows, hrows)]
    rs = {}

    def rs_send(way, step, piece):
        goal = at((steps - step) * (1 if way == 0 else -1))
        here = lanes[piece]
        if (way, step - 1, piece) in rs:
            rs[way, step - 1, piece].wait_recv()
            held[way, step - 1, here] = (
                held[way, step - 1, here].astype(jnp.float32) + parts[goal, here].astype(jnp.float32)
            ).astype(jnp.bfloat16)
            src = held.at[way, step - 1, here]
        else:
            src = parts.at[goal, here]
        rs[way, step, piece] = launch(copy_to(src, held.at[way, step, here], rs_s.at[way, step, piece], rs_r.at[way, step, piece], seq=peers[way]))

    part(at(steps))
    rs_send(0, 0, 0)
    rs_send(1, 0, 1)
    for way in (0, 1):
        part(at((steps - 1) * (1 if way == 0 else -1)))
        rs_send(way, 1, 1 - way)
    for offset in range(steps - 2, 0, -1):
        part(at(offset))
        part(at(-offset))
    part(me)
    rs_send(0, 1, 0)
    rs_send(1, 1, 1)
    for step in range(2, steps):
        for piece in (0, 1):
            for way in (0, 1):
                rs_send(way, step, 1 ^ piece ^ way)
    for piece in (0, 1):
        for way in (0, 1):
            rs[way, steps - 1, piece].wait_recv()
    summed = (tok_ref[...].astype(jnp.float32) + parts[me].astype(jnp.float32)
        + held[0, steps - 1].astype(jnp.float32) + held[1, steps - 1].astype(jnp.float32)).astype(jnp.bfloat16)
    hidden = summed.astype(jnp.float32)
    scale = lax.rsqrt(jnp.sum(hidden * hidden, axis=1, keepdims=True) / width + eps)
    normed = hidden * scale * attn_gain_ref[...]
    shard = wq.shape[1]
    for i in range(count):
        both[core, i] = normed[:, i * shard : (i + 1) * shard].astype(jnp.bfloat16)
    pair = launch(copy_to(both.at[core], both.at[core], pair_s.at[0], pair_r.at[0], pipe=other_core))

    for key in qx:
        qx[key].wait_recv()
    pair.wait_recv()

    def project(columns):
        total = None
        for i in range(count):
            x = both[:, i].reshape(2 * tok_count, shard)
            term = dot(x, wq[i, :, columns])
            total = term if total is None else total + term
        return total.astype(jnp.bfloat16).reshape(2, tok_count, -1)

    kv[...] = project(pl.ds(0, 2 * kw))
    along = launch(copy_to(kv, halo, halo_s.at[0], halo_r.at[0], seq=following))
    queries[...] = project(pl.ds(2 * kw, qw))
    along.wait_recv()

    lane = lax.broadcasted_iota(jnp.int32, (tok_count, 2 * tok_count), 1)
    row = lax.broadcasted_iota(jnp.int32, (tok_count, 2 * tok_count), 0)
    left = lane < tok_count
    past = jnp.where(left, lane, lane - tok_count) > row
    low = lax.broadcasted_iota(jnp.int32, (tok_count, 2 * HEAD_SIZE), 1) < HEAD_SIZE

    def stacked(tile, head):
        tile = tile.astype(jnp.float32)
        kept = jnp.where(low if head == 0 else ~low, tile, 0.0)
        turned = pltpu.roll(kept, HEAD_SIZE, 1)
        pair_of = (kept, turned) if head == 0 else (turned, kept)
        return jnp.concatenate(pair_of, axis=0).astype(jnp.bfloat16)

    tiles = qw // 128
    per_head = tiles // 2
    for m in range(2):
        source = jnp.where(me == 0, 0, m)
        known = (me > 0) if m == 0 else (me >= 0)
        for head in range(2):
            k_own = stacked(kv[m, :, :kw], head)
            v_own = stacked(kv[m, :, kw:], head)
            k_past = stacked(halo[source, :, :kw], head)
            v_past = stacked(halo[source, :, kw:], head)
            for t in range(head * per_head, (head + 1) * per_head):
                x = queries[m, :, t * 128 : (t + 1) * 128]
                score = jnp.where(past, dot(x, k_past, ((1,), (1,))), dot(x, k_own, ((1,), (1,))))
                weight = jnp.exp(score * (float(HEAD_SIZE) ** -0.5))
                weight = jnp.where(past & jnp.logical_not(known), 0.0, weight)
                mass = jnp.where(left, jnp.sum(weight[:, :tok_count], axis=1, keepdims=True),
                    jnp.sum(weight[:, tok_count:], axis=1, keepdims=True)) + sink_ref[t : t + 1, :]
                probs = weight / mass
                mixed[m, :, t * 128 : (t + 1) * 128] = (
                    dot(jnp.where(past, 0.0, probs).astype(jnp.bfloat16), v_own)
                    + dot(jnp.where(past, probs, 0.0).astype(jnp.bfloat16), v_past)
                ).astype(jnp.bfloat16)

    for way in (0, 1):
        for step in range(steps):
            cond, _, crossing = o_landed(way, step)

            @pl.when(cond)
            def _():
                crossing.wait_recv()

    share = wo.shape[2]

    def output(m):
        total = None
        for i in range(steps):
            term = dot(mixed[m, :, i * share : (i + 1) * share], wo[i], ((1,), (1,)))
            total = term if total is None else total + term
        return total

    given[...] = output(other_core).astype(jnp.bfloat16)
    last = launch(copy_to(given, back, pair_s.at[1], pair_r.at[1], pipe=other_core))
    kept = output(core)
    last.wait_recv()
    out_ref[...] = (hidden + kept + back[...].astype(jnp.float32)).astype(jnp.bfloat16)
    for _, copy in sends:
        copy.wait_send()
    for cond, copy in o_sends:
        @pl.when(cond)
        def _():
            copy.wait_send()


def whole_layer(
    tokens, routes, route_weights, moe_gain, gate_up, down_proj, attn_gain, qkv_proj,
    head_sink_logits, out_proj,
):
    count = lax.axis_size("seq")
    core = lax.axis_index("pipe")
    steps = count // 2
    tok_count, width = tokens.shape[1:]
    own = gate_up.shape[0] // 2
    half = down_proj.shape[1]
    heads = QUERY_HEADS // 2
    qw = heads * HEAD_SIZE
    kw = KEY_VALUE_HEADS * HEAD_SIZE // 2
    tok = tokens[0]
    gain = jnp.pad(moe_gain, (0, -width % 128)).reshape(-1, 128).T
    sinks = jnp.exp(lax.dynamic_slice_in_dim(head_sink_logits, core * heads, heads))
    sinks = jnp.repeat(sinks.reshape(heads // 2, 2), tok_count, axis=1)
    dma = pltpu.SemaphoreType.DMA
    bf16 = jnp.bfloat16
    vm = pl.BlockSpec(memory_space=pltpu.VMEM)
    hbm = pl.BlockSpec(memory_space=pl.ANY)
    out = pl.pallas_call(
        layer_kernel,
        out_shape=jax.ShapeDtypeStruct((tok_count, width), bf16),
        in_specs=[vm] * 7 + [hbm] * 4,
        out_specs=vm,
        scratch_shapes=[
            pltpu.VMEM((count, width + E, tok_count), bf16),
            pltpu.VMEM((own, count, CAP, width), bf16),
            pltpu.VMEM((count, tok_count, tok_count), bf16),
            pltpu.VMEM(gate_up.shape, bf16),
            pltpu.VMEM(down_proj.shape, bf16),
            pltpu.VMEM((count * CAP, 2 * half), jnp.float32),
            pltpu.VMEM((2, count * CAP, half), bf16),
            pltpu.VMEM((count, own * CAP, width), bf16),
            pltpu.VMEM((count, tok_count, width), bf16),
            pltpu.VMEM((2, steps, tok_count, width), bf16),
            pltpu.VMEM((count, qkv_proj.shape[0], 2 * kw + qw), bf16),
            pltpu.VMEM((steps, width, out_proj.shape[0]), bf16),
            pltpu.VMEM((2, count, tok_count, qkv_proj.shape[0]), bf16),
            pltpu.VMEM((2, tok_count, 2 * kw), bf16),
            pltpu.VMEM((2, tok_count, 2 * kw), bf16),
            pltpu.VMEM((2, tok_count, qw), bf16),
            pltpu.VMEM((2, tok_count, qw), bf16),
            pltpu.VMEM((tok_count, width), bf16),
            pltpu.VMEM((tok_count, width), bf16),
            dma((2 * own,)), dma((2 * own,)), dma((3,)), dma((1,)),
            dma((2, steps, 2)), dma((2, steps, 2)), dma((2, steps, 2)), dma((2, steps, 2)),
            dma((2, steps)), dma((2, steps)), dma((2, steps)), dma((2, steps)),
            dma((2, steps)), dma((2, steps)), dma((2, steps)), dma((2, steps)),
            dma((2,)), dma((2,)), dma((1,)), dma((1,)),
        ],
        compiler_params=pltpu.CompilerParams(
            collective_id=0, has_side_effects=True, vmem_limit_bytes=67043328),
    )(tok.T, tok, routes[0].T, route_weights[0].T, gain, attn_gain[None], sinks,
      gate_up, down_proj, qkv_proj, out_proj.T)
    return out[None]


def solution(mesh):
    in_specs = (
        P("pipe", ("groups", "seq"), None),
        P("pipe", ("groups", "seq"), None),
        P("pipe", ("groups", "seq"), None),
        P(),
        P("seq", None, None),
        P("seq", None, None),
        P(),
        P("seq", None),
        P(),
        P("seq", None),
    )
    out_specs = P("pipe", ("groups", "seq"), None)
    seq_count, pipe_count, group_count = mesh.shape["seq"], mesh.shape["pipe"], mesh.shape["groups"]
    whole = (
        pipe_count == 2
        and group_count == 2
        and seq_count % 2 == 0
        and 2 * E // seq_count == 4
        and QUERY_HEADS % (2 * seq_count) == 0
    )
    return jax.shard_map(
        whole_layer if whole else body, mesh=mesh, in_specs=in_specs, out_specs=out_specs, check_vma=False
    )
```

```python
import functools

import jax
import jax.numpy as jnp
from jax import lax
from jax.experimental import pallas as pl
from jax.experimental.pallas import tpu as pltpu
from jax.sharding import PartitionSpec as P

MESH = pl.DeviceIdType.MESH
E = 16
TOP = 4
QUERY_HEADS = 32
KEY_VALUE_HEADS = 4
HEAD_SIZE = 64
WINDOW_SPAN = 128
HALF = 720
CAP = 48


eps = 1e-05


def from_partner(value, axis, distance):
    return lax.ppermute(value, axis, [(i, i ^ 1 << distance) for i in range(lax.axis_size(axis))])


def shifted(value, axis, steps):
    count = lax.axis_size(axis)
    pairs = [(source, (source + steps) % count) for source in range(count)]
    return lax.ppermute(value, axis, pairs)


def passed_along(value, axis, steps):
    count = lax.axis_size(axis)
    first, last = (max(0, -steps), min(count, count - steps))
    return lax.ppermute(value, axis, [(source, source + steps) for source in range(first, last)])


def rms_scale(value_matrix, gain):
    widened = value_matrix.astype(jnp.float32)
    mean_square = jnp.mean(widened * widened, axis=-1, keepdims=True)
    return (widened * lax.rsqrt(mean_square + eps) * gain).astype(jnp.bfloat16)


def slot_positions(route_rows):
    flat = route_rows.reshape(-1)
    onehot = (flat[:, None] == jnp.arange(E, dtype=jnp.int32)[None, :]).astype(jnp.int32)
    earlier = jnp.cumsum(onehot, axis=0) - onehot
    return flat * CAP + jnp.sum(earlier * onehot, axis=1)


def expert_layer(local, route_rows, route_scale, moe_gain, gate_up, down_proj):
    tok_count, width = local.shape
    seq_count = lax.axis_size("seq")
    per_device = gate_up.shape[0]
    normed = rms_scale(local, moe_gain)
    positions = slot_positions(route_rows)
    select = (positions[None, :] == jnp.arange(E * CAP, dtype=jnp.int32)[:, None]).astype(
        jnp.bfloat16
    )
    repeated = jnp.repeat(normed, TOP, axis=0)
    table = jnp.dot(select, repeated, preferred_element_type=jnp.float32).astype(jnp.bfloat16)
    by_expert = table.reshape(E, CAP, width)
    first = lax.axis_index("seq") % 2 == 0
    outgoing = jnp.repeat(by_expert, 2, axis=0).reshape(seq_count, per_device, CAP, width)
    received = lax.all_to_all(outgoing, "seq", split_axis=0, concat_axis=0, tiled=True)
    projected = jnp.einsum("spcd,pdh->spch", received, gate_up, preferred_element_type=jnp.float32)
    gate_part = projected[..., :HALF]
    up_part = projected[..., HALF:]
    hidden = (gate_part * jax.nn.sigmoid(1.702 * gate_part) * (up_part + 1.0)).astype(jnp.bfloat16)
    partial_value = jnp.einsum(
        "spch,phd->spcd", hidden, down_proj, preferred_element_type=jnp.float32
    )
    if per_device >= 2:
        finished = (
            partial_value.reshape(seq_count, per_device // 2, 2, CAP, width)
            .sum(axis=2)
            .astype(jnp.bfloat16)
        )
    else:
        lower_rows = partial_value[:, :, : CAP // 2]
        upper_rows = partial_value[:, :, CAP // 2 :]
        kept = jnp.where(first, lower_rows, upper_rows)
        given = jnp.where(first, upper_rows, lower_rows)
        partner_part = from_partner(given.astype(jnp.bfloat16), "seq", 0).astype(given.dtype)
        finished = (kept + partner_part).astype(jnp.bfloat16)
    summed = lax.all_to_all(finished, "seq", split_axis=0, concat_axis=0, tiled=True).reshape(
        E * CAP, width
    )
    picked = lax.dot_general(
        select, summed, (((0,), (0,)), ((), ())), preferred_element_type=jnp.float32
    )
    weighted = jnp.sum(picked.reshape(tok_count, TOP, width) * route_scale[:, :, None], axis=1)
    return (local.astype(jnp.float32) + weighted).astype(jnp.bfloat16)


def attend(query_matrix, keys_extended, values_extended, head_sink_logits, halo_valid):
    tok_count = query_matrix.shape[0]
    query_groups = QUERY_HEADS // KEY_VALUE_HEADS
    attention_block = min(tok_count, 512)
    scale = float(HEAD_SIZE) ** (-0.5)
    sink_mass_total = jnp.exp(head_sink_logits).reshape(KEY_VALUE_HEADS, query_groups, 1, 1)
    block_queries = query_matrix.reshape(attention_block, KEY_VALUE_HEADS, query_groups, HEAD_SIZE)
    block_keys = keys_extended.reshape(attention_block + WINDOW_SPAN, KEY_VALUE_HEADS, HEAD_SIZE)
    block_values = values_extended.reshape(
        attention_block + WINDOW_SPAN, KEY_VALUE_HEADS, HEAD_SIZE
    )
    scores = (
        jnp.einsum("qhgd,khd->hgqk", block_queries, block_keys, preferred_element_type=jnp.float32)
        * scale
    )
    query_pos = jnp.arange(attention_block, dtype=jnp.int32)[:, None] + WINDOW_SPAN
    key_pos = jnp.arange(attention_block + WINDOW_SPAN, dtype=jnp.int32)[None, :]
    distance = query_pos - key_pos
    allowed = (
        (distance >= 0) & (distance < WINDOW_SPAN) & ((key_pos + 0 >= WINDOW_SPAN) | halo_valid)
    )
    weights = jnp.where(allowed, jnp.exp(scores), 0.0)
    probs = (weights / (jnp.sum(weights, axis=-1, keepdims=True) + sink_mass_total)).astype(
        jnp.bfloat16
    )
    mixed = jnp.einsum("hgqk,khd->qhgd", probs, block_values, preferred_element_type=jnp.float32)
    outputs = mixed.reshape(attention_block, QUERY_HEADS * HEAD_SIZE).astype(jnp.bfloat16)
    return outputs


def body(
    tokens,
    routes,
    route_weights,
    moe_gain,
    gate_up,
    down_proj,
    attn_gain,
    qkv_proj,
    head_sink_logits,
    out_proj,
):
    hidden = expert_layer(tokens[0], routes[0], route_weights[0], moe_gain, gate_up, down_proj)
    tok_count, width = hidden.shape
    normed = rms_scale(hidden, attn_gain)
    seq_index = lax.axis_index("seq")
    pipe_index = lax.axis_index("pipe")
    halo_valid = (seq_index > 0) | (pipe_index > 0)
    query_width = QUERY_HEADS * HEAD_SIZE
    width_of_pair = KEY_VALUE_HEADS * HEAD_SIZE
    columns = normed
    packed_heads = jnp.dot(
        columns,
        lax.all_gather(qkv_proj, "seq", axis=0, tiled=True),
        preferred_element_type=jnp.float32,
    ).astype(jnp.bfloat16)
    from_left = shifted(packed_heads[tok_count - WINDOW_SPAN :, query_width:], "seq", 1)
    from_section = passed_along(from_left, "pipe", 1)
    halo_pairs = jnp.where(seq_index == 0, from_section, from_left)
    query_matrix = packed_heads[:, :query_width]
    pairs_ext = jnp.concatenate([halo_pairs, packed_heads[:, query_width:]], axis=0)
    keys_extended = pairs_ext[:, :width_of_pair]
    values_extended = pairs_ext[:, width_of_pair:]
    attended = attend(query_matrix, keys_extended, values_extended, head_sink_logits, halo_valid)
    columns = attended
    projected = jnp.dot(
        columns,
        lax.all_gather(out_proj, "seq", axis=0, tiled=True),
        preferred_element_type=jnp.float32,
    )
    return (hidden.astype(jnp.float32) + projected).astype(jnp.bfloat16)[None]


def ring_place(index, count, folded):
    if not folded:
        return index
    line, side = index // 2, index % 2
    return line + side * (count - 1 - 2 * line)

def ring_index(place, count, folded):
    if not folded:
        return place
    side = place // (count // 2)
    line = place + side * (count - 1 - 2 * place)
    return 2 * line + side


def copy_to(src, dst, send, recv, **device):
    return pltpu.make_async_remote_copy(src_ref=src, dst_ref=dst, send_sem=send, recv_sem=recv,
        device_id=device, device_id_type=MESH)


def dot(a, b, dims=((1,), (0,))):
    return lax.dot_general(a, b, (dims, ((), ())), preferred_element_type=jnp.float32)


def layer_kernel(
    tok_t_ref, routes_ref, weights_ref, gain_ref, attn_gain_ref, sink_ref,
    gate_up_ref, down_ref, qkv_ref, out_t_ref,
    out_ref,
    blocks, picked, combine, gu, dn, proj, act, done, parts, held, wq, wo,
    both, kv, halo, queries, mixed, given, back, hid, hid_t,
    gu_sem, dn_sem, wq_sem, wo_sem, ag_s, ag_r, rs_s, rs_r, q_s, q_r, qx_s, qx_r,
    o_s, o_r, ox_s, ox_r, late_s, late_r, pair_s, pair_r, halo_s, halo_r,
):
    count = lax.axis_size("seq")
    steps = count // 2
    me = lax.axis_index("seq")
    core = lax.axis_index("pipe")
    group = lax.axis_index("groups")
    width, tok_count = tok_t_ref.shape
    own = picked.shape[0]
    slots = own * CAP
    place = ring_place(me, count, True)
    at = lambda offset: ring_index(lax.rem(place + offset + count, count), count, True)
    peers = (at(1), at(-1))
    following, preceding = lax.rem(me + 1, count), lax.rem(me + count - 1, count)
    other_core, other_group = 1 - core, 1 - group
    sends = []

    def launch(copy):
        copy.start()
        sends.append((None, copy))
        return copy

    qw, kw = queries.shape[2], kv.shape[2] // 2
    all_q = QUERY_HEADS * HEAD_SIZE
    all_k = KEY_VALUE_HEADS * HEAD_SIZE
    wo_slot = lax.rem(me, steps)
    holds = lambda origin: lax.div(origin, steps) == core
    wo_copy = pltpu.make_async_copy(out_t_ref, wo.at[wo_slot], wo_sem.at[0])

    @pl.when(holds(me))
    def _():
        wo_copy.start()

    wq_copies = []
    for i, (source, goal, size) in enumerate((
        (all_q + core * kw, 0, kw), (all_q + all_k + core * kw, kw, kw), (core * qw, 2 * kw, qw))):
        wq_copies.append(pltpu.make_async_copy(
            qkv_ref.at[:, pl.ds(pl.multiple_of(source, 128), size)],
            wq.at[me, :, pl.ds(goal, size)], wq_sem.at[i]))
    for copy in wq_copies:
        copy.start()
    gu_copies = [pltpu.make_async_copy(gate_up_ref.at[j], gu.at[j], gu_sem.at[j]) for j in range(2 * own)]
    dn_copies = [pltpu.make_async_copy(down_ref.at[j], dn.at[j], dn_sem.at[j]) for j in range(2 * own)]
    for copy in gu_copies + dn_copies:
        copy.start()

    tall = tok_t_ref[...].astype(jnp.float32)
    scale = lax.rsqrt(jnp.sum(tall * tall, axis=0, keepdims=True) / width + eps)
    for i in range(0, width, 128):
        size = min(128, width - i)
        gain = jnp.broadcast_to(gain_ref[pl.ds(i, size)].reshape(1, size), (tok_count, size)).T
        blocks[me, i : i + size, :] = (
            tok_t_ref[i : i + size, :].astype(jnp.float32) * scale * gain
        ).astype(jnp.bfloat16)
    expert_row = lax.broadcasted_iota(jnp.int32, (E, tok_count), 0)
    dense = jnp.zeros((E, tok_count), jnp.float32)
    for j in range(TOP):
        dense = dense + jnp.where(expert_row == routes_ref[j : j + 1, :], weights_ref[j : j + 1, :], 0.0)
    blocks[me, width : width + E, :] = dense.astype(jnp.bfloat16)

    barrier = pltpu.get_barrier_semaphore()
    for device in ({"seq": peers[0]}, {"seq": peers[1]}, {"seq": following}, {"seq": preceding},
                   {"pipe": other_core}, {"groups": other_group}):
        pl.semaphore_signal(barrier, inc=1, device_id=device, device_id_type=MESH)
    pl.semaphore_wait(barrier, 6)

    rows_all = blocks.shape[1]
    cut = (rows_all // 2 + 15) // 16 * 16
    pieces = (pl.ds(0, cut), pl.ds(cut, rows_all - cut))
    ag = {}

    def ag_send(way, step, piece):
        origin = at(-step if way == 0 else step)
        ref = blocks.at[origin, pieces[piece]]
        ag[way, step, piece] = launch(copy_to(ref, ref, ag_s.at[way, step, piece], ag_r.at[way, step, piece], seq=peers[way]))

    qcols = wq.shape[2] // 2
    qcut = (qcols // 2 + 127) // 128 * 128
    q = {}
    qx = {}

    def q_part(way, step):
        base = pl.multiple_of(group * qcols, 128)
        if step < steps - 1:
            return pl.ds(base, qcols)
        return pl.ds(base, qcut) if way == 0 else pl.ds(base + qcut, qcols - qcut)

    def q_send(way, step):
        ref = wq.at[at(-step if way == 0 else step), :, q_part(way, step)]
        q[way, step] = launch(copy_to(ref, ref, q_s.at[way, step], q_r.at[way, step], seq=peers[way]))

    def q_cross(way, step):
        q[way, step].wait_recv()
        ref = wq.at[at(-step - 1 if way == 0 else step + 1), :, q_part(way, step)]
        qx[way, step] = launch(copy_to(ref, ref, qx_s.at[way, step], qx_r.at[way, step], groups=other_group))

    def q_begin():
        for copy in wq_copies:
            copy.wait()
        for way in (0, 1):
            q_send(way, 0)

    def q_step(step):
        for way in (0, 1):
            q_cross(way, step - 1)
            if step < steps:
                q_send(way, step)

    orows = wo.shape[1] // 2
    ocut = (orows // 2 + 15) // 16 * 16
    o_sends = []

    def o_part(way, step):
        base = pl.multiple_of(group * orows, 16)
        if step < steps - 1:
            return pl.ds(base, orows)
        return pl.ds(base, ocut) if way == 0 else pl.ds(pl.multiple_of(base + ocut, 16), orows - ocut)

    def o_copy(way, step):
        origin = at(-step if way == 0 else step)
        ref = wo.at[lax.rem(origin, steps), o_part(way, step)]
        return holds(origin), copy_to(ref, ref, o_s.at[way, step], o_r.at[way, step], seq=peers[way])

    def o_landed(way, step):
        origin = at(-step - 1 if way == 0 else step + 1)
        ref = wo.at[lax.rem(origin, steps), o_part(way, step)]
        return (holds(origin), copy_to(ref, ref, o_s.at[way, step], o_r.at[way, step], seq=peers[way]),
                copy_to(ref, ref, ox_s.at[way, step], ox_r.at[way, step], groups=other_group))

    def o_begin():
        @pl.when(holds(me))
        def _():
            wo_copy.wait()
        for way in (0, 1):
            cond, copy = o_copy(way, 0)

            @pl.when(cond)
            def _():
                copy.start()
            o_sends.append((cond, copy))

    near = steps // 2

    def o_step(step):
        for way in (0, 1):
            cond, arrived, crossing = o_landed(way, step - 1)

            @pl.when(cond)
            def _():
                arrived.wait_recv()
                crossing.start()
            o_sends.append((cond, crossing))
            if step < near:
                onward, copy = o_copy(way, step)

                @pl.when(onward)
                def _():
                    copy.start()
                o_sends.append((onward, copy))

    def late_copy(way, step, piece):
        origin = at(-step if way == 0 else step)
        ref = wo.at[lax.rem(origin, steps), pl.ds(piece * orows, orows)]
        index = 2 * (step - near) + (piece ^ way)
        return holds(origin), copy_to(ref, ref, late_s.at[way, index], late_r.at[way, index], seq=peers[way])

    def late_send(step, order):
        for way in (0, 1):
            cond, copy = late_copy(way, step, order ^ way)
            if order == 0:
                if step == near:
                    _, _, before_it = o_landed(way, step - 1)
                    before_it_wait = before_it.wait_recv
                else:
                    origin_cond, before_it = late_landed(way, step - 1, 0)
                    before_it_wait = before_it.wait_recv

                @pl.when(cond)
                def _():
                    before_it_wait()
                    copy.start()
            else:
                @pl.when(cond)
                def _():
                    copy.start()
            o_sends.append((cond, copy))

    def late_landed(way, step, order):
        origin = at(-step - 1 if way == 0 else step + 1)
        piece = order ^ way
        ref = wo.at[lax.rem(origin, steps), pl.ds(piece * orows, orows)]
        index = 2 * (step - near) + order
        return holds(origin), copy_to(ref, ref, late_s.at[way, index], late_r.at[way, index], seq=peers[way])

    lane_tok = lax.broadcasted_iota(jnp.int32, (tok_count, tok_count), 1)
    row_tok = lax.broadcasted_iota(jnp.int32, (tok_count, tok_count), 0)
    before = jnp.where(row_tok < lane_tok, 1.0, 0.0).astype(jnp.bfloat16)
    slot_row = lax.broadcasted_iota(jnp.int32, (tok_count, tok_count), 0).astype(jnp.float32)

    def process(n):
        table = blocks[n, width : width + E, :].astype(jnp.float32)
        present = table > 0.0
        earlier = dot(jnp.where(present, 1.0, 0.0).astype(jnp.bfloat16), before)
        slot = jnp.where(present, earlier, -1.0)
        comb = jnp.zeros((tok_count, tok_count), jnp.float32)
        for e in range(own):
            mine = expert_row == me * own + e
            slot_e = jnp.sum(jnp.where(mine, slot, 0.0), axis=0, keepdims=True)
            scale_e = jnp.sum(jnp.where(mine, table, 0.0), axis=0, keepdims=True)
            hit = (slot_row == slot_e + float(e * CAP)) & (slot_e >= 0.0)
            comb = jnp.where(hit, scale_e, comb)
        combine[n] = comb.T.astype(jnp.bfloat16)
        select = jnp.where(comb > 0.0, 1.0, 0.0).astype(jnp.bfloat16)[:slots]
        rows = dot(select, blocks[n, :width, :], ((1,), (1,))).astype(jnp.bfloat16)
        for e in range(own):
            picked[e, n] = rows[e * CAP : (e + 1) * CAP]

    for piece in (0, 1):
        for way in (0, 1):
            ag_send(way, 0, piece ^ way)
    o_begin()
    process(me)
    for i in range(0, width, 128):
        size = min(128, width - i)
        hid[:, i : i + size] = tok_t_ref[i : i + size, :].astype(jnp.float32).T
    for step in range(1, steps):
        for piece in (0, 1):
            for way in (0, 1):
                ag[way, step - 1, piece ^ way].wait_recv()
                if step < steps - 1 or piece == 0:
                    ag_send(way, step, piece ^ way)
        if step <= near:
            o_step(step)
        process(at(-step))
        process(at(step))
    ag[0, steps - 1, 0].wait_recv()
    ag[1, steps - 1, 1].wait_recv()
    process(at(steps))

    q_begin()
    pos = {0: 1, 1: 2, 2: 3, 3: 4}
    half = dn.shape[1]
    chunk = CAP
    for e in range(own):
        for j in (2 * e, 2 * e + 1):
            gu_copies[j].wait()
            x = picked[e].reshape(count * CAP, width)
            proj[...] = dot(x, gu[j])

            @pl.loop(0, count)
            def _(i):
                r = pl.ds(pl.multiple_of(i * chunk, 16), chunk)
                gate = proj[r, :half]
                up = proj[r, half:]
                act[j % 2, r, :] = (gate * jax.nn.sigmoid(1.702 * gate) * (up + 1.0)).astype(jnp.bfloat16)

            if j < steps:
                q_step(j + 1)
        dn_copies[2 * e].wait()
        dn_copies[2 * e + 1].wait()
        result = dot(act[0], dn[2 * e]) + dot(act[1], dn[2 * e + 1])
        done[:, e * CAP : (e + 1) * CAP, :] = result.astype(jnp.bfloat16).reshape(count, CAP, width)
    for step in range(2 * own + 1, steps + 1):
        q_step(step)

    hrows = tok_count // 2
    tail = width % 128
    full = width - tail
    folds = 128 // tail
    trows = hrows // folds
    base = hrows * (full // 128)

    def part(n):
        value = dot(combine[n][:, :slots], done[n])
        for c in (0, 1):
            rows = value[c * hrows : (c + 1) * hrows]
            for i in range(0, full, 128):
                parts[n, c, i // 128 * hrows : (i // 128 + 1) * hrows, :] = rows[:, i : i + 128].astype(jnp.bfloat16)
            parts[n, c, base : base + trows, :] = jnp.concatenate(
                [rows[k * trows : (k + 1) * trows, full:] for k in range(folds)], axis=1
            ).astype(jnp.bfloat16)

    rs = {}

    def rs_send(way, step, piece):
        goal = at((steps - step) * (1 if way == 0 else -1))
        if (way, step - 1, piece) in rs:
            rs[way, step - 1, piece].wait_recv()
            held[way, step - 1, piece] = (
                held[way, step - 1, piece].astype(jnp.float32) + parts[goal, piece].astype(jnp.float32)
            ).astype(jnp.bfloat16)
            src = held.at[way, step - 1, piece]
        else:
            src = parts.at[goal, piece]
        rs[way, step, piece] = launch(copy_to(src, held.at[way, step, piece], rs_s.at[way, step, piece], rs_r.at[way, step, piece], seq=peers[way]))

    part(at(steps))
    rs_send(0, 0, 0)
    rs_send(1, 0, 1)
    for way in (0, 1):
        part(at((steps - 1) * (1 if way == 0 else -1)))
        rs_send(way, 1, 1 - way)
    for offset in range(steps - 2, 0, -1):
        part(at(offset))
        part(at(-offset))
    part(me)
    rs_send(0, 1, 0)
    rs_send(1, 1, 1)
    for step in range(2, steps):
        for piece in (0, 1):
            for way in (0, 1):
                rs_send(way, step, 1 ^ piece ^ way)
    late_send(near, 0)
    for c in (0, 1):
        for way in (0, 1):
            rs[way, steps - 1, c].wait_recv()
        rows = slice(c * hrows, (c + 1) * hrows)
        value = (parts[me, c].astype(jnp.float32) + held[0, steps - 1, c].astype(jnp.float32)
            + held[1, steps - 1, c].astype(jnp.float32))
        for i in range(0, full, 128):
            term = value[i // 128 * hrows : (i // 128 + 1) * hrows]
            hid[rows, i : i + 128] = (hid[rows, i : i + 128] + term).astype(jnp.bfloat16).astype(jnp.float32)
        term = jnp.concatenate(
            [value[base : base + trows, k * tail : (k + 1) * tail] for k in range(folds)], axis=0)
        hid[rows, full:] = (hid[rows, full:] + term).astype(jnp.bfloat16).astype(jnp.float32)
    hidden = hid[...]
    scale = lax.rsqrt(jnp.sum(hidden * hidden, axis=1, keepdims=True) / width + eps)
    normed = hidden * scale * attn_gain_ref[...].reshape(1, width)
    shard = wq.shape[1]
    for i in range(count):
        both[core, i] = normed[:, i * shard : (i + 1) * shard].astype(jnp.bfloat16)
    pair = launch(copy_to(both.at[core], both.at[core], pair_s.at[0], pair_r.at[0], pipe=other_core))

    for key in qx:
        qx[key].wait_recv()

    def project(m, columns):
        total = None
        for i in range(count):
            x = both[:, i].reshape(2 * tok_count, shard) if m is None else both[m, i]
            term = dot(x, wq[i, :, columns])
            total = term if total is None else total + term
        return total.astype(jnp.bfloat16)

    kv[core] = project(core, pl.ds(0, 2 * kw))
    along = [launch(copy_to(kv.at[core], halo.at[core], halo_s.at[0], halo_r.at[0], seq=following))]
    pair.wait_recv()
    kv[other_core] = project(other_core, pl.ds(0, 2 * kw))
    along.append(launch(copy_to(kv.at[other_core], halo.at[other_core], halo_s.at[1], halo_r.at[1], seq=following)))
    late_send(near, 1)
    queries[...] = project(None, pl.ds(2 * kw, qw)).reshape(2, tok_count, qw)
    for i in range(0, width, 128):
        size = min(128, width - i)
        hid_t[i : i + size, :] = hid[:, i : i + size].T
    late_send(near + 1, 0)
    for copy in along:
        copy.wait_recv()

    lane = lax.broadcasted_iota(jnp.int32, (tok_count, 2 * tok_count), 1)
    row = lax.broadcasted_iota(jnp.int32, (tok_count, 2 * tok_count), 0)
    left = lane < tok_count
    past = jnp.where(left, lane, lane - tok_count) > row
    low = lax.broadcasted_iota(jnp.int32, (tok_count, 2 * HEAD_SIZE), 1) < HEAD_SIZE

    def stacked(tile, head):
        tile = tile.astype(jnp.float32)
        kept = jnp.where(low if head == 0 else ~low, tile, 0.0)
        turned = pltpu.roll(kept, HEAD_SIZE, 1)
        pair_of = (kept, turned) if head == 0 else (turned, kept)
        return jnp.concatenate(pair_of, axis=0).astype(jnp.bfloat16)

    tiles = qw // 128
    per_head = tiles // 2
    for m in range(2):
        source = jnp.where(me == 0, 0, m)
        known = (me > 0) if m == 0 else (me >= 0)
        for head in range(2):
            k_own = stacked(kv[m, :, :kw], head)
            v_own = stacked(kv[m, :, kw:], head)
            k_past = stacked(halo[source, :, :kw], head)
            v_past = stacked(halo[source, :, kw:], head)
            for t in range(head * per_head, (head + 1) * per_head):
                first_head = core * 2 * tiles + 2 * t
                sink = jnp.exp(jnp.where(left[:1], sink_ref[first_head], sink_ref[first_head + 1]))
                x = queries[m, :, t * 128 : (t + 1) * 128]
                score = jnp.where(past, dot(x, k_past, ((1,), (1,))), dot(x, k_own, ((1,), (1,))))
                weight = jnp.exp(score * (float(HEAD_SIZE) ** -0.5))
                weight = jnp.where(past & jnp.logical_not(known), 0.0, weight)
                mass = jnp.where(left, jnp.sum(weight[:, :tok_count], axis=1, keepdims=True),
                    jnp.sum(weight[:, tok_count:], axis=1, keepdims=True)) + sink
                probs = weight / mass
                mixed[m, :, t * 128 : (t + 1) * 128] = (
                    dot(jnp.where(past, 0.0, probs).astype(jnp.bfloat16), v_own)
                    + dot(jnp.where(past, probs, 0.0).astype(jnp.bfloat16), v_past)
                ).astype(jnp.bfloat16)

    for way in (0, 1):
        for step in range(near - 1):
            cond, _, crossing = o_landed(way, step)

            @pl.when(cond)
            def _():
                crossing.wait_recv()
        cond, landed = late_landed(way, near, 1)

        @pl.when(cond)
        def _():
            landed.wait_recv()
        cond, landed = late_landed(way, near + 1, 0)

        @pl.when(cond)
        def _():
            landed.wait_recv()

    share = wo.shape[2]

    def output(m):
        total = None
        for i in range(steps):
            term = dot(wo[i], mixed[m, :, i * share : (i + 1) * share], ((1,), (1,)))
            total = term if total is None else total + term
        return total

    given[...] = output(other_core).astype(jnp.bfloat16)
    last = launch(copy_to(given, back, pair_s.at[1], pair_r.at[1], pipe=other_core))
    kept = output(core)
    last.wait_recv()
    out_ref[...] = (hid_t[...] + kept + back[...].astype(jnp.float32)).astype(jnp.bfloat16)
    for _, copy in sends:
        copy.wait_send()
    for cond, copy in o_sends:
        @pl.when(cond)
        def _():
            copy.wait_send()


def whole_layer(
    tokens, routes, route_weights, moe_gain, gate_up, down_proj, attn_gain, qkv_proj,
    head_sink_logits, out_proj,
):
    count = lax.axis_size("seq")
    steps = count // 2
    tok_count, width = tokens.shape[1:]
    own = gate_up.shape[0] // 2
    half = down_proj.shape[1]
    heads = QUERY_HEADS // 2
    qw = heads * HEAD_SIZE
    kw = KEY_VALUE_HEADS * HEAD_SIZE // 2
    chunk = tok_count // 2 * width // 128
    dma = pltpu.SemaphoreType.DMA
    bf16 = jnp.bfloat16
    vm = pl.BlockSpec(memory_space=pltpu.VMEM)
    hbm = pl.BlockSpec(memory_space=pl.ANY)
    out = pl.pallas_call(
        layer_kernel,
        out_shape=jax.ShapeDtypeStruct((width, tok_count), bf16),
        in_specs=[vm] * 5 + [pl.BlockSpec(memory_space=pltpu.SMEM)] + [hbm] * 4,
        out_specs=vm,
        scratch_shapes=[
            pltpu.VMEM((count, width + E, tok_count), bf16),
            pltpu.VMEM((own, count, CAP, width), bf16),
            pltpu.VMEM((count, tok_count, tok_count), bf16),
            pltpu.VMEM(gate_up.shape, bf16),
            pltpu.VMEM(down_proj.shape, bf16),
            pltpu.VMEM((count * CAP, 2 * half), jnp.float32),
            pltpu.VMEM((2, count * CAP, half), bf16),
            pltpu.VMEM((count, own * CAP, width), bf16),
            pltpu.VMEM((count, 2, chunk, 128), bf16),
            pltpu.VMEM((2, steps, 2, chunk, 128), bf16),
            pltpu.VMEM((count, qkv_proj.shape[0], 2 * kw + qw), bf16),
            pltpu.VMEM((steps, width, out_proj.shape[0]), bf16),
            pltpu.VMEM((2, count, tok_count, qkv_proj.shape[0]), bf16),
            pltpu.VMEM((2, tok_count, 2 * kw), bf16),
            pltpu.VMEM((2, tok_count, 2 * kw), bf16),
            pltpu.VMEM((2, tok_count, qw), bf16),
            pltpu.VMEM((2, tok_count, qw), bf16),
            pltpu.VMEM((width, tok_count), bf16),
            pltpu.VMEM((width, tok_count), bf16),
            pltpu.VMEM((tok_count, width), jnp.float32),
            pltpu.VMEM((width, tok_count), jnp.float32),
            dma((2 * own,)), dma((2 * own,)), dma((3,)), dma((1,)),
            dma((2, steps, 2)), dma((2, steps, 2)), dma((2, steps, 2)), dma((2, steps, 2)),
            dma((2, steps)), dma((2, steps)), dma((2, steps)), dma((2, steps)),
            dma((2, steps)), dma((2, steps)), dma((2, steps)), dma((2, steps)),
            dma((2, 3)), dma((2, 3)), dma((2,)), dma((2,)), dma((2,)), dma((2,)),
        ],
        compiler_params=pltpu.CompilerParams(
            collective_id=0, has_side_effects=True, vmem_limit_bytes=67043328),
    )(tokens[0].T, routes[0].T, route_weights[0].T, moe_gain, attn_gain, head_sink_logits,
      gate_up, down_proj, qkv_proj, out_proj.T)
    return out.T[None]


def solution(mesh):
    in_specs = (
        P("pipe", ("groups", "seq"), None),
        P("pipe", ("groups", "seq"), None),
        P("pipe", ("groups", "seq"), None),
        P(),
        P("seq", None, None),
        P("seq", None, None),
        P(),
        P("seq", None),
        P(),
        P("seq", None),
    )
    out_specs = P("pipe", ("groups", "seq"), None)
    seq_count, pipe_count, group_count = mesh.shape["seq"], mesh.shape["pipe"], mesh.shape["groups"]
    whole = (
        pipe_count == 2
        and group_count == 2
        and seq_count % 2 == 0
        and 2 * E // seq_count == 4
        and QUERY_HEADS % (2 * seq_count) == 0
    )
    return jax.shard_map(
        whole_layer if whole else body, mesh=mesh, in_specs=in_specs, out_specs=out_specs, check_vma=False
    )
```

```python
import functools

import jax
import jax.numpy as jnp
from jax import lax
from jax.experimental import pallas as pl
from jax.experimental.pallas import tpu as pltpu
from jax.sharding import PartitionSpec as P

MESH = pl.DeviceIdType.MESH
E = 16
TOP = 4
QUERY_HEADS = 32
KEY_VALUE_HEADS = 4
HEAD_SIZE = 64
WINDOW_SPAN = 128
HALF = 720
CAP = 48


eps = 1e-05


def from_partner(value, axis, distance):
    return lax.ppermute(value, axis, [(i, i ^ 1 << distance) for i in range(lax.axis_size(axis))])


def shifted(value, axis, steps):
    count = lax.axis_size(axis)
    pairs = [(source, (source + steps) % count) for source in range(count)]
    return lax.ppermute(value, axis, pairs)


def passed_along(value, axis, steps):
    count = lax.axis_size(axis)
    first, last = (max(0, -steps), min(count, count - steps))
    return lax.ppermute(value, axis, [(source, source + steps) for source in range(first, last)])


def rms_scale(value_matrix, gain):
    widened = value_matrix.astype(jnp.float32)
    mean_square = jnp.mean(widened * widened, axis=-1, keepdims=True)
    return (widened * lax.rsqrt(mean_square + eps) * gain).astype(jnp.bfloat16)


def slot_positions(route_rows):
    flat = route_rows.reshape(-1)
    onehot = (flat[:, None] == jnp.arange(E, dtype=jnp.int32)[None, :]).astype(jnp.int32)
    earlier = jnp.cumsum(onehot, axis=0) - onehot
    return flat * CAP + jnp.sum(earlier * onehot, axis=1)


def expert_layer(local, route_rows, route_scale, moe_gain, gate_up, down_proj):
    tok_count, width = local.shape
    seq_count = lax.axis_size("seq")
    per_device = gate_up.shape[0]
    normed = rms_scale(local, moe_gain)
    positions = slot_positions(route_rows)
    select = (positions[None, :] == jnp.arange(E * CAP, dtype=jnp.int32)[:, None]).astype(
        jnp.bfloat16
    )
    repeated = jnp.repeat(normed, TOP, axis=0)
    table = jnp.dot(select, repeated, preferred_element_type=jnp.float32).astype(jnp.bfloat16)
    by_expert = table.reshape(E, CAP, width)
    first = lax.axis_index("seq") % 2 == 0
    outgoing = jnp.repeat(by_expert, 2, axis=0).reshape(seq_count, per_device, CAP, width)
    received = lax.all_to_all(outgoing, "seq", split_axis=0, concat_axis=0, tiled=True)
    projected = jnp.einsum("spcd,pdh->spch", received, gate_up, preferred_element_type=jnp.float32)
    gate_part = projected[..., :HALF]
    up_part = projected[..., HALF:]
    hidden = (gate_part * jax.nn.sigmoid(1.702 * gate_part) * (up_part + 1.0)).astype(jnp.bfloat16)
    partial_value = jnp.einsum(
        "spch,phd->spcd", hidden, down_proj, preferred_element_type=jnp.float32
    )
    if per_device >= 2:
        finished = (
            partial_value.reshape(seq_count, per_device // 2, 2, CAP, width)
            .sum(axis=2)
            .astype(jnp.bfloat16)
        )
    else:
        lower_rows = partial_value[:, :, : CAP // 2]
        upper_rows = partial_value[:, :, CAP // 2 :]
        kept = jnp.where(first, lower_rows, upper_rows)
        given = jnp.where(first, upper_rows, lower_rows)
        partner_part = from_partner(given.astype(jnp.bfloat16), "seq", 0).astype(given.dtype)
        finished = (kept + partner_part).astype(jnp.bfloat16)
    summed = lax.all_to_all(finished, "seq", split_axis=0, concat_axis=0, tiled=True).reshape(
        E * CAP, width
    )
    picked = lax.dot_general(
        select, summed, (((0,), (0,)), ((), ())), preferred_element_type=jnp.float32
    )
    weighted = jnp.sum(picked.reshape(tok_count, TOP, width) * route_scale[:, :, None], axis=1)
    return (local.astype(jnp.float32) + weighted).astype(jnp.bfloat16)


def attend(query_matrix, keys_extended, values_extended, head_sink_logits, halo_valid):
    tok_count = query_matrix.shape[0]
    query_groups = QUERY_HEADS // KEY_VALUE_HEADS
    attention_block = min(tok_count, 512)
    scale = float(HEAD_SIZE) ** (-0.5)
    sink_mass_total = jnp.exp(head_sink_logits).reshape(KEY_VALUE_HEADS, query_groups, 1, 1)
    block_queries = query_matrix.reshape(attention_block, KEY_VALUE_HEADS, query_groups, HEAD_SIZE)
    block_keys = keys_extended.reshape(attention_block + WINDOW_SPAN, KEY_VALUE_HEADS, HEAD_SIZE)
    block_values = values_extended.reshape(
        attention_block + WINDOW_SPAN, KEY_VALUE_HEADS, HEAD_SIZE
    )
    scores = (
        jnp.einsum("qhgd,khd->hgqk", block_queries, block_keys, preferred_element_type=jnp.float32)
        * scale
    )
    query_pos = jnp.arange(attention_block, dtype=jnp.int32)[:, None] + WINDOW_SPAN
    key_pos = jnp.arange(attention_block + WINDOW_SPAN, dtype=jnp.int32)[None, :]
    distance = query_pos - key_pos
    allowed = (
        (distance >= 0) & (distance < WINDOW_SPAN) & ((key_pos + 0 >= WINDOW_SPAN) | halo_valid)
    )
    weights = jnp.where(allowed, jnp.exp(scores), 0.0)
    probs = (weights / (jnp.sum(weights, axis=-1, keepdims=True) + sink_mass_total)).astype(
        jnp.bfloat16
    )
    mixed = jnp.einsum("hgqk,khd->qhgd", probs, block_values, preferred_element_type=jnp.float32)
    outputs = mixed.reshape(attention_block, QUERY_HEADS * HEAD_SIZE).astype(jnp.bfloat16)
    return outputs


def body(
    tokens,
    routes,
    route_weights,
    moe_gain,
    gate_up,
    down_proj,
    attn_gain,
    qkv_proj,
    head_sink_logits,
    out_proj,
):
    hidden = expert_layer(tokens[0], routes[0], route_weights[0], moe_gain, gate_up, down_proj)
    tok_count, width = hidden.shape
    normed = rms_scale(hidden, attn_gain)
    seq_index = lax.axis_index("seq")
    pipe_index = lax.axis_index("pipe")
    halo_valid = (seq_index > 0) | (pipe_index > 0)
    query_width = QUERY_HEADS * HEAD_SIZE
    width_of_pair = KEY_VALUE_HEADS * HEAD_SIZE
    columns = normed
    packed_heads = jnp.dot(
        columns,
        lax.all_gather(qkv_proj, "seq", axis=0, tiled=True),
        preferred_element_type=jnp.float32,
    ).astype(jnp.bfloat16)
    from_left = shifted(packed_heads[tok_count - WINDOW_SPAN :, query_width:], "seq", 1)
    from_section = passed_along(from_left, "pipe", 1)
    halo_pairs = jnp.where(seq_index == 0, from_section, from_left)
    query_matrix = packed_heads[:, :query_width]
    pairs_ext = jnp.concatenate([halo_pairs, packed_heads[:, query_width:]], axis=0)
    keys_extended = pairs_ext[:, :width_of_pair]
    values_extended = pairs_ext[:, width_of_pair:]
    attended = attend(query_matrix, keys_extended, values_extended, head_sink_logits, halo_valid)
    columns = attended
    projected = jnp.dot(
        columns,
        lax.all_gather(out_proj, "seq", axis=0, tiled=True),
        preferred_element_type=jnp.float32,
    )
    return (hidden.astype(jnp.float32) + projected).astype(jnp.bfloat16)[None]


def ring_place(index, count, folded):
    if not folded:
        return index
    line, side = index // 2, index % 2
    return line + side * (count - 1 - 2 * line)

def ring_index(place, count, folded):
    if not folded:
        return place
    side = place // (count // 2)
    line = place + side * (count - 1 - 2 * place)
    return 2 * line + side


def copy_to(src, dst, send, recv, **device):
    return pltpu.make_async_remote_copy(src_ref=src, dst_ref=dst, send_sem=send, recv_sem=recv,
        device_id=device, device_id_type=MESH)


def dot(a, b, dims=((1,), (0,))):
    return lax.dot_general(a, b, (dims, ((), ())), preferred_element_type=jnp.float32)


def layer_kernel(
    tok_t_ref, routes_ref, weights_ref, gain_ref, attn_gain_ref, sink_ref,
    gate_up_ref, down_ref, qkv_ref, out_t_ref,
    out_ref,
    blocks, picked, combine, gu, dn, proj, act, done, parts, held, wq, wo,
    both, kv, halo, queries, mixed, given, back, hid, hid_t, wkv, kv_other,
    gu_sem, dn_sem, wq_sem, wo_sem, ag_s, ag_r, rs_s, rs_r, q_s, q_r, qx_s, qx_r,
    o_s, o_r, ox_s, ox_r, late_s, late_r, lx_s, lx_r, pair_s, pair_r, halo_s, halo_r,
    wkv_s, wkv_r,
):
    count = lax.axis_size("seq")
    steps = count // 2
    me = lax.axis_index("seq")
    core = lax.axis_index("pipe")
    group = lax.axis_index("groups")
    width, tok_count = tok_t_ref.shape
    own = picked.shape[0]
    slots = own * CAP
    place = ring_place(me, count, True)
    at = lambda offset: ring_index(lax.rem(place + offset + count, count), count, True)
    peers = (at(1), at(-1))
    following, preceding = lax.rem(me + 1, count), lax.rem(me + count - 1, count)
    other_core, other_group = 1 - core, 1 - group
    sends = []

    def launch(copy):
        copy.start()
        sends.append((None, copy))
        return copy

    barrier = pltpu.get_barrier_semaphore()
    for device in ({"seq": peers[0]}, {"seq": peers[1]}, {"seq": following}, {"seq": preceding},
                   {"pipe": other_core}, {"groups": other_group},
                   {"seq": following, "pipe": other_core}, {"seq": preceding, "pipe": other_core}):
        pl.semaphore_signal(barrier, inc=1, device_id=device, device_id_type=MESH)

    qw, kw = queries.shape[2], kv.shape[2] // 2
    all_q = QUERY_HEADS * HEAD_SIZE
    all_k = KEY_VALUE_HEADS * HEAD_SIZE
    wo_slot = lax.rem(me, steps)
    holds = lambda origin: lax.div(origin, steps) == core
    wo_copy = pltpu.make_async_copy(out_t_ref, wo.at[wo_slot], wo_sem.at[0])

    @pl.when(holds(me))
    def _():
        wo_copy.start()

    wq_copies = []
    for i, (source, goal, size) in enumerate((
        (all_q + core * kw, 0, kw), (all_q + all_k + core * kw, kw, kw), (core * qw, 2 * kw, qw))):
        wq_copies.append(pltpu.make_async_copy(
            qkv_ref.at[:, pl.ds(pl.multiple_of(source, 128), size)],
            wq.at[me, :, pl.ds(goal, size)], wq_sem.at[i]))
    for copy in wq_copies:
        copy.start()
    gu_copies = [pltpu.make_async_copy(gate_up_ref.at[j], gu.at[j], gu_sem.at[j]) for j in range(2 * own)]
    dn_copies = [pltpu.make_async_copy(down_ref.at[j], dn.at[j], dn_sem.at[j]) for j in range(2 * own)]
    for copy in gu_copies + dn_copies:
        copy.start()

    rows_all = blocks.shape[1]
    cut = (rows_all // 2 + 15) // 16 * 16
    pieces = (pl.ds(0, cut), pl.ds(cut, rows_all - cut))
    ag = {}

    def ag_send(way, step, piece):
        origin = at(-step if way == 0 else step)
        ref = blocks.at[origin, pieces[piece]]
        ag[way, step, piece] = launch(copy_to(ref, ref, ag_s.at[way, step, piece], ag_r.at[way, step, piece], seq=peers[way]))

    qcols = wq.shape[2] // 2
    qcut = (qcols // 2 + 127) // 128 * 128
    q = {}
    qx = {}

    def q_part(way, step):
        base = pl.multiple_of(group * qcols, 128)
        if step < steps - 1:
            return pl.ds(base, qcols)
        return pl.ds(base, qcut) if way == 0 else pl.ds(base + qcut, qcols - qcut)

    def q_send(way, step):
        ref = wq.at[at(-step if way == 0 else step), :, q_part(way, step)]
        q[way, step] = launch(copy_to(ref, ref, q_s.at[way, step], q_r.at[way, step], seq=peers[way]))

    def q_cross(way, step):
        q[way, step].wait_recv()
        ref = wq.at[at(-step - 1 if way == 0 else step + 1), :, q_part(way, step)]
        qx[way, step] = launch(copy_to(ref, ref, qx_s.at[way, step], qx_r.at[way, step], groups=other_group))

    def q_begin():
        for copy in wq_copies:
            copy.wait()
        for way in (0, 1):
            q_send(way, 0)

    def q_step(step):
        for way in (0, 1):
            q_cross(way, step - 1)
            if step < steps:
                q_send(way, step)

    orows = wo.shape[1] // 2
    ocut = (orows // 2 + 15) // 16 * 16
    o_sends = []

    def o_part(way, step):
        base = pl.multiple_of(group * orows, 16)
        if step < steps - 1:
            return pl.ds(base, orows)
        return pl.ds(base, ocut) if way == 0 else pl.ds(pl.multiple_of(base + ocut, 16), orows - ocut)

    def o_copy(way, step):
        origin = at(-step if way == 0 else step)
        ref = wo.at[lax.rem(origin, steps), o_part(way, step)]
        return holds(origin), copy_to(ref, ref, o_s.at[way, step], o_r.at[way, step], seq=peers[way])

    def o_landed(way, step):
        origin = at(-step - 1 if way == 0 else step + 1)
        ref = wo.at[lax.rem(origin, steps), o_part(way, step)]
        return (holds(origin), copy_to(ref, ref, o_s.at[way, step], o_r.at[way, step], seq=peers[way]),
                copy_to(ref, ref, ox_s.at[way, step], ox_r.at[way, step], groups=other_group))

    def o_begin():
        @pl.when(holds(me))
        def _():
            wo_copy.wait()
        for way in (0, 1):
            cond, copy = o_copy(way, 0)

            @pl.when(cond)
            def _():
                copy.start()
            o_sends.append((cond, copy))

    near = steps // 2

    def o_step(step):
        for way in (0, 1):
            cond, arrived, crossing = o_landed(way, step - 1)

            @pl.when(cond)
            def _():
                arrived.wait_recv()
                crossing.start()
            o_sends.append((cond, crossing))
            if step < near:
                onward, copy = o_copy(way, step)

                @pl.when(onward)
                def _():
                    copy.start()
                o_sends.append((onward, copy))

    quarter = (orows // 2 + 15) // 16 * 16
    mid = (orows - quarter // 2 + 15) // 16 * 16
    crossed = pl.ds(pl.multiple_of(group * (2 * orows - quarter), 16), quarter)
    inner = (pl.ds(quarter, mid - quarter), pl.ds(mid, 2 * orows - quarter - mid))

    def late_piece(name):
        return {"x": crossed, "a": inner[0], "b": inner[1]}[name]

    def late_copy(way, step, name, landed=False):
        hops = step + 1 if landed else step
        origin = at(-hops if way == 0 else hops)
        ref = wo.at[lax.rem(origin, steps), late_piece(name)]
        index = 3 * (step - near) + "xab".index(name)
        return holds(origin), copy_to(ref, ref, late_s.at[way, index], late_r.at[way, index], seq=peers[way])

    def late_send(way, step, names, after=()):
        cond, _ = late_copy(way, step, names[0])
        copies = [late_copy(way, step, name)[1] for name in names]

        @pl.when(cond)
        def _():
            for copy in after:
                copy.wait_recv()
            for copy in copies:
                copy.start()
        o_sends.extend((cond, copy) for copy in copies)

    def late_cross(way, step, index):
        cond, landed = late_copy(way, step, "x", True)
        origin = at(-step - 1 if way == 0 else step + 1)
        ref = wo.at[lax.rem(origin, steps), crossed]
        crossing = copy_to(ref, ref, lx_s.at[index], lx_r.at[index], groups=other_group)

        @pl.when(cond)
        def _():
            landed.wait_recv()
            crossing.start()
        o_sends.append((cond, crossing))
        return cond, crossing

    expert_row = lax.broadcasted_iota(jnp.int32, (E, tok_count), 0)
    lane_tok = lax.broadcasted_iota(jnp.int32, (tok_count, tok_count), 1)
    row_tok = lax.broadcasted_iota(jnp.int32, (tok_count, tok_count), 0)
    before = jnp.where(row_tok < lane_tok, 1.0, 0.0).astype(jnp.bfloat16)
    slot_row = lax.broadcasted_iota(jnp.int32, (tok_count, tok_count), 0).astype(jnp.float32)

    def process(n):
        table = blocks[n, width : width + E, :].astype(jnp.float32)
        present = table > 0.0
        earlier = dot(jnp.where(present, 1.0, 0.0).astype(jnp.bfloat16), before)
        slot = jnp.where(present, earlier, -1.0)
        comb = jnp.zeros((tok_count, tok_count), jnp.float32)
        for e in range(own):
            mine = expert_row == me * own + e
            slot_e = jnp.sum(jnp.where(mine, slot, 0.0), axis=0, keepdims=True)
            scale_e = jnp.sum(jnp.where(mine, table, 0.0), axis=0, keepdims=True)
            hit = (slot_row == slot_e + float(e * CAP)) & (slot_e >= 0.0)
            comb = jnp.where(hit, scale_e, comb)
        combine[n] = comb.T.astype(jnp.bfloat16)
        select = jnp.where(comb > 0.0, 1.0, 0.0).astype(jnp.bfloat16)[:slots]
        rows = dot(select, blocks[n, :width, :], ((1,), (1,))).astype(jnp.bfloat16)
        for e in range(own):
            picked[e, n] = rows[e * CAP : (e + 1) * CAP]

    tall = tok_t_ref[...].astype(jnp.float32)
    scale = lax.rsqrt(jnp.sum(tall * tall, axis=0, keepdims=True) / width + eps)
    pl.semaphore_wait(barrier, 8)
    o_begin()
    for i in range(0, width, 128):
        size = min(128, width - i)
        gain = jnp.broadcast_to(gain_ref[pl.ds(i, size)].reshape(1, size), (tok_count, size)).T
        blocks[me, i : i + size, :] = (
            tok_t_ref[i : i + size, :].astype(jnp.float32) * scale * gain
        ).astype(jnp.bfloat16)
    dense = jnp.zeros((E, tok_count), jnp.float32)
    for j in range(TOP):
        dense = dense + jnp.where(expert_row == routes_ref[j : j + 1, :], weights_ref[j : j + 1, :], 0.0)
    blocks[me, width : width + E, :] = dense.astype(jnp.bfloat16)
    for piece in (0, 1):
        for way in (0, 1):
            ag_send(way, 0, piece ^ way)
    process(me)
    for i in range(0, width, 128):
        size = min(128, width - i)
        hid[:, i : i + size] = tok_t_ref[i : i + size, :].astype(jnp.float32).T
    for step in range(1, steps):
        for piece in (0, 1):
            for way in (0, 1):
                ag[way, step - 1, piece ^ way].wait_recv()
                if step < steps - 1 or piece == 0:
                    ag_send(way, step, piece ^ way)
        if step <= near:
            o_step(step)
        process(at(-step))
        process(at(step))
    ag[0, steps - 1, 0].wait_recv()
    ag[1, steps - 1, 1].wait_recv()
    process(at(steps))

    q_begin()
    pos = {0: 1, 1: 2, 2: 3, 3: 4}
    half = dn.shape[1]
    chunk = CAP
    for e in range(own):
        for j in (2 * e, 2 * e + 1):
            gu_copies[j].wait()
            x = picked[e].reshape(count * CAP, width)
            proj[...] = dot(x, gu[j])

            @pl.loop(0, count)
            def _(i):
                r = pl.ds(pl.multiple_of(i * chunk, 16), chunk)
                gate = proj[r, :half]
                up = proj[r, half:]
                act[j % 2, r, :] = (gate * jax.nn.sigmoid(1.702 * gate) * (up + 1.0)).astype(jnp.bfloat16)

            if j < steps:
                q_step(j + 1)
        dn_copies[2 * e].wait()
        dn_copies[2 * e + 1].wait()
        result = dot(act[0], dn[2 * e]) + dot(act[1], dn[2 * e + 1])
        done[:, e * CAP : (e + 1) * CAP, :] = result.astype(jnp.bfloat16).reshape(count, CAP, width)
    for step in range(2 * own + 1, steps + 1):
        q_step(step)

    hrows = tok_count // 2
    tail = width % 128
    full = width - tail
    folds = 128 // tail
    trows = hrows // folds
    base = hrows * (full // 128)

    def part(n):
        value = dot(combine[n][:, :slots], done[n])
        for c in (0, 1):
            rows = value[c * hrows : (c + 1) * hrows]
            for i in range(0, full, 128):
                parts[n, c, i // 128 * hrows : (i // 128 + 1) * hrows, :] = rows[:, i : i + 128].astype(jnp.bfloat16)
            parts[n, c, base : base + trows, :] = jnp.concatenate(
                [rows[k * trows : (k + 1) * trows, full:] for k in range(folds)], axis=1
            ).astype(jnp.bfloat16)

    rs = {}

    def rs_send(way, step, piece):
        goal = at((steps - step) * (1 if way == 0 else -1))
        if (way, step - 1, piece) in rs:
            rs[way, step - 1, piece].wait_recv()
            held[way, step - 1, piece] = (
                held[way, step - 1, piece].astype(jnp.float32) + parts[goal, piece].astype(jnp.float32)
            ).astype(jnp.bfloat16)
            src = held.at[way, step - 1, piece]
        else:
            src = parts.at[goal, piece]
        rs[way, step, piece] = launch(copy_to(src, held.at[way, step, piece], rs_s.at[way, step, piece], rs_r.at[way, step, piece], seq=peers[way]))

    part(at(steps))
    rs_send(0, 0, 0)
    rs_send(1, 0, 1)
    for way in (0, 1):
        part(at((steps - 1) * (1 if way == 0 else -1)))
        rs_send(way, 1, 1 - way)
    for offset in range(steps - 2, 0, -1):
        part(at(offset))
        part(at(-offset))
    part(me)
    for key in qx:
        if key[1] < steps - 2:
            qx[key].wait_recv()
    rs_send(0, 1, 0)
    rs_send(1, 1, 1)
    for step in range(2, steps):
        for piece in (0, 1):
            for way in (0, 1):
                rs_send(way, step, 1 ^ piece ^ way)
    for key in qx:
        if key[1] >= steps - 2:
            qx[key].wait_recv()
    own_kv = wq.at[:, :, pl.ds(0, 2 * kw)]
    keys_over = launch(copy_to(own_kv, wkv, wkv_s.at[0], wkv_r.at[0], pipe=other_core))
    for way in (0, 1):
        late_send(way, near, "xa" if way == 0 else "bx", (o_landed(way, near - 1)[2],))
    for c in (0, 1):
        for way in (0, 1):
            rs[way, steps - 1, c].wait_recv()
        rows = slice(c * hrows, (c + 1) * hrows)
        value = (parts[me, c].astype(jnp.float32) + held[0, steps - 1, c].astype(jnp.float32)
            + held[1, steps - 1, c].astype(jnp.float32))
        for i in range(0, full, 128):
            term = value[i // 128 * hrows : (i // 128 + 1) * hrows]
            hid[rows, i : i + 128] = (hid[rows, i : i + 128] + term).astype(jnp.bfloat16).astype(jnp.float32)
        term = jnp.concatenate(
            [value[base : base + trows, k * tail : (k + 1) * tail] for k in range(folds)], axis=0)
        hid[rows, full:] = (hid[rows, full:] + term).astype(jnp.bfloat16).astype(jnp.float32)
    hidden = hid[...]
    scale = lax.rsqrt(jnp.sum(hidden * hidden, axis=1, keepdims=True) / width + eps)
    normed = hidden * scale * attn_gain_ref[...].reshape(1, width)
    shard = wq.shape[1]
    for i in range(count):
        both[core, i] = normed[:, i * shard : (i + 1) * shard].astype(jnp.bfloat16)
    pair = launch(copy_to(both.at[core], both.at[core], pair_s.at[0], pair_r.at[0], pipe=other_core))

    def project(m, weights, columns):
        total = None
        for i in range(count):
            x = both[:, i].reshape(2 * tok_count, shard) if m is None else both[m, i]
            term = dot(x, weights[i, :, columns])
            total = term if total is None else total + term
        return total.astype(jnp.bfloat16)

    pairs_cols = pl.ds(0, 2 * kw)
    kv[core] = project(core, wq, pairs_cols)
    along = [launch(copy_to(kv.at[core], halo.at[core], halo_s.at[0], halo_r.at[0], seq=following))]
    keys_over.wait_recv()
    kv_other[...] = project(core, wkv, pairs_cols)
    along.append(launch(copy_to(kv_other, halo.at[core], halo_s.at[1], halo_r.at[1], seq=following, pipe=other_core)))
    beside = launch(copy_to(kv_other, kv.at[core], pair_s.at[2], pair_r.at[2], pipe=other_core))
    for way in (0, 1):
        late_send(way, near, "b" if way == 0 else "a")
    crossings = [late_cross(0, near, 0)]
    pair.wait_recv()
    queries[...] = project(None, wq, pl.ds(2 * kw, qw)).reshape(2, tok_count, qw)
    late_send(0, near + 1, "xa", (late_copy(0, near, "a", True)[1],))
    late_send(1, near + 1, "b", (late_copy(1, near, "b", True)[1],))
    crossings.append(late_cross(1, near, 1))
    for i in range(0, width, 128):
        size = min(128, width - i)
        hid_t[i : i + size, :] = hid[:, i : i + size].T
    crossings.append(late_cross(0, near + 1, 2))
    beside.wait_recv()
    for copy in along:
        copy.wait_recv()

    lane = lax.broadcasted_iota(jnp.int32, (tok_count, 2 * tok_count), 1)
    row = lax.broadcasted_iota(jnp.int32, (tok_count, 2 * tok_count), 0)
    left = lane < tok_count
    past = jnp.where(left, lane, lane - tok_count) > row
    low = lax.broadcasted_iota(jnp.int32, (tok_count, 2 * HEAD_SIZE), 1) < HEAD_SIZE

    def stacked(tile, head):
        tile = tile.astype(jnp.float32)
        kept = jnp.where(low if head == 0 else ~low, tile, 0.0)
        turned = pltpu.roll(kept, HEAD_SIZE, 1)
        pair_of = (kept, turned) if head == 0 else (turned, kept)
        return jnp.concatenate(pair_of, axis=0).astype(jnp.bfloat16)

    tiles = qw // 128
    per_head = tiles // 2
    for m in range(2):
        source = jnp.where(me == 0, 0, m)
        known = (me > 0) if m == 0 else (me >= 0)
        for head in range(2):
            k_own = stacked(kv[m, :, :kw], head)
            v_own = stacked(kv[m, :, kw:], head)
            k_past = stacked(halo[source, :, :kw], head)
            v_past = stacked(halo[source, :, kw:], head)
            for t in range(head * per_head, (head + 1) * per_head):
                first_head = core * 2 * tiles + 2 * t
                sink = jnp.exp(jnp.where(left[:1], sink_ref[first_head], sink_ref[first_head + 1]))
                x = queries[m, :, t * 128 : (t + 1) * 128]
                score = jnp.where(past, dot(x, k_past, ((1,), (1,))), dot(x, k_own, ((1,), (1,))))
                weight = jnp.exp(score * (float(HEAD_SIZE) ** -0.5))
                weight = jnp.where(past & jnp.logical_not(known), 0.0, weight)
                mass_a = jnp.sum(weight[:, :tok_count], axis=1, keepdims=True) + sink[:, :1]
                mass_b = jnp.sum(weight[:, tok_count:], axis=1, keepdims=True) + sink[:, tok_count : tok_count + 1]
                probs = weight * jnp.where(left, 1.0 / mass_a, 1.0 / mass_b)
                mixed[m, :, t * 128 : (t + 1) * 128] = (
                    dot(jnp.where(past, 0.0, probs).astype(jnp.bfloat16), v_own)
                    + dot(jnp.where(past, probs, 0.0).astype(jnp.bfloat16), v_past)
                ).astype(jnp.bfloat16)

    for way in (0, 1):
        for step in range(near - 1):
            cond, _, crossing = o_landed(way, step)

            @pl.when(cond)
            def _():
                crossing.wait_recv()
        cond, landed = late_copy(way, near, "b" if way == 0 else "a", True)

        @pl.when(cond)
        def _():
            landed.wait_recv()
    cond, landed = late_copy(0, near + 1, "a", True)
    _, landed_b = late_copy(1, near + 1, "b", True)

    @pl.when(cond)
    def _():
        landed.wait_recv()
        landed_b.wait_recv()
    for cond, crossing in crossings:
        @pl.when(cond)
        def _():
            crossing.wait_recv()

    share = wo.shape[2]

    def output(m):
        total = None
        for i in range(steps):
            term = dot(wo[i], mixed[m, :, i * share : (i + 1) * share], ((1,), (1,)))
            total = term if total is None else total + term
        return total

    given[...] = output(other_core).astype(jnp.bfloat16)
    last = launch(copy_to(given, back, pair_s.at[1], pair_r.at[1], pipe=other_core))
    kept = output(core)
    last.wait_recv()
    out_ref[...] = (hid_t[...] + kept + back[...].astype(jnp.float32)).astype(jnp.bfloat16)
    for _, copy in sends:
        copy.wait_send()
    for cond, copy in o_sends:
        @pl.when(cond)
        def _():
            copy.wait_send()


def whole_layer(
    tokens, routes, route_weights, moe_gain, gate_up, down_proj, attn_gain, qkv_proj,
    head_sink_logits, out_proj,
):
    count = lax.axis_size("seq")
    steps = count // 2
    tok_count, width = tokens.shape[1:]
    own = gate_up.shape[0] // 2
    half = down_proj.shape[1]
    heads = QUERY_HEADS // 2
    qw = heads * HEAD_SIZE
    kw = KEY_VALUE_HEADS * HEAD_SIZE // 2
    chunk = tok_count // 2 * width // 128
    dma = pltpu.SemaphoreType.DMA
    bf16 = jnp.bfloat16
    vm = pl.BlockSpec(memory_space=pltpu.VMEM)
    hbm = pl.BlockSpec(memory_space=pl.ANY)
    out = pl.pallas_call(
        layer_kernel,
        out_shape=jax.ShapeDtypeStruct((width, tok_count), bf16),
        in_specs=[vm] * 5 + [pl.BlockSpec(memory_space=pltpu.SMEM)] + [hbm] * 4,
        out_specs=vm,
        scratch_shapes=[
            pltpu.VMEM((count, width + E, tok_count), bf16),
            pltpu.VMEM((own, count, CAP, width), bf16),
            pltpu.VMEM((count, tok_count, tok_count), bf16),
            pltpu.VMEM(gate_up.shape, bf16),
            pltpu.VMEM(down_proj.shape, bf16),
            pltpu.VMEM((count * CAP, 2 * half), jnp.float32),
            pltpu.VMEM((2, count * CAP, half), bf16),
            pltpu.VMEM((count, own * CAP, width), bf16),
            pltpu.VMEM((count, 2, chunk, 128), bf16),
            pltpu.VMEM((2, steps, 2, chunk, 128), bf16),
            pltpu.VMEM((count, qkv_proj.shape[0], 2 * kw + qw), bf16),
            pltpu.VMEM((steps, width, out_proj.shape[0]), bf16),
            pltpu.VMEM((2, count, tok_count, qkv_proj.shape[0]), bf16),
            pltpu.VMEM((2, tok_count, 2 * kw), bf16),
            pltpu.VMEM((2, tok_count, 2 * kw), bf16),
            pltpu.VMEM((2, tok_count, qw), bf16),
            pltpu.VMEM((2, tok_count, qw), bf16),
            pltpu.VMEM((width, tok_count), bf16),
            pltpu.VMEM((width, tok_count), bf16),
            pltpu.VMEM((tok_count, width), jnp.float32),
            pltpu.VMEM((width, tok_count), jnp.float32),
            pltpu.VMEM((count, qkv_proj.shape[0], 2 * kw), bf16),
            pltpu.VMEM((tok_count, 2 * kw), bf16),
            dma((2 * own,)), dma((2 * own,)), dma((3,)), dma((1,)),
            dma((2, steps, 2)), dma((2, steps, 2)), dma((2, steps, 2)), dma((2, steps, 2)),
            dma((2, steps)), dma((2, steps)), dma((2, steps)), dma((2, steps)),
            dma((2, steps)), dma((2, steps)), dma((2, steps)), dma((2, steps)),
            dma((2, 6)), dma((2, 6)), dma((3,)), dma((3,)), dma((3,)), dma((3,)), dma((2,)), dma((2,)),
            dma((1,)), dma((1,)),
        ],
        compiler_params=pltpu.CompilerParams(
            collective_id=0, has_side_effects=True, vmem_limit_bytes=67043328),
    )(tokens[0].T, routes[0].T, route_weights[0].T, moe_gain, attn_gain, head_sink_logits,
      gate_up, down_proj, qkv_proj, out_proj.T)
    return out.T[None]


def solution(mesh):
    in_specs = (
        P("pipe", ("groups", "seq"), None),
        P("pipe", ("groups", "seq"), None),
        P("pipe", ("groups", "seq"), None),
        P(),
        P("seq", None, None),
        P("seq", None, None),
        P(),
        P("seq", None),
        P(),
        P("seq", None),
    )
    out_specs = P("pipe", ("groups", "seq"), None)
    seq_count, pipe_count, group_count = mesh.shape["seq"], mesh.shape["pipe"], mesh.shape["groups"]
    whole = (
        pipe_count == 2
        and group_count == 2
        and seq_count % 2 == 0
        and 2 * E // seq_count == 4
        and QUERY_HEADS % (2 * seq_count) == 0
    )
    return jax.shard_map(
        whole_layer if whole else body, mesh=mesh, in_specs=in_specs, out_specs=out_specs, check_vma=False
    )
```

```python
import functools

import jax
import jax.numpy as jnp
from jax import lax
from jax.experimental import pallas as pl
from jax.experimental.pallas import tpu as pltpu
from jax.sharding import PartitionSpec as P

MESH = pl.DeviceIdType.MESH
E = 16
TOP = 4
QUERY_HEADS = 32
KEY_VALUE_HEADS = 4
HEAD_SIZE = 64
WINDOW_SPAN = 128
HALF = 720
CAP = 48


eps = 1e-05


def from_partner(value, axis, distance):
    return lax.ppermute(value, axis, [(i, i ^ 1 << distance) for i in range(lax.axis_size(axis))])


def shifted(value, axis, steps):
    count = lax.axis_size(axis)
    pairs = [(source, (source + steps) % count) for source in range(count)]
    return lax.ppermute(value, axis, pairs)


def passed_along(value, axis, steps):
    count = lax.axis_size(axis)
    first, last = (max(0, -steps), min(count, count - steps))
    return lax.ppermute(value, axis, [(source, source + steps) for source in range(first, last)])


def rms_scale(value_matrix, gain):
    widened = value_matrix.astype(jnp.float32)
    mean_square = jnp.mean(widened * widened, axis=-1, keepdims=True)
    return (widened * lax.rsqrt(mean_square + eps) * gain).astype(jnp.bfloat16)


def slot_positions(route_rows):
    flat = route_rows.reshape(-1)
    onehot = (flat[:, None] == jnp.arange(E, dtype=jnp.int32)[None, :]).astype(jnp.int32)
    earlier = jnp.cumsum(onehot, axis=0) - onehot
    return flat * CAP + jnp.sum(earlier * onehot, axis=1)


def expert_layer(local, route_rows, route_scale, moe_gain, gate_up, down_proj):
    tok_count, width = local.shape
    seq_count = lax.axis_size("seq")
    per_device = gate_up.shape[0]
    normed = rms_scale(local, moe_gain)
    positions = slot_positions(route_rows)
    select = (positions[None, :] == jnp.arange(E * CAP, dtype=jnp.int32)[:, None]).astype(
        jnp.bfloat16
    )
    repeated = jnp.repeat(normed, TOP, axis=0)
    table = jnp.dot(select, repeated, preferred_element_type=jnp.float32).astype(jnp.bfloat16)
    by_expert = table.reshape(E, CAP, width)
    first = lax.axis_index("seq") % 2 == 0
    outgoing = jnp.repeat(by_expert, 2, axis=0).reshape(seq_count, per_device, CAP, width)
    received = lax.all_to_all(outgoing, "seq", split_axis=0, concat_axis=0, tiled=True)
    projected = jnp.einsum("spcd,pdh->spch", received, gate_up, preferred_element_type=jnp.float32)
    gate_part = projected[..., :HALF]
    up_part = projected[..., HALF:]
    hidden = (gate_part * jax.nn.sigmoid(1.702 * gate_part) * (up_part + 1.0)).astype(jnp.bfloat16)
    partial_value = jnp.einsum(
        "spch,phd->spcd", hidden, down_proj, preferred_element_type=jnp.float32
    )
    if per_device >= 2:
        finished = (
            partial_value.reshape(seq_count, per_device // 2, 2, CAP, width)
            .sum(axis=2)
            .astype(jnp.bfloat16)
        )
    else:
        lower_rows = partial_value[:, :, : CAP // 2]
        upper_rows = partial_value[:, :, CAP // 2 :]
        kept = jnp.where(first, lower_rows, upper_rows)
        given = jnp.where(first, upper_rows, lower_rows)
        partner_part = from_partner(given.astype(jnp.bfloat16), "seq", 0).astype(given.dtype)
        finished = (kept + partner_part).astype(jnp.bfloat16)
    summed = lax.all_to_all(finished, "seq", split_axis=0, concat_axis=0, tiled=True).reshape(
        E * CAP, width
    )
    picked = lax.dot_general(
        select, summed, (((0,), (0,)), ((), ())), preferred_element_type=jnp.float32
    )
    weighted = jnp.sum(picked.reshape(tok_count, TOP, width) * route_scale[:, :, None], axis=1)
    return (local.astype(jnp.float32) + weighted).astype(jnp.bfloat16)


def attend(query_matrix, keys_extended, values_extended, head_sink_logits, halo_valid):
    tok_count = query_matrix.shape[0]
    query_groups = QUERY_HEADS // KEY_VALUE_HEADS
    attention_block = min(tok_count, 512)
    scale = float(HEAD_SIZE) ** (-0.5)
    sink_mass_total = jnp.exp(head_sink_logits).reshape(KEY_VALUE_HEADS, query_groups, 1, 1)
    block_queries = query_matrix.reshape(attention_block, KEY_VALUE_HEADS, query_groups, HEAD_SIZE)
    block_keys = keys_extended.reshape(attention_block + WINDOW_SPAN, KEY_VALUE_HEADS, HEAD_SIZE)
    block_values = values_extended.reshape(
        attention_block + WINDOW_SPAN, KEY_VALUE_HEADS, HEAD_SIZE
    )
    scores = (
        jnp.einsum("qhgd,khd->hgqk", block_queries, block_keys, preferred_element_type=jnp.float32)
        * scale
    )
    query_pos = jnp.arange(attention_block, dtype=jnp.int32)[:, None] + WINDOW_SPAN
    key_pos = jnp.arange(attention_block + WINDOW_SPAN, dtype=jnp.int32)[None, :]
    distance = query_pos - key_pos
    allowed = (
        (distance >= 0) & (distance < WINDOW_SPAN) & ((key_pos + 0 >= WINDOW_SPAN) | halo_valid)
    )
    weights = jnp.where(allowed, jnp.exp(scores), 0.0)
    probs = (weights / (jnp.sum(weights, axis=-1, keepdims=True) + sink_mass_total)).astype(
        jnp.bfloat16
    )
    mixed = jnp.einsum("hgqk,khd->qhgd", probs, block_values, preferred_element_type=jnp.float32)
    outputs = mixed.reshape(attention_block, QUERY_HEADS * HEAD_SIZE).astype(jnp.bfloat16)
    return outputs


def body(
    tokens,
    routes,
    route_weights,
    moe_gain,
    gate_up,
    down_proj,
    attn_gain,
    qkv_proj,
    head_sink_logits,
    out_proj,
):
    hidden = expert_layer(tokens[0], routes[0], route_weights[0], moe_gain, gate_up, down_proj)
    tok_count, width = hidden.shape
    normed = rms_scale(hidden, attn_gain)
    seq_index = lax.axis_index("seq")
    pipe_index = lax.axis_index("pipe")
    halo_valid = (seq_index > 0) | (pipe_index > 0)
    query_width = QUERY_HEADS * HEAD_SIZE
    width_of_pair = KEY_VALUE_HEADS * HEAD_SIZE
    columns = normed
    packed_heads = jnp.dot(
        columns,
        lax.all_gather(qkv_proj, "seq", axis=0, tiled=True),
        preferred_element_type=jnp.float32,
    ).astype(jnp.bfloat16)
    from_left = shifted(packed_heads[tok_count - WINDOW_SPAN :, query_width:], "seq", 1)
    from_section = passed_along(from_left, "pipe", 1)
    halo_pairs = jnp.where(seq_index == 0, from_section, from_left)
    query_matrix = packed_heads[:, :query_width]
    pairs_ext = jnp.concatenate([halo_pairs, packed_heads[:, query_width:]], axis=0)
    keys_extended = pairs_ext[:, :width_of_pair]
    values_extended = pairs_ext[:, width_of_pair:]
    attended = attend(query_matrix, keys_extended, values_extended, head_sink_logits, halo_valid)
    columns = attended
    projected = jnp.dot(
        columns,
        lax.all_gather(out_proj, "seq", axis=0, tiled=True),
        preferred_element_type=jnp.float32,
    )
    return (hidden.astype(jnp.float32) + projected).astype(jnp.bfloat16)[None]


def ring_place(index, count, folded):
    if not folded:
        return index
    line, side = index // 2, index % 2
    return line + side * (count - 1 - 2 * line)

def ring_index(place, count, folded):
    if not folded:
        return place
    side = place // (count // 2)
    line = place + side * (count - 1 - 2 * place)
    return 2 * line + side


def copy_to(src, dst, send, recv, **device):
    return pltpu.make_async_remote_copy(src_ref=src, dst_ref=dst, send_sem=send, recv_sem=recv,
        device_id=device, device_id_type=MESH)


def dot(a, b, dims=((1,), (0,))):
    return lax.dot_general(a, b, (dims, ((), ())), preferred_element_type=jnp.float32)


def layer_kernel(
    tok_t_ref, routes_ref, weights_ref, gain_ref, attn_gain_ref, sink_ref,
    gate_up_ref, down_ref, qkv_ref, out_t_ref,
    out_ref,
    blocks, picked, combine, gu, dn, proj, act, done, parts, held, wq, wo,
    both, kv, halo, queries, mixed, given, back, hid, hid_t,
    gu_sem, dn_sem, wq_sem, wo_sem, ag_s, ag_r, rs_s, rs_r, q_s, q_r, qx_s, qx_r,
    o_s, o_r, ox_s, ox_r, side_s, side_r, feed_s, feed_r, fx_s, fx_r, pair_s, pair_r, halo_s, halo_r,
):
    count = lax.axis_size("seq")
    steps = count // 2
    me = lax.axis_index("seq")
    core = lax.axis_index("pipe")
    group = lax.axis_index("groups")
    width, tok_count = tok_t_ref.shape
    own = picked.shape[0]
    slots = own * CAP
    place = ring_place(me, count, True)
    at = lambda offset: ring_index(lax.rem(place + offset + count, count), count, True)
    spot = lambda p: ring_index(lax.rem(p + count, count), count, True)
    peers = (at(1), at(-1))
    column = lax.rem(place, steps)
    inner = (column > 0) & (column < steps - 1)
    corner = jnp.logical_not(inner)
    low = column < steps // 2
    toward = jnp.where(low, 1, -1)
    outward = (jnp.logical_not(low), low)
    inner_out = [inner & outward[way] for way in (0, 1)]
    inner_in = [inner & jnp.logical_not(outward[way]) for way in (0, 1)]
    corner_fresh = [corner & outward[way] for way in (0, 1)]
    beside_place = count - 1 - place
    beside = spot(beside_place)
    following, preceding = lax.rem(me + 1, count), lax.rem(me + count - 1, count)
    other_core, other_group = 1 - core, 1 - group
    sends = []

    def launch(copy):
        copy.start()
        sends.append((None, copy))
        return copy

    qw, kw = queries.shape[2], kv.shape[2] // 2
    all_q = QUERY_HEADS * HEAD_SIZE
    all_k = KEY_VALUE_HEADS * HEAD_SIZE
    wo_slot = lax.rem(me, steps)
    holds = lambda origin: lax.div(origin, steps) == core
    wo_copy = pltpu.make_async_copy(out_t_ref, wo.at[wo_slot], wo_sem.at[0])

    @pl.when(holds(me))
    def _():
        wo_copy.start()

    wq_copies = []
    for i, (source, goal, size) in enumerate((
        (all_q + core * kw, 0, kw), (all_q + all_k + core * kw, kw, kw), (core * qw, 2 * kw, qw))):
        wq_copies.append(pltpu.make_async_copy(
            qkv_ref.at[:, pl.ds(pl.multiple_of(source, 128), size)],
            wq.at[me, :, pl.ds(goal, size)], wq_sem.at[i]))
    for copy in wq_copies:
        copy.start()
    gu_copies = [pltpu.make_async_copy(gate_up_ref.at[j], gu.at[j], gu_sem.at[j]) for j in range(2 * own)]
    dn_copies = [pltpu.make_async_copy(down_ref.at[j], dn.at[j], dn_sem.at[j]) for j in range(2 * own)]
    for copy in gu_copies + dn_copies:
        copy.start()

    tall = tok_t_ref[...].astype(jnp.float32)
    scale = lax.rsqrt(jnp.sum(tall * tall, axis=0, keepdims=True) / width + eps)
    for i in range(0, width, 128):
        size = min(128, width - i)
        gain = jnp.broadcast_to(gain_ref[pl.ds(i, size)].reshape(1, size), (tok_count, size)).T
        blocks[me, i : i + size, :] = (
            tok_t_ref[i : i + size, :].astype(jnp.float32) * scale * gain
        ).astype(jnp.bfloat16)
    expert_row = lax.broadcasted_iota(jnp.int32, (E, tok_count), 0)
    dense = jnp.zeros((E, tok_count), jnp.float32)
    for j in range(TOP):
        dense = dense + jnp.where(expert_row == routes_ref[j : j + 1, :], weights_ref[j : j + 1, :], 0.0)
    blocks[me, width : width + E, :] = dense.astype(jnp.bfloat16)

    barrier = pltpu.get_barrier_semaphore()
    for device in ({"seq": peers[0]}, {"seq": peers[1]}, {"seq": following}, {"seq": preceding},
                   {"pipe": other_core}, {"groups": other_group}, {"seq": beside}):
        pl.semaphore_signal(barrier, inc=1, device_id=device, device_id_type=MESH)
    pl.semaphore_wait(barrier, 7)

    rows_all = blocks.shape[1]
    cut = (rows_all // 2 + 15) // 16 * 16
    pieces = (pl.ds(0, cut), pl.ds(cut, rows_all - cut))
    ag = {}

    def ag_send(way, step, piece):
        origin = at(-step if way == 0 else step)
        ref = blocks.at[origin, pieces[piece]]
        ag[way, step, piece] = launch(copy_to(ref, ref, ag_s.at[way, step, piece], ag_r.at[way, step, piece], seq=peers[way]))

    qcols = wq.shape[2] // 2
    qcut = (qcols // 2 + 127) // 128 * 128
    q = {}
    qx = {}

    def q_part(way, step):
        base = pl.multiple_of(group * qcols, 128)
        if step < steps - 1:
            return pl.ds(base, qcols)
        return pl.ds(base, qcut) if way == 0 else pl.ds(base + qcut, qcols - qcut)

    def q_send(way, step):
        ref = wq.at[at(-step if way == 0 else step), :, q_part(way, step)]
        q[way, step] = launch(copy_to(ref, ref, q_s.at[way, step], q_r.at[way, step], seq=peers[way]))

    def q_cross(way, step):
        q[way, step].wait_recv()
        ref = wq.at[at(-step - 1 if way == 0 else step + 1), :, q_part(way, step)]
        qx[way, step] = launch(copy_to(ref, ref, qx_s.at[way, step], qx_r.at[way, step], groups=other_group))

    def q_begin():
        for copy in wq_copies:
            copy.wait()
        for way in (0, 1):
            q_send(way, 0)

    def q_step(step):
        for way in (0, 1):
            q_cross(way, step - 1)
            if step < steps:
                q_send(way, step)

    orows = wo.shape[1] // 2
    ocut = (orows // 2 + 15) // 16 * 16
    o_sends = []

    def o_part(way, step):
        base = pl.multiple_of(group * orows, 16)
        if step < steps - 1:
            return pl.ds(base, orows)
        return pl.ds(base, ocut) if way == 0 else pl.ds(pl.multiple_of(base + ocut, 16), orows - ocut)

    def o_copy(way, step):
        origin = at(-step if way == 0 else step)
        ref = wo.at[lax.rem(origin, steps), o_part(way, step)]
        return holds(origin), copy_to(ref, ref, o_s.at[way, step], o_r.at[way, step], seq=peers[way])

    def o_landed(way, step):
        origin = at(-step - 1 if way == 0 else step + 1)
        ref = wo.at[lax.rem(origin, steps), o_part(way, step)]
        return (holds(origin), copy_to(ref, ref, o_s.at[way, step], o_r.at[way, step], seq=peers[way]),
                copy_to(ref, ref, ox_s.at[way, step], ox_r.at[way, step], groups=other_group))

    def o_begin():
        @pl.when(holds(me))
        def _():
            wo_copy.wait()
        for way in (0, 1):
            cond, copy = o_copy(way, 0)

            @pl.when(cond)
            def _():
                copy.start()
            o_sends.append((cond, copy))

    near = steps // 2

    def o_step(step):
        for way in (0, 1):
            cond, arrived, crossing = o_landed(way, step - 1)

            @pl.when(cond)
            def _():
                arrived.wait_recv()
                crossing.start()
            o_sends.append((cond, crossing))
            if step < near:
                onward, copy = o_copy(way, step)

                @pl.when(onward)
                def _():
                    copy.start()
                o_sends.append((onward, copy))

    def o_crossed(step):
        for way in (0, 1):
            cond, _, crossing = o_landed(way, step)

            @pl.when(cond)
            def _():
                crossing.wait_recv()

    def side_copy(origin, hop):
        ref = wo.at[lax.rem(origin, steps)]
        return inner & holds(origin), copy_to(ref, ref, side_s.at[hop], side_r.at[hop], seq=beside)

    def side_send(hop):
        cond, copy = side_copy(at(toward * hop), hop)

        @pl.when(cond)
        def _():
            copy.start()
        o_sends.append((cond, copy))

    def side_wait(hop):
        cond, copy = side_copy(spot(beside_place - toward * hop), hop)

        @pl.when(cond)
        def _():
            copy.wait_recv()

    feed_part = pl.ds(pl.multiple_of(group * orows, 16), orows)

    def feed_copy(origin, index):
        ref = wo.at[lax.rem(origin, steps), feed_part]
        return holds(origin), copy_to(ref, ref, feed_s.at[index], feed_r.at[index], seq=spot(place - toward))

    def feed_send():
        for index, origin in enumerate((
            at(2 * toward), spot(beside_place - toward), spot(beside_place - 2 * toward))):
            cond, copy = feed_copy(origin, index)

            @pl.when(inner & cond)
            def _():
                copy.start()
            o_sends.append((inner & cond, copy))

    feed_crossings = []

    def feed_cross(index):
        origin = (spot(place + 3 * toward), spot(beside_place - 2 * toward), spot(beside_place - 3 * toward))[index]
        held_here, landed = feed_copy(origin, index)
        cond = corner & held_here
        ref = wo.at[lax.rem(origin, steps), feed_part]
        crossing = copy_to(ref, ref, fx_s.at[index], fx_r.at[index], groups=other_group)

        @pl.when(cond)
        def _():
            landed.wait_recv()
            crossing.start()
        o_sends.append((cond, crossing))
        feed_crossings.append((cond, crossing))

    lane_tok = lax.broadcasted_iota(jnp.int32, (tok_count, tok_count), 1)
    row_tok = lax.broadcasted_iota(jnp.int32, (tok_count, tok_count), 0)
    before = jnp.where(row_tok < lane_tok, 1.0, 0.0).astype(jnp.bfloat16)
    slot_row = lax.broadcasted_iota(jnp.int32, (tok_count, tok_count), 0).astype(jnp.float32)

    def process(n):
        table = blocks[n, width : width + E, :].astype(jnp.float32)
        present = table > 0.0
        earlier = dot(jnp.where(present, 1.0, 0.0).astype(jnp.bfloat16), before)
        slot = jnp.where(present, earlier, -1.0)
        comb = jnp.zeros((tok_count, tok_count), jnp.float32)
        for e in range(own):
            mine = expert_row == me * own + e
            slot_e = jnp.sum(jnp.where(mine, slot, 0.0), axis=0, keepdims=True)
            scale_e = jnp.sum(jnp.where(mine, table, 0.0), axis=0, keepdims=True)
            hit = (slot_row == slot_e + float(e * CAP)) & (slot_e >= 0.0)
            comb = jnp.where(hit, scale_e, comb)
        combine[n] = comb.T.astype(jnp.bfloat16)
        select = jnp.where(comb > 0.0, 1.0, 0.0).astype(jnp.bfloat16)[:slots]
        rows = dot(select, blocks[n, :width, :], ((1,), (1,))).astype(jnp.bfloat16)
        for e in range(own):
            picked[e, n] = rows[e * CAP : (e + 1) * CAP]

    for piece in (0, 1):
        for way in (0, 1):
            ag_send(way, 0, piece ^ way)
    o_begin()
    side_send(0)
    process(me)
    for i in range(0, width, 128):
        size = min(128, width - i)
        hid[:, i : i + size] = tok_t_ref[i : i + size, :].astype(jnp.float32).T
    for step in range(1, steps):
        for piece in (0, 1):
            for way in (0, 1):
                ag[way, step - 1, piece ^ way].wait_recv()
                if step < steps - 1 or piece == 0:
                    ag_send(way, step, piece ^ way)
        if step <= near:
            o_step(step)
        else:
            o_crossed(step - near - 1)
            side_send(1)
        process(at(-step))
        process(at(step))
    ag[0, steps - 1, 0].wait_recv()
    ag[1, steps - 1, 1].wait_recv()
    process(at(steps))

    o_crossed(1)
    side_send(2)
    q_begin()
    pos = {0: 1, 1: 2, 2: 3, 3: 4}
    half = dn.shape[1]
    chunk = CAP
    for e in range(own):
        for j in (2 * e, 2 * e + 1):
            gu_copies[j].wait()
            x = picked[e].reshape(count * CAP, width)
            proj[...] = dot(x, gu[j])

            @pl.loop(0, count)
            def _(i):
                r = pl.ds(pl.multiple_of(i * chunk, 16), chunk)
                gate = proj[r, :half]
                up = proj[r, half:]
                act[j % 2, r, :] = (gate * jax.nn.sigmoid(1.702 * gate) * (up + 1.0)).astype(jnp.bfloat16)

            if j < steps:
                q_step(j + 1)
        dn_copies[2 * e].wait()
        dn_copies[2 * e + 1].wait()
        result = dot(act[0], dn[2 * e]) + dot(act[1], dn[2 * e + 1])
        done[:, e * CAP : (e + 1) * CAP, :] = result.astype(jnp.bfloat16).reshape(count, CAP, width)
    for step in range(2 * own + 1, steps + 1):
        q_step(step)

    hrows = tok_count // 2
    tail = width % 128
    full = width - tail
    folds = 128 // tail
    trows = hrows // folds
    base = hrows * (full // 128)

    def part(n):
        value = dot(combine[n][:, :slots], done[n])
        for c in (0, 1):
            rows = value[c * hrows : (c + 1) * hrows]
            for i in range(0, full, 128):
                parts[n, c, i // 128 * hrows : (i // 128 + 1) * hrows, :] = rows[:, i : i + 128].astype(jnp.bfloat16)
            parts[n, c, base : base + trows, :] = jnp.concatenate(
                [rows[k * trows : (k + 1) * trows, full:] for k in range(folds)], axis=1
            ).astype(jnp.bfloat16)

    rs = {}

    def rs_add(goal, way, step, piece):
        here = held.at[way, step, piece]
        copy_to(here, here, rs_s.at[0, step, piece], rs_r.at[way, step, piece], seq=peers[0]).wait_recv()
        parts[goal, piece] = (
            parts[goal, piece].astype(jnp.float32) + held[way, step, piece].astype(jnp.float32)
        ).astype(jnp.bfloat16)

    def rs_send(way, step, piece):
        goal = at((steps - step) * (1 if way == 0 else -1))
        if (way, step - 1, piece) in rs:
            @pl.when(jnp.logical_not(corner_fresh[way]))
            def _():
                rs_add(goal, way, step - 1, piece)
        if step == steps - 1:
            @pl.when(inner_out[way])
            def _():
                rs_add(goal, 2, 2, piece)
            if piece == way:
                @pl.when(inner_in[way])
                def _():
                    rs_add(goal, 2, 0, piece)
        landing, peer = way, peers[way]
        if step < steps - 1:
            landing = jnp.where(inner_out[way], 2, way)
            peer = jnp.where(inner_out[way], beside, peer)
        rs[way, step, piece] = launch(copy_to(parts.at[goal, piece], held.at[landing, step, piece],
            rs_s.at[way, step, piece], rs_r.at[landing, step, piece], seq=peer))

    part(at(steps))
    rs_send(0, 0, 0)
    rs_send(1, 0, 1)
    for way in (0, 1):
        part(at((steps - 1) * (1 if way == 0 else -1)))
        rs_send(way, 1, 1 - way)
    for offset in range(steps - 2, 0, -1):
        part(at(offset))
        part(at(-offset))
    part(me)
    for hop in range(3):
        side_wait(hop)
    feed_send()
    rs_send(0, 1, 0)
    rs_send(1, 1, 1)
    for step in range(2, steps):
        for piece in (0, 1):
            for way in (0, 1):
                rs_send(way, step, 1 ^ piece ^ way)
        feed_cross(step - 2)
    feed_cross(2)
    for c in (0, 1):
        @pl.when(inner)
        def _():
            rs_add(me, 2, 1, c)
        for way in (0, 1):
            copy_to(held.at[way, steps - 1, c], held.at[way, steps - 1, c], rs_s.at[way, steps - 1, c],
                rs_r.at[way, steps - 1, c], seq=peers[way]).wait_recv()
        rows = slice(c * hrows, (c + 1) * hrows)
        value = (parts[me, c].astype(jnp.float32) + held[0, steps - 1, c].astype(jnp.float32)
            + held[1, steps - 1, c].astype(jnp.float32))
        for i in range(0, full, 128):
            term = value[i // 128 * hrows : (i // 128 + 1) * hrows]
            hid[rows, i : i + 128] = (hid[rows, i : i + 128] + term).astype(jnp.bfloat16).astype(jnp.float32)
        term = jnp.concatenate(
            [value[base : base + trows, k * tail : (k + 1) * tail] for k in range(folds)], axis=0)
        hid[rows, full:] = (hid[rows, full:] + term).astype(jnp.bfloat16).astype(jnp.float32)
    hidden = hid[...]
    scale = lax.rsqrt(jnp.sum(hidden * hidden, axis=1, keepdims=True) / width + eps)
    normed = hidden * scale * attn_gain_ref[...].reshape(1, width)
    shard = wq.shape[1]
    for i in range(count):
        both[core, i] = normed[:, i * shard : (i + 1) * shard].astype(jnp.bfloat16)
    pair = launch(copy_to(both.at[core], both.at[core], pair_s.at[0], pair_r.at[0], pipe=other_core))

    for key in qx:
        qx[key].wait_recv()

    def project(m, columns):
        total = None
        for i in range(count):
            x = both[:, i].reshape(2 * tok_count, shard) if m is None else both[m, i]
            term = dot(x, wq[i, :, columns])
            total = term if total is None else total + term
        return total.astype(jnp.bfloat16)

    kv[core] = project(core, pl.ds(0, 2 * kw))
    along = [launch(copy_to(kv.at[core], halo.at[core], halo_s.at[0], halo_r.at[0], seq=following))]
    pair.wait_recv()
    kv[other_core] = project(other_core, pl.ds(0, 2 * kw))
    along.append(launch(copy_to(kv.at[other_core], halo.at[other_core], halo_s.at[1], halo_r.at[1], seq=following)))
    queries[...] = project(None, pl.ds(2 * kw, qw)).reshape(2, tok_count, qw)
    for i in range(0, width, 128):
        size = min(128, width - i)
        hid_t[i : i + size, :] = hid[:, i : i + size].T
    for copy in along:
        copy.wait_recv()

    lane = lax.broadcasted_iota(jnp.int32, (tok_count, 2 * tok_count), 1)
    row = lax.broadcasted_iota(jnp.int32, (tok_count, 2 * tok_count), 0)
    left = lane < tok_count
    past = jnp.where(left, lane, lane - tok_count) > row
    low = lax.broadcasted_iota(jnp.int32, (tok_count, 2 * HEAD_SIZE), 1) < HEAD_SIZE

    def stacked(tile, head):
        tile = tile.astype(jnp.float32)
        kept = jnp.where(low if head == 0 else ~low, tile, 0.0)
        turned = pltpu.roll(kept, HEAD_SIZE, 1)
        pair_of = (kept, turned) if head == 0 else (turned, kept)
        return jnp.concatenate(pair_of, axis=0).astype(jnp.bfloat16)

    tiles = qw // 128
    per_head = tiles // 2
    for m in range(2):
        source = jnp.where(me == 0, 0, m)
        known = (me > 0) if m == 0 else (me >= 0)
        for head in range(2):
            k_own = stacked(kv[m, :, :kw], head)
            v_own = stacked(kv[m, :, kw:], head)
            k_past = stacked(halo[source, :, :kw], head)
            v_past = stacked(halo[source, :, kw:], head)
            for t in range(head * per_head, (head + 1) * per_head):
                first_head = core * 2 * tiles + 2 * t
                sink = jnp.exp(jnp.where(left[:1], sink_ref[first_head], sink_ref[first_head + 1]))
                x = queries[m, :, t * 128 : (t + 1) * 128]
                score = jnp.where(past, dot(x, k_past, ((1,), (1,))), dot(x, k_own, ((1,), (1,))))
                weight = jnp.exp(score * (float(HEAD_SIZE) ** -0.5))
                weight = jnp.where(past & jnp.logical_not(known), 0.0, weight)
                mass = jnp.where(left, jnp.sum(weight[:, :tok_count], axis=1, keepdims=True),
                    jnp.sum(weight[:, tok_count:], axis=1, keepdims=True)) + sink
                probs = weight / mass
                mixed[m, :, t * 128 : (t + 1) * 128] = (
                    dot(jnp.where(past, 0.0, probs).astype(jnp.bfloat16), v_own)
                    + dot(jnp.where(past, probs, 0.0).astype(jnp.bfloat16), v_past)
                ).astype(jnp.bfloat16)

    for cond, crossing in feed_crossings:
        @pl.when(cond)
        def _():
            crossing.wait_recv()

    share = wo.shape[2]

    def output(m):
        total = None
        for i in range(steps):
            term = dot(wo[i], mixed[m, :, i * share : (i + 1) * share], ((1,), (1,)))
            total = term if total is None else total + term
        return total

    given[...] = output(other_core).astype(jnp.bfloat16)
    last = launch(copy_to(given, back, pair_s.at[1], pair_r.at[1], pipe=other_core))
    kept = output(core)
    last.wait_recv()
    out_ref[...] = (hid_t[...] + kept + back[...].astype(jnp.float32)).astype(jnp.bfloat16)
    for _, copy in sends:
        copy.wait_send()
    for cond, copy in o_sends:
        @pl.when(cond)
        def _():
            copy.wait_send()


def whole_layer(
    tokens, routes, route_weights, moe_gain, gate_up, down_proj, attn_gain, qkv_proj,
    head_sink_logits, out_proj,
):
    count = lax.axis_size("seq")
    steps = count // 2
    tok_count, width = tokens.shape[1:]
    own = gate_up.shape[0] // 2
    half = down_proj.shape[1]
    heads = QUERY_HEADS // 2
    qw = heads * HEAD_SIZE
    kw = KEY_VALUE_HEADS * HEAD_SIZE // 2
    chunk = tok_count // 2 * width // 128
    dma = pltpu.SemaphoreType.DMA
    bf16 = jnp.bfloat16
    vm = pl.BlockSpec(memory_space=pltpu.VMEM)
    hbm = pl.BlockSpec(memory_space=pl.ANY)
    out = pl.pallas_call(
        layer_kernel,
        out_shape=jax.ShapeDtypeStruct((width, tok_count), bf16),
        in_specs=[vm] * 5 + [pl.BlockSpec(memory_space=pltpu.SMEM)] + [hbm] * 4,
        out_specs=vm,
        scratch_shapes=[
            pltpu.VMEM((count, width + E, tok_count), bf16),
            pltpu.VMEM((own, count, CAP, width), bf16),
            pltpu.VMEM((count, tok_count, tok_count), bf16),
            pltpu.VMEM(gate_up.shape, bf16),
            pltpu.VMEM(down_proj.shape, bf16),
            pltpu.VMEM((count * CAP, 2 * half), jnp.float32),
            pltpu.VMEM((2, count * CAP, half), bf16),
            pltpu.VMEM((count, own * CAP, width), bf16),
            pltpu.VMEM((count, 2, chunk, 128), bf16),
            pltpu.VMEM((3, steps, 2, chunk, 128), bf16),
            pltpu.VMEM((count, qkv_proj.shape[0], 2 * kw + qw), bf16),
            pltpu.VMEM((steps, width, out_proj.shape[0]), bf16),
            pltpu.VMEM((2, count, tok_count, qkv_proj.shape[0]), bf16),
            pltpu.VMEM((2, tok_count, 2 * kw), bf16),
            pltpu.VMEM((2, tok_count, 2 * kw), bf16),
            pltpu.VMEM((2, tok_count, qw), bf16),
            pltpu.VMEM((2, tok_count, qw), bf16),
            pltpu.VMEM((width, tok_count), bf16),
            pltpu.VMEM((width, tok_count), bf16),
            pltpu.VMEM((tok_count, width), jnp.float32),
            pltpu.VMEM((width, tok_count), jnp.float32),
            dma((2 * own,)), dma((2 * own,)), dma((3,)), dma((1,)),
            dma((2, steps, 2)), dma((2, steps, 2)), dma((2, steps, 2)), dma((3, steps, 2)),
            dma((2, steps)), dma((2, steps)), dma((2, steps)), dma((2, steps)),
            dma((2, steps)), dma((2, steps)), dma((2, steps)), dma((2, steps)),
            dma((3,)), dma((3,)), dma((3,)), dma((3,)), dma((3,)), dma((3,)), dma((2,)), dma((2,)), dma((2,)), dma((2,)),
        ],
        compiler_params=pltpu.CompilerParams(
            collective_id=0, has_side_effects=True, vmem_limit_bytes=67043328),
    )(tokens[0].T, routes[0].T, route_weights[0].T, moe_gain, attn_gain, head_sink_logits,
      gate_up, down_proj, qkv_proj, out_proj.T)
    return out.T[None]


def solution(mesh):
    in_specs = (
        P("pipe", ("groups", "seq"), None),
        P("pipe", ("groups", "seq"), None),
        P("pipe", ("groups", "seq"), None),
        P(),
        P("seq", None, None),
        P("seq", None, None),
        P(),
        P("seq", None),
        P(),
        P("seq", None),
    )
    out_specs = P("pipe", ("groups", "seq"), None)
    seq_count, pipe_count, group_count = mesh.shape["seq"], mesh.shape["pipe"], mesh.shape["groups"]
    whole = (
        pipe_count == 2
        and group_count == 2
        and seq_count % 2 == 0
        and 2 * E // seq_count == 4
        and seq_count == 8
        and QUERY_HEADS % (2 * seq_count) == 0
    )
    return jax.shard_map(
        whole_layer if whole else body, mesh=mesh, in_specs=in_specs, out_specs=out_specs, check_vma=False
    )
```

```python
import functools

import jax
import jax.numpy as jnp
from jax import lax
from jax.experimental import pallas as pl
from jax.experimental.pallas import tpu as pltpu
from jax.sharding import PartitionSpec as P

MESH = pl.DeviceIdType.MESH
E = 16
TOP = 4
QUERY_HEADS = 32
KEY_VALUE_HEADS = 4
HEAD_SIZE = 64
WINDOW_SPAN = 128
HALF = 720
CAP = 48


eps = 1e-05


def from_partner(value, axis, distance):
    return lax.ppermute(value, axis, [(i, i ^ 1 << distance) for i in range(lax.axis_size(axis))])


def shifted(value, axis, steps):
    count = lax.axis_size(axis)
    pairs = [(source, (source + steps) % count) for source in range(count)]
    return lax.ppermute(value, axis, pairs)


def passed_along(value, axis, steps):
    count = lax.axis_size(axis)
    first, last = (max(0, -steps), min(count, count - steps))
    return lax.ppermute(value, axis, [(source, source + steps) for source in range(first, last)])


def rms_scale(value_matrix, gain):
    widened = value_matrix.astype(jnp.float32)
    mean_square = jnp.mean(widened * widened, axis=-1, keepdims=True)
    return (widened * lax.rsqrt(mean_square + eps) * gain).astype(jnp.bfloat16)


def slot_positions(route_rows):
    flat = route_rows.reshape(-1)
    onehot = (flat[:, None] == jnp.arange(E, dtype=jnp.int32)[None, :]).astype(jnp.int32)
    earlier = jnp.cumsum(onehot, axis=0) - onehot
    return flat * CAP + jnp.sum(earlier * onehot, axis=1)


def expert_layer(local, route_rows, route_scale, moe_gain, gate_up, down_proj):
    tok_count, width = local.shape
    seq_count = lax.axis_size("seq")
    per_device = gate_up.shape[0]
    normed = rms_scale(local, moe_gain)
    positions = slot_positions(route_rows)
    select = (positions[None, :] == jnp.arange(E * CAP, dtype=jnp.int32)[:, None]).astype(
        jnp.bfloat16
    )
    repeated = jnp.repeat(normed, TOP, axis=0)
    table = jnp.dot(select, repeated, preferred_element_type=jnp.float32).astype(jnp.bfloat16)
    by_expert = table.reshape(E, CAP, width)
    first = lax.axis_index("seq") % 2 == 0
    outgoing = jnp.repeat(by_expert, 2, axis=0).reshape(seq_count, per_device, CAP, width)
    received = lax.all_to_all(outgoing, "seq", split_axis=0, concat_axis=0, tiled=True)
    projected = jnp.einsum("spcd,pdh->spch", received, gate_up, preferred_element_type=jnp.float32)
    gate_part = projected[..., :HALF]
    up_part = projected[..., HALF:]
    hidden = (gate_part * jax.nn.sigmoid(1.702 * gate_part) * (up_part + 1.0)).astype(jnp.bfloat16)
    partial_value = jnp.einsum(
        "spch,phd->spcd", hidden, down_proj, preferred_element_type=jnp.float32
    )
    if per_device >= 2:
        finished = (
            partial_value.reshape(seq_count, per_device // 2, 2, CAP, width)
            .sum(axis=2)
            .astype(jnp.bfloat16)
        )
    else:
        lower_rows = partial_value[:, :, : CAP // 2]
        upper_rows = partial_value[:, :, CAP // 2 :]
        kept = jnp.where(first, lower_rows, upper_rows)
        given = jnp.where(first, upper_rows, lower_rows)
        partner_part = from_partner(given.astype(jnp.bfloat16), "seq", 0).astype(given.dtype)
        finished = (kept + partner_part).astype(jnp.bfloat16)
    summed = lax.all_to_all(finished, "seq", split_axis=0, concat_axis=0, tiled=True).reshape(
        E * CAP, width
    )
    picked = lax.dot_general(
        select, summed, (((0,), (0,)), ((), ())), preferred_element_type=jnp.float32
    )
    weighted = jnp.sum(picked.reshape(tok_count, TOP, width) * route_scale[:, :, None], axis=1)
    return (local.astype(jnp.float32) + weighted).astype(jnp.bfloat16)


def attend(query_matrix, keys_extended, values_extended, head_sink_logits, halo_valid):
    tok_count = query_matrix.shape[0]
    query_groups = QUERY_HEADS // KEY_VALUE_HEADS
    attention_block = min(tok_count, 512)
    scale = float(HEAD_SIZE) ** (-0.5)
    sink_mass_total = jnp.exp(head_sink_logits).reshape(KEY_VALUE_HEADS, query_groups, 1, 1)
    block_queries = query_matrix.reshape(attention_block, KEY_VALUE_HEADS, query_groups, HEAD_SIZE)
    block_keys = keys_extended.reshape(attention_block + WINDOW_SPAN, KEY_VALUE_HEADS, HEAD_SIZE)
    block_values = values_extended.reshape(
        attention_block + WINDOW_SPAN, KEY_VALUE_HEADS, HEAD_SIZE
    )
    scores = (
        jnp.einsum("qhgd,khd->hgqk", block_queries, block_keys, preferred_element_type=jnp.float32)
        * scale
    )
    query_pos = jnp.arange(attention_block, dtype=jnp.int32)[:, None] + WINDOW_SPAN
    key_pos = jnp.arange(attention_block + WINDOW_SPAN, dtype=jnp.int32)[None, :]
    distance = query_pos - key_pos
    allowed = (
        (distance >= 0) & (distance < WINDOW_SPAN) & ((key_pos + 0 >= WINDOW_SPAN) | halo_valid)
    )
    weights = jnp.where(allowed, jnp.exp(scores), 0.0)
    probs = (weights / (jnp.sum(weights, axis=-1, keepdims=True) + sink_mass_total)).astype(
        jnp.bfloat16
    )
    mixed = jnp.einsum("hgqk,khd->qhgd", probs, block_values, preferred_element_type=jnp.float32)
    outputs = mixed.reshape(attention_block, QUERY_HEADS * HEAD_SIZE).astype(jnp.bfloat16)
    return outputs


def body(
    tokens,
    routes,
    route_weights,
    moe_gain,
    gate_up,
    down_proj,
    attn_gain,
    qkv_proj,
    head_sink_logits,
    out_proj,
):
    hidden = expert_layer(tokens[0], routes[0], route_weights[0], moe_gain, gate_up, down_proj)
    tok_count, width = hidden.shape
    normed = rms_scale(hidden, attn_gain)
    seq_index = lax.axis_index("seq")
    pipe_index = lax.axis_index("pipe")
    halo_valid = (seq_index > 0) | (pipe_index > 0)
    query_width = QUERY_HEADS * HEAD_SIZE
    width_of_pair = KEY_VALUE_HEADS * HEAD_SIZE
    columns = normed
    packed_heads = jnp.dot(
        columns,
        lax.all_gather(qkv_proj, "seq", axis=0, tiled=True),
        preferred_element_type=jnp.float32,
    ).astype(jnp.bfloat16)
    from_left = shifted(packed_heads[tok_count - WINDOW_SPAN :, query_width:], "seq", 1)
    from_section = passed_along(from_left, "pipe", 1)
    halo_pairs = jnp.where(seq_index == 0, from_section, from_left)
    query_matrix = packed_heads[:, :query_width]
    pairs_ext = jnp.concatenate([halo_pairs, packed_heads[:, query_width:]], axis=0)
    keys_extended = pairs_ext[:, :width_of_pair]
    values_extended = pairs_ext[:, width_of_pair:]
    attended = attend(query_matrix, keys_extended, values_extended, head_sink_logits, halo_valid)
    columns = attended
    projected = jnp.dot(
        columns,
        lax.all_gather(out_proj, "seq", axis=0, tiled=True),
        preferred_element_type=jnp.float32,
    )
    return (hidden.astype(jnp.float32) + projected).astype(jnp.bfloat16)[None]


def ring_place(index, count, folded):
    if not folded:
        return index
    line, side = index // 2, index % 2
    return line + side * (count - 1 - 2 * line)

def ring_index(place, count, folded):
    if not folded:
        return place
    side = place // (count // 2)
    line = place + side * (count - 1 - 2 * place)
    return 2 * line + side


def copy_to(src, dst, send, recv, **device):
    return pltpu.make_async_remote_copy(src_ref=src, dst_ref=dst, send_sem=send, recv_sem=recv,
        device_id=device, device_id_type=MESH)


def dot(a, b, dims=((1,), (0,))):
    return lax.dot_general(a, b, (dims, ((), ())), preferred_element_type=jnp.float32)


def layer_kernel(
    tok_t_ref, routes_ref, weights_ref, gain_ref, attn_gain_ref, sink_ref,
    gate_up_ref, down_ref, qkv_ref, out_t_ref,
    out_ref,
    blocks, picked, combine, gu, dn, proj, act, done, parts, held, wq, wo,
    both, kv, halo, queries, mixed, given, back, hid, hid_t, passed,
    gu_sem, dn_sem, wq_sem, wo_sem, ag_s, ag_r, rs_s, rs_r, q_s, q_r, qx_s, qx_r,
    o_s, o_r, ox_s, ox_r, side_s, side_r, feed_s, feed_r, fx_s, fx_r, pair_s, pair_r, halo_s, halo_r,
):
    count = lax.axis_size("seq")
    steps = count // 2
    me = lax.axis_index("seq")
    core = lax.axis_index("pipe")
    group = lax.axis_index("groups")
    width, tok_count = tok_t_ref.shape
    own = picked.shape[0]
    slots = own * CAP
    place = ring_place(me, count, True)
    at = lambda offset: ring_index(lax.rem(place + offset + count, count), count, True)
    spot = lambda p: ring_index(lax.rem(p + count, count), count, True)
    peers = (at(1), at(-1))
    column = lax.rem(place, steps)
    inner = (column > 0) & (column < steps - 1)
    corner = jnp.logical_not(inner)
    low = column < steps // 2
    toward = jnp.where(low, 1, -1)
    outward = (jnp.logical_not(low), low)
    inner_out = [inner & outward[way] for way in (0, 1)]
    inner_in = [inner & jnp.logical_not(outward[way]) for way in (0, 1)]
    corner_fresh = [corner & outward[way] for way in (0, 1)]
    beside_place = count - 1 - place
    beside = spot(beside_place)
    following, preceding = lax.rem(me + 1, count), lax.rem(me + count - 1, count)
    other_core, other_group = 1 - core, 1 - group
    sends = []

    def launch(copy):
        copy.start()
        sends.append((None, copy))
        return copy

    barrier = pltpu.get_barrier_semaphore()
    for device in ({"seq": peers[0]}, {"seq": peers[1]}, {"seq": following}, {"seq": preceding},
                   {"pipe": other_core}, {"groups": other_group}, {"seq": beside}):
        pl.semaphore_signal(barrier, inc=1, device_id=device, device_id_type=MESH)
    qw, kw = queries.shape[2], kv.shape[2] // 2
    all_q = QUERY_HEADS * HEAD_SIZE
    all_k = KEY_VALUE_HEADS * HEAD_SIZE
    wo_slot = lax.rem(me, steps)
    holds = lambda origin: lax.div(origin, steps) == core
    wo_copy = pltpu.make_async_copy(out_t_ref, wo.at[wo_slot], wo_sem.at[0])

    @pl.when(holds(me))
    def _():
        wo_copy.start()

    wq_copies = []
    for i, (source, goal, size) in enumerate((
        (all_q + core * kw, 0, kw), (all_q + all_k + core * kw, kw, kw), (core * qw, 2 * kw, qw))):
        wq_copies.append(pltpu.make_async_copy(
            qkv_ref.at[:, pl.ds(pl.multiple_of(source, 128), size)],
            wq.at[me, :, pl.ds(goal, size)], wq_sem.at[i]))
    for copy in wq_copies:
        copy.start()
    gu_copies = [pltpu.make_async_copy(gate_up_ref.at[j], gu.at[j], gu_sem.at[j]) for j in range(2 * own)]
    dn_copies = [pltpu.make_async_copy(down_ref.at[j], dn.at[j], dn_sem.at[j]) for j in range(2 * own)]
    for copy in gu_copies + dn_copies:
        copy.start()

    tall = tok_t_ref[...].astype(jnp.float32)
    scale = lax.rsqrt(jnp.sum(tall * tall, axis=0, keepdims=True) / width + eps)
    for i in range(0, width, 128):
        size = min(128, width - i)
        gain = jnp.broadcast_to(gain_ref[pl.ds(i, size)].reshape(1, size), (tok_count, size)).T
        blocks[me, i : i + size, :] = (
            tok_t_ref[i : i + size, :].astype(jnp.float32) * scale * gain
        ).astype(jnp.bfloat16)
    expert_row = lax.broadcasted_iota(jnp.int32, (E, tok_count), 0)
    dense = jnp.zeros((E, tok_count), jnp.float32)
    for j in range(TOP):
        dense = dense + jnp.where(expert_row == routes_ref[j : j + 1, :], weights_ref[j : j + 1, :], 0.0)
    blocks[me, width : width + E, :] = dense.astype(jnp.bfloat16)

    pl.semaphore_wait(barrier, 7)

    rows_all = blocks.shape[1]
    cut = (rows_all // 2 + 15) // 16 * 16
    pieces = (pl.ds(0, cut), pl.ds(cut, rows_all - cut))
    ag = {}

    def ag_send(way, step, piece):
        origin = at(-step if way == 0 else step)
        ref = blocks.at[origin, pieces[piece]]
        ag[way, step, piece] = launch(copy_to(ref, ref, ag_s.at[way, step, piece], ag_r.at[way, step, piece], seq=peers[way]))

    qcols = wq.shape[2] // 2
    qcut = (qcols // 2 + 127) // 128 * 128
    q = {}
    qx = {}

    def q_part(way, step):
        base = pl.multiple_of(group * qcols, 128)
        if step < steps - 1:
            return pl.ds(base, qcols)
        return pl.ds(base, qcut) if way == 0 else pl.ds(base + qcut, qcols - qcut)

    def q_send(way, step):
        ref = wq.at[at(-step if way == 0 else step), :, q_part(way, step)]
        q[way, step] = launch(copy_to(ref, ref, q_s.at[way, step], q_r.at[way, step], seq=peers[way]))

    def q_cross(way, step):
        q[way, step].wait_recv()
        ref = wq.at[at(-step - 1 if way == 0 else step + 1), :, q_part(way, step)]
        qx[way, step] = launch(copy_to(ref, ref, qx_s.at[way, step], qx_r.at[way, step], groups=other_group))

    def q_begin():
        for copy in wq_copies:
            copy.wait()
        for way in (0, 1):
            q_send(way, 0)

    def q_step(step):
        for way in (0, 1):
            q_cross(way, step - 1)
            if step < steps:
                q_send(way, step)

    orows = wo.shape[1] // 2
    ocut = (orows // 2 + 15) // 16 * 16
    o_sends = []

    def o_part(way, step):
        base = pl.multiple_of(group * orows, 16)
        if step < steps - 1:
            return pl.ds(base, orows)
        return pl.ds(base, ocut) if way == 0 else pl.ds(pl.multiple_of(base + ocut, 16), orows - ocut)

    def o_copy(way, step):
        origin = at(-step if way == 0 else step)
        ref = wo.at[lax.rem(origin, steps), o_part(way, step)]
        return holds(origin), copy_to(ref, ref, o_s.at[way, step], o_r.at[way, step], seq=peers[way])

    def o_landed(way, step):
        origin = at(-step - 1 if way == 0 else step + 1)
        ref = wo.at[lax.rem(origin, steps), o_part(way, step)]
        return (holds(origin), copy_to(ref, ref, o_s.at[way, step], o_r.at[way, step], seq=peers[way]),
                copy_to(ref, ref, ox_s.at[way, step], ox_r.at[way, step], groups=other_group))

    def o_begin():
        @pl.when(holds(me))
        def _():
            wo_copy.wait()
        for way in (0, 1):
            cond, copy = o_copy(way, 0)

            @pl.when(cond)
            def _():
                copy.start()
            o_sends.append((cond, copy))

    near = steps // 2

    def o_step(step):
        for way in (0, 1):
            cond, arrived, crossing = o_landed(way, step - 1)

            @pl.when(cond)
            def _():
                arrived.wait_recv()
                crossing.start()
            o_sends.append((cond, crossing))
            if step < near:
                onward, copy = o_copy(way, step)

                @pl.when(onward)
                def _():
                    copy.start()
                o_sends.append((onward, copy))

    def o_crossed(step):
        for way in (0, 1):
            cond, _, crossing = o_landed(way, step)

            @pl.when(cond)
            def _():
                crossing.wait_recv()

    def side_copy(origin, hop):
        ref = wo.at[lax.rem(origin, steps)]
        return inner & holds(origin), copy_to(ref, ref, side_s.at[hop], side_r.at[hop], seq=beside)

    def side_send(hop):
        cond, copy = side_copy(at(toward * hop), hop)

        @pl.when(cond)
        def _():
            copy.start()
        o_sends.append((cond, copy))

    def side_wait(hop):
        cond, copy = side_copy(spot(beside_place - toward * hop), hop)

        @pl.when(cond)
        def _():
            copy.wait_recv()

    feed_part = pl.ds(pl.multiple_of(group * orows, 16), orows)

    def feed_copy(origin, index):
        ref = wo.at[lax.rem(origin, steps), feed_part]
        return holds(origin), copy_to(ref, ref, feed_s.at[index], feed_r.at[index], seq=spot(place - toward))

    def feed_send():
        for index, origin in enumerate((
            at(2 * toward), spot(beside_place - toward), spot(beside_place - 2 * toward))):
            cond, copy = feed_copy(origin, index)

            @pl.when(inner & cond)
            def _():
                copy.start()
            o_sends.append((inner & cond, copy))

    feed_crossings = []

    def feed_cross(index):
        origin = (spot(place + 3 * toward), spot(beside_place - 2 * toward), spot(beside_place - 3 * toward))[index]
        held_here, landed = feed_copy(origin, index)
        cond = corner & held_here
        ref = wo.at[lax.rem(origin, steps), feed_part]
        crossing = copy_to(ref, ref, fx_s.at[index], fx_r.at[index], groups=other_group)

        @pl.when(cond)
        def _():
            landed.wait_recv()
            crossing.start()
        o_sends.append((cond, crossing))
        feed_crossings.append((cond, crossing))

    lane_tok = lax.broadcasted_iota(jnp.int32, (tok_count, tok_count), 1)
    row_tok = lax.broadcasted_iota(jnp.int32, (tok_count, tok_count), 0)
    before = jnp.where(row_tok < lane_tok, 1.0, 0.0).astype(jnp.bfloat16)
    slot_row = lax.broadcasted_iota(jnp.int32, (tok_count, tok_count), 0).astype(jnp.float32)

    def process(n):
        table = blocks[n, width : width + E, :].astype(jnp.float32)
        present = table > 0.0
        earlier = dot(jnp.where(present, 1.0, 0.0).astype(jnp.bfloat16), before)
        slot = jnp.where(present, earlier, -1.0)
        comb = jnp.zeros((tok_count, tok_count), jnp.float32)
        for e in range(own):
            mine = expert_row == me * own + e
            slot_e = jnp.sum(jnp.where(mine, slot, 0.0), axis=0, keepdims=True)
            scale_e = jnp.sum(jnp.where(mine, table, 0.0), axis=0, keepdims=True)
            hit = (slot_row == slot_e + float(e * CAP)) & (slot_e >= 0.0)
            comb = jnp.where(hit, scale_e, comb)
        combine[n] = comb.T.astype(jnp.bfloat16)
        select = jnp.where(comb > 0.0, 1.0, 0.0).astype(jnp.bfloat16)[:slots]
        rows = dot(select, blocks[n, :width, :], ((1,), (1,))).astype(jnp.bfloat16)
        for e in range(own):
            picked[e, n] = rows[e * CAP : (e + 1) * CAP]

    for piece in (0, 1):
        for way in (0, 1):
            ag_send(way, 0, piece ^ way)
    o_begin()
    side_send(0)
    process(me)
    for i in range(0, width, 128):
        size = min(128, width - i)
        hid[:, i : i + size] = tok_t_ref[i : i + size, :].astype(jnp.float32).T
    for step in range(1, steps):
        for piece in (0, 1):
            for way in (0, 1):
                ag[way, step - 1, piece ^ way].wait_recv()
                if step < steps - 1 or piece == 0:
                    ag_send(way, step, piece ^ way)
        if step <= near:
            o_step(step)
        else:
            o_crossed(step - near - 1)
            side_send(1)
        process(at(-step))
        process(at(step))
    ag[0, steps - 1, 0].wait_recv()
    ag[1, steps - 1, 1].wait_recv()
    process(at(steps))

    o_crossed(1)
    side_send(2)
    q_begin()
    pos = {0: 1, 1: 2, 2: 3, 3: 4}
    half = dn.shape[1]
    chunk = CAP
    for e in range(own):
        for j in (2 * e, 2 * e + 1):
            gu_copies[j].wait()
            x = picked[e].reshape(count * CAP, width)
            proj[...] = dot(x, gu[j])

            @pl.loop(0, count)
            def _(i):
                r = pl.ds(pl.multiple_of(i * chunk, 16), chunk)
                gate = proj[r, :half]
                up = proj[r, half:]
                act[j % 2, r, :] = (gate * jax.nn.sigmoid(1.702 * gate) * (up + 1.0)).astype(jnp.bfloat16)

            if j < steps:
                q_step(j + 1)
        dn_copies[2 * e].wait()
        dn_copies[2 * e + 1].wait()
        result = dot(act[0], dn[2 * e]) + dot(act[1], dn[2 * e + 1])
        done[:, e * CAP : (e + 1) * CAP, :] = result.astype(jnp.bfloat16).reshape(count, CAP, width)
    for step in range(2 * own + 1, steps + 1):
        q_step(step)

    hrows = tok_count // 2
    tail = width % 128
    full = width - tail
    folds = 128 // tail
    trows = hrows // folds
    base = hrows * (full // 128)

    def part(n):
        value = dot(combine[n][:, :slots], done[n])
        for c in (0, 1):
            rows = value[c * hrows : (c + 1) * hrows]
            for i in range(0, full, 128):
                parts[n, c, i // 128 * hrows : (i // 128 + 1) * hrows, :] = rows[:, i : i + 128].astype(jnp.bfloat16)
            parts[n, c, base : base + trows, :] = jnp.concatenate(
                [rows[k * trows : (k + 1) * trows, full:] for k in range(folds)], axis=1
            ).astype(jnp.bfloat16)

    rs = {}

    def rs_add(goal, way, step, piece):
        here = held.at[way, step, piece]
        copy_to(here, here, rs_s.at[0, step, piece], rs_r.at[way, step, piece], seq=peers[0]).wait_recv()
        parts[goal, piece] = (
            parts[goal, piece].astype(jnp.float32) + held[way, step, piece].astype(jnp.float32)
        ).astype(jnp.bfloat16)

    def rs_send(way, step, piece):
        goal = at((steps - step) * (1 if way == 0 else -1))
        if (way, step - 1, piece) in rs:
            @pl.when(jnp.logical_not(corner_fresh[way]))
            def _():
                rs_add(goal, way, step - 1, piece)
        if step == steps - 1:
            @pl.when(inner_out[way])
            def _():
                rs_add(goal, 2, 2, piece)
            if piece == way:
                @pl.when(inner_in[way])
                def _():
                    rs_add(goal, 2, 0, piece)
        landing, peer = way, peers[way]
        if step < steps - 1:
            landing = jnp.where(inner_out[way], 2, way)
            peer = jnp.where(inner_out[way], beside, peer)
        rs[way, step, piece] = launch(copy_to(parts.at[goal, piece], held.at[landing, step, piece],
            rs_s.at[way, step, piece], rs_r.at[landing, step, piece], seq=peer))

    part(at(steps))
    rs_send(0, 0, 0)
    rs_send(1, 0, 1)
    for way in (0, 1):
        part(at((steps - 1) * (1 if way == 0 else -1)))
        rs_send(way, 1, 1 - way)
    for offset in range(steps - 2, 0, -1):
        part(at(offset))
        part(at(-offset))
    part(me)
    for hop in range(3):
        side_wait(hop)
    feed_send()
    rs_send(0, 1, 0)
    rs_send(1, 1, 1)
    for step in range(2, steps):
        for piece in (0, 1):
            for way in (0, 1):
                rs_send(way, step, 1 ^ piece ^ way)
        feed_cross(step - 2)
    feed_cross(2)
    for c in (0, 1):
        @pl.when(inner)
        def _():
            rs_add(me, 2, 1, c)
        for way in (0, 1):
            copy_to(held.at[way, steps - 1, c], held.at[way, steps - 1, c], rs_s.at[way, steps - 1, c],
                rs_r.at[way, steps - 1, c], seq=peers[way]).wait_recv()
        rows = slice(c * hrows, (c + 1) * hrows)
        value = (parts[me, c].astype(jnp.float32) + held[0, steps - 1, c].astype(jnp.float32)
            + held[1, steps - 1, c].astype(jnp.float32))
        for i in range(0, full, 128):
            term = value[i // 128 * hrows : (i // 128 + 1) * hrows]
            hid[rows, i : i + 128] = (hid[rows, i : i + 128] + term).astype(jnp.bfloat16).astype(jnp.float32)
        term = jnp.concatenate(
            [value[base : base + trows, k * tail : (k + 1) * tail] for k in range(folds)], axis=0)
        hid[rows, full:] = (hid[rows, full:] + term).astype(jnp.bfloat16).astype(jnp.float32)
    hidden = hid[...]
    scale = lax.rsqrt(jnp.sum(hidden * hidden, axis=1, keepdims=True) / width + eps)
    normed = hidden * scale * attn_gain_ref[...].reshape(1, width)
    shard = wq.shape[1]
    for i in range(count):
        both[core, i] = normed[:, i * shard : (i + 1) * shard].astype(jnp.bfloat16)
    pair = launch(copy_to(both.at[core], both.at[core], pair_s.at[0], pair_r.at[0], pipe=other_core))

    for key in qx:
        qx[key].wait_recv()

    def project(m, columns):
        total = None
        for i in range(count):
            x = both[:, i].reshape(2 * tok_count, shard) if m is None else both[m, i]
            term = dot(x, wq[i, :, columns])
            total = term if total is None else total + term
        return total

    kv[core] = project(core, pl.ds(0, 2 * kw)).astype(jnp.bfloat16)
    along = [launch(copy_to(kv.at[core], halo.at[core], halo_s.at[0], halo_r.at[0], seq=following))]
    for i in range(0, width, 128):
        size = min(128, width - i)
        hid_t[i : i + size, :] = hid[:, i : i + size].T
    pair.wait_recv()
    kv[other_core] = project(other_core, pl.ds(0, 2 * kw)).astype(jnp.bfloat16)
    along.append(launch(copy_to(kv.at[other_core], halo.at[other_core], halo_s.at[1], halo_r.at[1], seq=following)))
    packed = project(None, pl.ds(2 * kw, qw)).astype(jnp.bfloat16)
    queries[...] = (packed * (float(HEAD_SIZE) ** -0.5)).reshape(2, tok_count, qw)

    lane = lax.broadcasted_iota(jnp.int32, (tok_count, 2 * tok_count), 1)
    row = lax.broadcasted_iota(jnp.int32, (tok_count, 2 * tok_count), 0)
    left = lane < tok_count
    past = jnp.where(left, lane, lane - tok_count) > row
    low = lax.broadcasted_iota(jnp.int32, (tok_count, 2 * HEAD_SIZE), 1) < HEAD_SIZE

    def stacked(tile, head):
        tile = tile.astype(jnp.float32)
        kept = jnp.where(low if head == 0 else ~low, tile, 0.0)
        turned = pltpu.roll(kept, HEAD_SIZE, 1)
        pair_of = (kept, turned) if head == 0 else (turned, kept)
        return jnp.concatenate(pair_of, axis=0).astype(jnp.bfloat16)

    tiles = qw // 128
    per_head = tiles // 2

    def attention(m, known):
        past_kv = passed[...]
        dropped = past & jnp.logical_not(known)
        for head in range(2):
            k_own = stacked(kv[m, :, :kw], head)
            v_own = stacked(kv[m, :, kw:], head)
            k_past = stacked(past_kv[:, :kw], head)
            v_past = stacked(past_kv[:, kw:], head)
            for t in range(head * per_head, (head + 1) * per_head):
                first_head = core * 2 * tiles + 2 * t
                sink_a = jnp.exp(jnp.full((1, 1), sink_ref[first_head]))
                sink_b = jnp.exp(jnp.full((1, 1), sink_ref[first_head + 1]))
                x = queries[m, :, t * 128 : (t + 1) * 128]
                score = jnp.where(past, dot(x, k_past, ((1,), (1,))), dot(x, k_own, ((1,), (1,))))
                weight = jnp.where(dropped, 0.0, jnp.exp(score))
                mass_a = jnp.sum(weight[:, :tok_count], axis=1, keepdims=True) + sink_a
                mass_b = jnp.sum(weight[:, tok_count:], axis=1, keepdims=True) + sink_b
                probs = weight * jnp.where(left, 1.0 / mass_a, 1.0 / mass_b)
                mixed[m, :, t * 128 : (t + 1) * 128] = (
                    dot(jnp.where(past, 0.0, probs).astype(jnp.bfloat16), v_own)
                    + dot(jnp.where(past, probs, 0.0).astype(jnp.bfloat16), v_past)
                ).astype(jnp.bfloat16)

    share = wo.shape[2]
    last = copy_to(given, back, pair_s.at[1], pair_r.at[1], pipe=other_core)

    def output(m):
        total = None
        for i in range(steps):
            term = dot(wo[i], mixed[m, :, i * share : (i + 1) * share], ((1,), (1,)))
            total = term if total is None else total + term

        @pl.when(m == other_core)
        def _():
            given[...] = total.astype(jnp.bfloat16)
            last.start()

        @pl.when(m == core)
        def _():
            hid_t[...] = hid_t[...] + total

    early = jnp.where(me == 0, 0, other_core)
    late = 1 - early

    @pl.when(me > 0)
    def _():
        for copy in along:
            copy.wait_recv()
        passed[...] = halo[other_core]

    @pl.when(me == 0)
    def _():
        passed[...] = jnp.zeros_like(passed)
    attention(early, me > 0)
    for cond, crossing in feed_crossings:
        @pl.when(cond)
        def _():
            crossing.wait_recv()
    output(early)

    @pl.when(me == 0)
    def _():
        for copy in along:
            copy.wait_recv()
    passed[...] = halo[jnp.where(me == 0, 0, core)]
    attention(late, me >= 0)
    output(late)
    last.wait_recv()
    out_ref[...] = (hid_t[...] + back[...].astype(jnp.float32)).astype(jnp.bfloat16)
    last.wait_send()
    for _, copy in sends:
        copy.wait_send()
    for cond, copy in o_sends:
        @pl.when(cond)
        def _():
            copy.wait_send()


def whole_layer(
    tokens, routes, route_weights, moe_gain, gate_up, down_proj, attn_gain, qkv_proj,
    head_sink_logits, out_proj,
):
    count = lax.axis_size("seq")
    steps = count // 2
    tok_count, width = tokens.shape[1:]
    own = gate_up.shape[0] // 2
    half = down_proj.shape[1]
    heads = QUERY_HEADS // 2
    qw = heads * HEAD_SIZE
    kw = KEY_VALUE_HEADS * HEAD_SIZE // 2
    chunk = tok_count // 2 * width // 128
    dma = pltpu.SemaphoreType.DMA
    bf16 = jnp.bfloat16
    vm = pl.BlockSpec(memory_space=pltpu.VMEM)
    hbm = pl.BlockSpec(memory_space=pl.ANY)
    out = pl.pallas_call(
        layer_kernel,
        out_shape=jax.ShapeDtypeStruct((width, tok_count), bf16),
        in_specs=[vm] * 5 + [pl.BlockSpec(memory_space=pltpu.SMEM)] + [hbm] * 4,
        out_specs=vm,
        scratch_shapes=[
            pltpu.VMEM((count, width + E, tok_count), bf16),
            pltpu.VMEM((own, count, CAP, width), bf16),
            pltpu.VMEM((count, tok_count, tok_count), bf16),
            pltpu.VMEM(gate_up.shape, bf16),
            pltpu.VMEM(down_proj.shape, bf16),
            pltpu.VMEM((count * CAP, 2 * half), jnp.float32),
            pltpu.VMEM((2, count * CAP, half), bf16),
            pltpu.VMEM((count, own * CAP, width), bf16),
            pltpu.VMEM((count, 2, chunk, 128), bf16),
            pltpu.VMEM((3, steps, 2, chunk, 128), bf16),
            pltpu.VMEM((count, qkv_proj.shape[0], 2 * kw + qw), bf16),
            pltpu.VMEM((steps, width, out_proj.shape[0]), bf16),
            pltpu.VMEM((2, count, tok_count, qkv_proj.shape[0]), bf16),
            pltpu.VMEM((2, tok_count, 2 * kw), bf16),
            pltpu.VMEM((2, tok_count, 2 * kw), bf16),
            pltpu.VMEM((2, tok_count, qw), bf16),
            pltpu.VMEM((2, tok_count, qw), bf16),
            pltpu.VMEM((width, tok_count), bf16),
            pltpu.VMEM((width, tok_count), bf16),
            pltpu.VMEM((tok_count, width), jnp.float32),
            pltpu.VMEM((width, tok_count), jnp.float32),
            pltpu.VMEM((tok_count, 2 * kw), bf16),
            dma((2 * own,)), dma((2 * own,)), dma((3,)), dma((1,)),
            dma((2, steps, 2)), dma((2, steps, 2)), dma((2, steps, 2)), dma((3, steps, 2)),
            dma((2, steps)), dma((2, steps)), dma((2, steps)), dma((2, steps)),
            dma((2, steps)), dma((2, steps)), dma((2, steps)), dma((2, steps)),
            dma((3,)), dma((3,)), dma((3,)), dma((3,)), dma((3,)), dma((3,)), dma((2,)), dma((2,)), dma((2,)), dma((2,)),
        ],
        compiler_params=pltpu.CompilerParams(
            collective_id=0, has_side_effects=True, vmem_limit_bytes=67043328),
    )(tokens[0].T, routes[0].T, route_weights[0].T, moe_gain, attn_gain, head_sink_logits,
      gate_up, down_proj, qkv_proj, out_proj.T)
    return out.T[None]


def solution(mesh):
    in_specs = (
        P("pipe", ("groups", "seq"), None),
        P("pipe", ("groups", "seq"), None),
        P("pipe", ("groups", "seq"), None),
        P(),
        P("seq", None, None),
        P("seq", None, None),
        P(),
        P("seq", None),
        P(),
        P("seq", None),
    )
    out_specs = P("pipe", ("groups", "seq"), None)
    seq_count, pipe_count, group_count = mesh.shape["seq"], mesh.shape["pipe"], mesh.shape["groups"]
    whole = (
        pipe_count == 2
        and group_count == 2
        and seq_count % 2 == 0
        and 2 * E // seq_count == 4
        and seq_count == 8
        and QUERY_HEADS % (2 * seq_count) == 0
    )
    return jax.shard_map(
        whole_layer if whole else body, mesh=mesh, in_specs=in_specs, out_specs=out_specs, check_vma=False
    )
```

```python
import functools

import jax
import jax.numpy as jnp
from jax import lax
from jax.experimental import pallas as pl
from jax.experimental.pallas import tpu as pltpu
from jax.sharding import PartitionSpec as P

MESH = pl.DeviceIdType.MESH
E = 16
TOP = 4
QUERY_HEADS = 32
KEY_VALUE_HEADS = 4
HEAD_SIZE = 64
WINDOW_SPAN = 128
HALF = 720
CAP = 48


eps = 1e-05


def from_partner(value, axis, distance):
    return lax.ppermute(value, axis, [(i, i ^ 1 << distance) for i in range(lax.axis_size(axis))])


def shifted(value, axis, steps):
    count = lax.axis_size(axis)
    pairs = [(source, (source + steps) % count) for source in range(count)]
    return lax.ppermute(value, axis, pairs)


def passed_along(value, axis, steps):
    count = lax.axis_size(axis)
    first, last = (max(0, -steps), min(count, count - steps))
    return lax.ppermute(value, axis, [(source, source + steps) for source in range(first, last)])


def rms_scale(value_matrix, gain):
    widened = value_matrix.astype(jnp.float32)
    mean_square = jnp.mean(widened * widened, axis=-1, keepdims=True)
    return (widened * lax.rsqrt(mean_square + eps) * gain).astype(jnp.bfloat16)


def slot_positions(route_rows):
    flat = route_rows.reshape(-1)
    onehot = (flat[:, None] == jnp.arange(E, dtype=jnp.int32)[None, :]).astype(jnp.int32)
    earlier = jnp.cumsum(onehot, axis=0) - onehot
    return flat * CAP + jnp.sum(earlier * onehot, axis=1)


def expert_layer(local, route_rows, route_scale, moe_gain, gate_up, down_proj):
    tok_count, width = local.shape
    seq_count = lax.axis_size("seq")
    per_device = gate_up.shape[0]
    normed = rms_scale(local, moe_gain)
    positions = slot_positions(route_rows)
    select = (positions[None, :] == jnp.arange(E * CAP, dtype=jnp.int32)[:, None]).astype(
        jnp.bfloat16
    )
    repeated = jnp.repeat(normed, TOP, axis=0)
    table = jnp.dot(select, repeated, preferred_element_type=jnp.float32).astype(jnp.bfloat16)
    by_expert = table.reshape(E, CAP, width)
    first = lax.axis_index("seq") % 2 == 0
    outgoing = jnp.repeat(by_expert, 2, axis=0).reshape(seq_count, per_device, CAP, width)
    received = lax.all_to_all(outgoing, "seq", split_axis=0, concat_axis=0, tiled=True)
    projected = jnp.einsum("spcd,pdh->spch", received, gate_up, preferred_element_type=jnp.float32)
    gate_part = projected[..., :HALF]
    up_part = projected[..., HALF:]
    hidden = (gate_part * jax.nn.sigmoid(1.702 * gate_part) * (up_part + 1.0)).astype(jnp.bfloat16)
    partial_value = jnp.einsum(
        "spch,phd->spcd", hidden, down_proj, preferred_element_type=jnp.float32
    )
    if per_device >= 2:
        finished = (
            partial_value.reshape(seq_count, per_device // 2, 2, CAP, width)
            .sum(axis=2)
            .astype(jnp.bfloat16)
        )
    else:
        lower_rows = partial_value[:, :, : CAP // 2]
        upper_rows = partial_value[:, :, CAP // 2 :]
        kept = jnp.where(first, lower_rows, upper_rows)
        given = jnp.where(first, upper_rows, lower_rows)
        partner_part = from_partner(given.astype(jnp.bfloat16), "seq", 0).astype(given.dtype)
        finished = (kept + partner_part).astype(jnp.bfloat16)
    summed = lax.all_to_all(finished, "seq", split_axis=0, concat_axis=0, tiled=True).reshape(
        E * CAP, width
    )
    picked = lax.dot_general(
        select, summed, (((0,), (0,)), ((), ())), preferred_element_type=jnp.float32
    )
    weighted = jnp.sum(picked.reshape(tok_count, TOP, width) * route_scale[:, :, None], axis=1)
    return (local.astype(jnp.float32) + weighted).astype(jnp.bfloat16)


def attend(query_matrix, keys_extended, values_extended, head_sink_logits, halo_valid):
    tok_count = query_matrix.shape[0]
    query_groups = QUERY_HEADS // KEY_VALUE_HEADS
    attention_block = min(tok_count, 512)
    scale = float(HEAD_SIZE) ** (-0.5)
    sink_mass_total = jnp.exp(head_sink_logits).reshape(KEY_VALUE_HEADS, query_groups, 1, 1)
    block_queries = query_matrix.reshape(attention_block, KEY_VALUE_HEADS, query_groups, HEAD_SIZE)
    block_keys = keys_extended.reshape(attention_block + WINDOW_SPAN, KEY_VALUE_HEADS, HEAD_SIZE)
    block_values = values_extended.reshape(
        attention_block + WINDOW_SPAN, KEY_VALUE_HEADS, HEAD_SIZE
    )
    scores = (
        jnp.einsum("qhgd,khd->hgqk", block_queries, block_keys, preferred_element_type=jnp.float32)
        * scale
    )
    query_pos = jnp.arange(attention_block, dtype=jnp.int32)[:, None] + WINDOW_SPAN
    key_pos = jnp.arange(attention_block + WINDOW_SPAN, dtype=jnp.int32)[None, :]
    distance = query_pos - key_pos
    allowed = (
        (distance >= 0) & (distance < WINDOW_SPAN) & ((key_pos + 0 >= WINDOW_SPAN) | halo_valid)
    )
    weights = jnp.where(allowed, jnp.exp(scores), 0.0)
    probs = (weights / (jnp.sum(weights, axis=-1, keepdims=True) + sink_mass_total)).astype(
        jnp.bfloat16
    )
    mixed = jnp.einsum("hgqk,khd->qhgd", probs, block_values, preferred_element_type=jnp.float32)
    outputs = mixed.reshape(attention_block, QUERY_HEADS * HEAD_SIZE).astype(jnp.bfloat16)
    return outputs


def body(
    tokens,
    routes,
    route_weights,
    moe_gain,
    gate_up,
    down_proj,
    attn_gain,
    qkv_proj,
    head_sink_logits,
    out_proj,
):
    hidden = expert_layer(tokens[0], routes[0], route_weights[0], moe_gain, gate_up, down_proj)
    tok_count, width = hidden.shape
    normed = rms_scale(hidden, attn_gain)
    seq_index = lax.axis_index("seq")
    pipe_index = lax.axis_index("pipe")
    halo_valid = (seq_index > 0) | (pipe_index > 0)
    query_width = QUERY_HEADS * HEAD_SIZE
    width_of_pair = KEY_VALUE_HEADS * HEAD_SIZE
    columns = normed
    packed_heads = jnp.dot(
        columns,
        lax.all_gather(qkv_proj, "seq", axis=0, tiled=True),
        preferred_element_type=jnp.float32,
    ).astype(jnp.bfloat16)
    from_left = shifted(packed_heads[tok_count - WINDOW_SPAN :, query_width:], "seq", 1)
    from_section = passed_along(from_left, "pipe", 1)
    halo_pairs = jnp.where(seq_index == 0, from_section, from_left)
    query_matrix = packed_heads[:, :query_width]
    pairs_ext = jnp.concatenate([halo_pairs, packed_heads[:, query_width:]], axis=0)
    keys_extended = pairs_ext[:, :width_of_pair]
    values_extended = pairs_ext[:, width_of_pair:]
    attended = attend(query_matrix, keys_extended, values_extended, head_sink_logits, halo_valid)
    columns = attended
    projected = jnp.dot(
        columns,
        lax.all_gather(out_proj, "seq", axis=0, tiled=True),
        preferred_element_type=jnp.float32,
    )
    return (hidden.astype(jnp.float32) + projected).astype(jnp.bfloat16)[None]


def ring_place(index, count, folded):
    if not folded:
        return index
    line, side = index // 2, index % 2
    return line + side * (count - 1 - 2 * line)

def ring_index(place, count, folded):
    if not folded:
        return place
    side = place // (count // 2)
    line = place + side * (count - 1 - 2 * place)
    return 2 * line + side


def copy_to(src, dst, send, recv, **device):
    return pltpu.make_async_remote_copy(src_ref=src, dst_ref=dst, send_sem=send, recv_sem=recv,
        device_id=device, device_id_type=MESH)


def dot(a, b, dims=((1,), (0,))):
    return lax.dot_general(a, b, (dims, ((), ())), preferred_element_type=jnp.float32)


def layer_kernel(
    tok_t_ref, routes_ref, weights_ref, gain_ref, attn_gain_ref, sink_ref,
    gate_up_ref, down_ref, qkv_ref, out_t_ref,
    out_ref,
    blocks, picked, combine, gu, dn, proj, act, done, parts, held, wq, wo,
    both, kv, halo, queries, mixed, given, back, hid, hid_t, passed,
    gu_sem, dn_sem, wq_sem, wo_sem, ag_s, ag_r, rs_s, rs_r, q_s, q_r, qx_s, qx_r,
    o_s, o_r, ox_s, ox_r, far_s, far_r, far_xs, far_xr, side_s, side_r, feed_s, feed_r, fx_s, fx_r, pair_s, pair_r, halo_s, halo_r,
):
    count = lax.axis_size("seq")
    steps = count // 2
    me = lax.axis_index("seq")
    core = lax.axis_index("pipe")
    group = lax.axis_index("groups")
    width, tok_count = tok_t_ref.shape
    own = picked.shape[0]
    slots = own * CAP
    place = ring_place(me, count, True)
    at = lambda offset: ring_index(lax.rem(place + offset + count, count), count, True)
    spot = lambda p: ring_index(lax.rem(p + count, count), count, True)
    peers = (at(1), at(-1))
    column = lax.rem(place, steps)
    inner = (column > 0) & (column < steps - 1)
    corner = jnp.logical_not(inner)
    low = column < steps // 2
    toward = jnp.where(low, 1, -1)
    outward = (jnp.logical_not(low), low)
    inner_out = [inner & outward[way] for way in (0, 1)]
    inner_in = [inner & jnp.logical_not(outward[way]) for way in (0, 1)]
    corner_fresh = [corner & outward[way] for way in (0, 1)]
    beside_place = count - 1 - place
    beside = spot(beside_place)
    following, preceding = lax.rem(me + 1, count), lax.rem(me + count - 1, count)
    other_core, other_group = 1 - core, 1 - group
    sends = []

    def launch(copy):
        copy.start()
        sends.append((None, copy))
        return copy

    barrier = pltpu.get_barrier_semaphore()
    for device in ({"seq": peers[0]}, {"seq": peers[1]}, {"seq": following}, {"seq": preceding},
                   {"pipe": other_core}, {"groups": other_group}, {"seq": beside}):
        pl.semaphore_signal(barrier, inc=1, device_id=device, device_id_type=MESH)
    qw, kw = queries.shape[2], kv.shape[2] // 2
    all_q = QUERY_HEADS * HEAD_SIZE
    all_k = KEY_VALUE_HEADS * HEAD_SIZE
    wo_slot = lax.rem(me, steps)
    holds = lambda origin: lax.div(origin, steps) == core
    wo_copy = pltpu.make_async_copy(out_t_ref, wo.at[wo_slot], wo_sem.at[0])

    @pl.when(holds(me))
    def _():
        wo_copy.start()

    wq_copies = []
    for i, (source, goal, size) in enumerate((
        (all_q + core * kw, 0, kw), (all_q + all_k + core * kw, kw, kw), (core * qw, 2 * kw, qw))):
        wq_copies.append(pltpu.make_async_copy(
            qkv_ref.at[:, pl.ds(pl.multiple_of(source, 128), size)],
            wq.at[me, :, pl.ds(goal, size)], wq_sem.at[i]))
    for copy in wq_copies:
        copy.start()
    gu_copies = [pltpu.make_async_copy(gate_up_ref.at[j], gu.at[j], gu_sem.at[j]) for j in range(2 * own)]
    dn_copies = [pltpu.make_async_copy(down_ref.at[j], dn.at[j], dn_sem.at[j]) for j in range(2 * own)]
    for copy in gu_copies + dn_copies:
        copy.start()

    tall = tok_t_ref[...].astype(jnp.float32)
    scale = lax.rsqrt(jnp.sum(tall * tall, axis=0, keepdims=True) / width + eps)
    for i in range(0, width, 128):
        size = min(128, width - i)
        gain = jnp.broadcast_to(gain_ref[pl.ds(i, size)].reshape(1, size), (tok_count, size)).T
        blocks[me, i : i + size, :] = (
            tok_t_ref[i : i + size, :].astype(jnp.float32) * scale * gain
        ).astype(jnp.bfloat16)
    expert_row = lax.broadcasted_iota(jnp.int32, (E, tok_count), 0)
    dense = jnp.zeros((E, tok_count), jnp.float32)
    for j in range(TOP):
        dense = dense + jnp.where(expert_row == routes_ref[j : j + 1, :], weights_ref[j : j + 1, :], 0.0)
    blocks[me, width : width + E, :] = dense.astype(jnp.bfloat16)

    pl.semaphore_wait(barrier, 7)

    rows_all = blocks.shape[1]
    cut = (rows_all // 2 + 15) // 16 * 16
    pieces = (pl.ds(0, cut), pl.ds(cut, rows_all - cut))
    ag = {}

    def ag_send(way, step, piece):
        origin = at(-step if way == 0 else step)
        ref = blocks.at[origin, pieces[piece]]
        ag[way, step, piece] = launch(copy_to(ref, ref, ag_s.at[way, step, piece], ag_r.at[way, step, piece], seq=peers[way]))

    qcols = wq.shape[2] // 2
    q = {}
    qx = {}

    qpart = pl.ds(pl.multiple_of(group * qcols, 128), qcols)
    near = steps // 2

    def q_send(way, step):
        ref = wq.at[at(-step if way == 0 else step), :, qpart]
        q[way, step] = launch(copy_to(ref, ref, q_s.at[way, step], q_r.at[way, step], seq=peers[way]))

    def q_cross(way, step):
        q[way, step].wait_recv()
        ref = wq.at[at(-step - 1 if way == 0 else step + 1), :, qpart]
        qx[way, step] = launch(copy_to(ref, ref, qx_s.at[way, step], qx_r.at[way, step], groups=other_group))

    def q_begin():
        for way in (0, 1):
            q_send(way, 0)

    def q_step(step):
        for way in (0, 1):
            q_cross(way, step - 1)
            if step < steps - 1:
                q_send(way, step)

    far_sends = []

    def far_out(origin, kind, peer):
        ref = wq.at[origin, :, qpart]
        copy = copy_to(ref, ref, far_s.at[kind], far_r.at[0], seq=peer)

        @pl.when(inner)
        def _():
            copy.start()
        far_sends.append((inner, copy))

    def far_side():
        far_out(at(toward), 0, beside)

    def far_feed():
        far_out(at(3 * toward), 1, spot(place - toward))

    def far_copy():
        ref = wq.at[at(steps), :, qpart]
        return (copy_to(ref, ref, far_s.at[0], far_r.at[0], seq=beside),
            copy_to(ref, ref, far_xs.at[0], far_xr.at[0], groups=other_group))

    def far_cross(role):
        landed, crossing = far_copy()

        @pl.when(role)
        def _():
            landed.wait_recv()
            crossing.start()

    orows = wo.shape[1] // 2
    ocut = (orows // 2 + 15) // 16 * 16
    o_sends = []

    def o_part(way, step):
        base = pl.multiple_of(group * orows, 16)
        if step < steps - 1:
            return pl.ds(base, orows)
        return pl.ds(base, ocut) if way == 0 else pl.ds(pl.multiple_of(base + ocut, 16), orows - ocut)

    def o_copy(way, step):
        origin = at(-step if way == 0 else step)
        ref = wo.at[lax.rem(origin, steps), o_part(way, step)]
        return holds(origin), copy_to(ref, ref, o_s.at[way, step], o_r.at[way, step], seq=peers[way])

    def o_landed(way, step):
        origin = at(-step - 1 if way == 0 else step + 1)
        ref = wo.at[lax.rem(origin, steps), o_part(way, step)]
        return (holds(origin), copy_to(ref, ref, o_s.at[way, step], o_r.at[way, step], seq=peers[way]),
                copy_to(ref, ref, ox_s.at[way, step], ox_r.at[way, step], groups=other_group))

    def o_begin():
        @pl.when(holds(me))
        def _():
            wo_copy.wait()
        for way in (0, 1):
            cond, copy = o_copy(way, 0)

            @pl.when(cond)
            def _():
                copy.start()
            o_sends.append((cond, copy))

    def o_step(step):
        for way in (0, 1):
            cond, arrived, crossing = o_landed(way, step - 1)

            @pl.when(cond)
            def _():
                arrived.wait_recv()
                crossing.start()
            o_sends.append((cond, crossing))
            if step < near:
                onward, copy = o_copy(way, step)

                @pl.when(onward)
                def _():
                    copy.start()
                o_sends.append((onward, copy))

    def o_crossed(step):
        for way in (0, 1):
            cond, _, crossing = o_landed(way, step)

            @pl.when(cond)
            def _():
                crossing.wait_recv()

    def side_copy(origin, hop):
        ref = wo.at[lax.rem(origin, steps)]
        return inner & holds(origin), copy_to(ref, ref, side_s.at[hop], side_r.at[hop], seq=beside)

    def side_send(hop):
        cond, copy = side_copy(at(toward * hop), hop)

        @pl.when(cond)
        def _():
            copy.start()
        o_sends.append((cond, copy))

    def side_wait(hop):
        cond, copy = side_copy(spot(beside_place - toward * hop), hop)

        @pl.when(cond)
        def _():
            copy.wait_recv()

    feed_part = pl.ds(pl.multiple_of(group * orows, 16), orows)

    def feed_copy(origin, index):
        ref = wo.at[lax.rem(origin, steps), feed_part]
        return holds(origin), copy_to(ref, ref, feed_s.at[index], feed_r.at[index], seq=spot(place - toward))

    def feed_send(which):
        origins = (at(2 * toward), spot(beside_place - toward), spot(beside_place - 2 * toward))
        for index in which:
            origin = origins[index]
            cond, copy = feed_copy(origin, index)

            @pl.when(inner & cond)
            def _():
                copy.start()
            o_sends.append((inner & cond, copy))

    feed_crossings = []

    def feed_cross(index):
        origin = (spot(place + 3 * toward), spot(beside_place - 2 * toward), spot(beside_place - 3 * toward))[index]
        held_here, landed = feed_copy(origin, index)
        cond = corner & held_here
        ref = wo.at[lax.rem(origin, steps), feed_part]
        crossing = copy_to(ref, ref, fx_s.at[index], fx_r.at[index], groups=other_group)

        @pl.when(cond)
        def _():
            landed.wait_recv()
            crossing.start()
        o_sends.append((cond, crossing))
        feed_crossings.append((cond, crossing))

    lane_tok = lax.broadcasted_iota(jnp.int32, (tok_count, tok_count), 1)
    row_tok = lax.broadcasted_iota(jnp.int32, (tok_count, tok_count), 0)
    before = jnp.where(row_tok < lane_tok, 1.0, 0.0).astype(jnp.bfloat16)
    slot_row = lax.broadcasted_iota(jnp.int32, (tok_count, tok_count), 0).astype(jnp.float32)

    def process(n):
        table = blocks[n, width : width + E, :].astype(jnp.float32)
        present = table > 0.0
        earlier = dot(jnp.where(present, 1.0, 0.0).astype(jnp.bfloat16), before)
        slot = jnp.where(present, earlier, -1.0)
        comb = jnp.zeros((tok_count, tok_count), jnp.float32)
        for e in range(own):
            mine = expert_row == me * own + e
            slot_e = jnp.sum(jnp.where(mine, slot, 0.0), axis=0, keepdims=True)
            scale_e = jnp.sum(jnp.where(mine, table, 0.0), axis=0, keepdims=True)
            hit = (slot_row == slot_e + float(e * CAP)) & (slot_e >= 0.0)
            comb = jnp.where(hit, scale_e, comb)
        combine[n] = comb.T.astype(jnp.bfloat16)
        select = jnp.where(comb > 0.0, 1.0, 0.0).astype(jnp.bfloat16)[:slots]
        rows = dot(select, blocks[n, :width, :], ((1,), (1,))).astype(jnp.bfloat16)
        for e in range(own):
            picked[e, n] = rows[e * CAP : (e + 1) * CAP]

    for piece in (0, 1):
        for way in (0, 1):
            ag_send(way, 0, piece ^ way)
    o_begin()
    side_send(0)
    for copy in wq_copies:
        copy.wait()
    process(me)
    for i in range(0, width, 128):
        size = min(128, width - i)
        hid[:, i : i + size] = tok_t_ref[i : i + size, :].astype(jnp.float32).T
    for step in range(1, steps):
        for piece in (0, 1):
            for way in (0, 1):
                ag[way, step - 1, piece ^ way].wait_recv()
                if step < steps - 1 or piece == 0:
                    ag_send(way, step, piece ^ way)
        if step <= near:
            o_step(step)
        else:
            q_begin()
            o_crossed(step - near - 1)
            side_send(1)
        process(at(-step))
        process(at(step))
    ag[0, steps - 1, 0].wait_recv()
    ag[1, steps - 1, 1].wait_recv()
    process(at(steps))

    o_crossed(1)
    side_send(2)
    pos = {0: 1, 1: 2, 2: 3, 3: 4}
    half = dn.shape[1]
    chunk = CAP
    for e in range(own):
        for j in (2 * e, 2 * e + 1):
            gu_copies[j].wait()
            x = picked[e].reshape(count * CAP, width)
            proj[...] = dot(x, gu[j])

            @pl.loop(0, count)
            def _(i):
                r = pl.ds(pl.multiple_of(i * chunk, 16), chunk)
                gate = proj[r, :half]
                up = proj[r, half:]
                act[j % 2, r, :] = (gate * jax.nn.sigmoid(1.702 * gate) * (up + 1.0)).astype(jnp.bfloat16)

            if j in (1, 2):
                q_step((1, 2).index(j) + 1)
                if j == 1:
                    far_side()
        dn_copies[2 * e].wait()
        dn_copies[2 * e + 1].wait()
        result = dot(act[0], dn[2 * e]) + dot(act[1], dn[2 * e + 1])
        done[:, e * CAP : (e + 1) * CAP, :] = result.astype(jnp.bfloat16).reshape(count, CAP, width)

    q_step(3)
    far_cross(inner)
    far_feed()
    hrows = tok_count // 2
    tail = width % 128
    full = width - tail
    folds = 128 // tail
    trows = hrows // folds
    base = hrows * (full // 128)

    def part(n):
        value = dot(combine[n][:, :slots], done[n])
        for c in (0, 1):
            rows = value[c * hrows : (c + 1) * hrows]
            for i in range(0, full, 128):
                parts[n, c, i // 128 * hrows : (i // 128 + 1) * hrows, :] = rows[:, i : i + 128].astype(jnp.bfloat16)
            parts[n, c, base : base + trows, :] = jnp.concatenate(
                [rows[k * trows : (k + 1) * trows, full:] for k in range(folds)], axis=1
            ).astype(jnp.bfloat16)

    rs = {}

    def rs_add(goal, way, step, piece):
        here = held.at[way, step, piece]
        copy_to(here, here, rs_s.at[0, step, piece], rs_r.at[way, step, piece], seq=peers[0]).wait_recv()
        parts[goal, piece] = (
            parts[goal, piece].astype(jnp.float32) + held[way, step, piece].astype(jnp.float32)
        ).astype(jnp.bfloat16)

    def rs_send(way, step, piece):
        goal = at((steps - step) * (1 if way == 0 else -1))
        if (way, step - 1, piece) in rs:
            @pl.when(jnp.logical_not(corner_fresh[way]))
            def _():
                rs_add(goal, way, step - 1, piece)
        if step == steps - 1:
            @pl.when(inner_out[way])
            def _():
                rs_add(goal, 2, 2, piece)
            if piece == way:
                @pl.when(inner_in[way])
                def _():
                    rs_add(goal, 2, 0, piece)
        landing, peer = way, peers[way]
        if step < steps - 1:
            landing = jnp.where(inner_out[way], 2, way)
            peer = jnp.where(inner_out[way], beside, peer)
        rs[way, step, piece] = launch(copy_to(parts.at[goal, piece], held.at[landing, step, piece],
            rs_s.at[way, step, piece], rs_r.at[landing, step, piece], seq=peer))

    part(at(steps))
    rs_send(0, 0, 0)
    rs_send(1, 0, 1)
    for way in (0, 1):
        part(at((steps - 1) * (1 if way == 0 else -1)))
        rs_send(way, 1, 1 - way)
    for offset in range(steps - 2, 0, -1):
        part(at(offset))
        part(at(-offset))
    part(me)
    for hop in range(3):
        side_wait(hop)
    feed_send((0, 1, 2))
    rs_send(0, 1, 0)
    rs_send(1, 1, 1)
    for step in range(2, steps):
        for piece in (0, 1):
            for way in (0, 1):
                rs_send(way, step, 1 ^ piece ^ way)
        if step == 2:
            far_cross(corner)
        feed_cross(step - 2)
    feed_cross(2)
    for c in (0, 1):
        @pl.when(inner)
        def _():
            rs_add(me, 2, 1, c)
        for way in (0, 1):
            copy_to(held.at[way, steps - 1, c], held.at[way, steps - 1, c], rs_s.at[way, steps - 1, c],
                rs_r.at[way, steps - 1, c], seq=peers[way]).wait_recv()
        rows = slice(c * hrows, (c + 1) * hrows)
        value = (parts[me, c].astype(jnp.float32) + held[0, steps - 1, c].astype(jnp.float32)
            + held[1, steps - 1, c].astype(jnp.float32))
        for i in range(0, full, 128):
            term = value[i // 128 * hrows : (i // 128 + 1) * hrows]
            hid[rows, i : i + 128] = (hid[rows, i : i + 128] + term).astype(jnp.bfloat16).astype(jnp.float32)
        term = jnp.concatenate(
            [value[base : base + trows, k * tail : (k + 1) * tail] for k in range(folds)], axis=0)
        hid[rows, full:] = (hid[rows, full:] + term).astype(jnp.bfloat16).astype(jnp.float32)
    hidden = hid[...]
    scale = lax.rsqrt(jnp.sum(hidden * hidden, axis=1, keepdims=True) / width + eps)
    normed = hidden * scale * attn_gain_ref[...].reshape(1, width)
    shard = wq.shape[1]
    for i in range(count):
        both[core, i] = normed[:, i * shard : (i + 1) * shard].astype(jnp.bfloat16)
    pair = launch(copy_to(both.at[core], both.at[core], pair_s.at[0], pair_r.at[0], pipe=other_core))

    for key in qx:
        qx[key].wait_recv()
    far_copy()[1].wait_recv()

    def project(m, columns):
        total = None
        for i in range(count):
            x = both[:, i].reshape(2 * tok_count, shard) if m is None else both[m, i]
            term = dot(x, wq[i, :, columns])
            total = term if total is None else total + term
        return total

    kv[core] = project(core, pl.ds(0, 2 * kw)).astype(jnp.bfloat16)
    along = [launch(copy_to(kv.at[core], halo.at[core], halo_s.at[0], halo_r.at[0], seq=following))]
    for i in range(0, width, 128):
        size = min(128, width - i)
        hid_t[i : i + size, :] = hid[:, i : i + size].T
    pair.wait_recv()
    kv[other_core] = project(other_core, pl.ds(0, 2 * kw)).astype(jnp.bfloat16)
    along.append(launch(copy_to(kv.at[other_core], halo.at[other_core], halo_s.at[1], halo_r.at[1], seq=following)))
    packed = project(None, pl.ds(2 * kw, qw)).astype(jnp.bfloat16)
    queries[...] = (packed * (float(HEAD_SIZE) ** -0.5)).reshape(2, tok_count, qw)

    lane = lax.broadcasted_iota(jnp.int32, (tok_count, 2 * tok_count), 1)
    row = lax.broadcasted_iota(jnp.int32, (tok_count, 2 * tok_count), 0)
    left = lane < tok_count
    past = jnp.where(left, lane, lane - tok_count) > row
    low = lax.broadcasted_iota(jnp.int32, (tok_count, 2 * HEAD_SIZE), 1) < HEAD_SIZE

    def stacked(tile, head):
        tile = tile.astype(jnp.float32)
        kept = jnp.where(low if head == 0 else ~low, tile, 0.0)
        turned = pltpu.roll(kept, HEAD_SIZE, 1)
        pair_of = (kept, turned) if head == 0 else (turned, kept)
        return jnp.concatenate(pair_of, axis=0).astype(jnp.bfloat16)

    tiles = qw // 128
    per_head = tiles // 2

    def attention(m, known):
        past_kv = passed[...]
        dropped = past & jnp.logical_not(known)
        for head in range(2):
            k_own = stacked(kv[m, :, :kw], head)
            v_own = stacked(kv[m, :, kw:], head)
            k_past = stacked(past_kv[:, :kw], head)
            v_past = stacked(past_kv[:, kw:], head)
            for t in range(head * per_head, (head + 1) * per_head):
                first_head = core * 2 * tiles + 2 * t
                sink_a = jnp.exp(jnp.full((1, 1), sink_ref[first_head]))
                sink_b = jnp.exp(jnp.full((1, 1), sink_ref[first_head + 1]))
                x = queries[m, :, t * 128 : (t + 1) * 128]
                score = jnp.where(past, dot(x, k_past, ((1,), (1,))), dot(x, k_own, ((1,), (1,))))
                weight = jnp.where(dropped, 0.0, jnp.exp(score))
                mass_a = jnp.sum(weight[:, :tok_count], axis=1, keepdims=True) + sink_a
                mass_b = jnp.sum(weight[:, tok_count:], axis=1, keepdims=True) + sink_b
                probs = weight * jnp.where(left, 1.0 / mass_a, 1.0 / mass_b)
                mixed[m, :, t * 128 : (t + 1) * 128] = (
                    dot(jnp.where(past, 0.0, probs).astype(jnp.bfloat16), v_own)
                    + dot(jnp.where(past, probs, 0.0).astype(jnp.bfloat16), v_past)
                ).astype(jnp.bfloat16)

    share = wo.shape[2]
    last = copy_to(given, back, pair_s.at[1], pair_r.at[1], pipe=other_core)

    def output(m):
        total = None
        for i in range(steps):
            term = dot(wo[i], mixed[m, :, i * share : (i + 1) * share], ((1,), (1,)))
            total = term if total is None else total + term

        @pl.when(m == other_core)
        def _():
            given[...] = total.astype(jnp.bfloat16)
            last.start()

        @pl.when(m == core)
        def _():
            hid_t[...] = hid_t[...] + total

    early = jnp.where(me == 0, 0, other_core)
    late = 1 - early

    @pl.when(me > 0)
    def _():
        for copy in along:
            copy.wait_recv()
        passed[...] = halo[other_core]

    @pl.when(me == 0)
    def _():
        passed[...] = jnp.zeros_like(passed)
    attention(early, me > 0)
    for cond, crossing in feed_crossings:
        @pl.when(cond)
        def _():
            crossing.wait_recv()
    output(early)

    @pl.when(me == 0)
    def _():
        for copy in along:
            copy.wait_recv()
    passed[...] = halo[jnp.where(me == 0, 0, core)]
    attention(late, me >= 0)
    output(late)
    last.wait_recv()
    out_ref[...] = (hid_t[...] + back[...].astype(jnp.float32)).astype(jnp.bfloat16)
    last.wait_send()
    for _, copy in sends:
        copy.wait_send()
    far_copy()[1].wait_send()
    for cond, copy in o_sends + far_sends:
        @pl.when(cond)
        def _():
            copy.wait_send()


def whole_layer(
    tokens, routes, route_weights, moe_gain, gate_up, down_proj, attn_gain, qkv_proj,
    head_sink_logits, out_proj,
):
    count = lax.axis_size("seq")
    steps = count // 2
    tok_count, width = tokens.shape[1:]
    own = gate_up.shape[0] // 2
    half = down_proj.shape[1]
    heads = QUERY_HEADS // 2
    qw = heads * HEAD_SIZE
    kw = KEY_VALUE_HEADS * HEAD_SIZE // 2
    chunk = tok_count // 2 * width // 128
    dma = pltpu.SemaphoreType.DMA
    bf16 = jnp.bfloat16
    vm = pl.BlockSpec(memory_space=pltpu.VMEM)
    hbm = pl.BlockSpec(memory_space=pl.ANY)
    out = pl.pallas_call(
        layer_kernel,
        out_shape=jax.ShapeDtypeStruct((width, tok_count), bf16),
        in_specs=[vm] * 5 + [pl.BlockSpec(memory_space=pltpu.SMEM)] + [hbm] * 4,
        out_specs=vm,
        scratch_shapes=[
            pltpu.VMEM((count, width + E, tok_count), bf16),
            pltpu.VMEM((own, count, CAP, width), bf16),
            pltpu.VMEM((count, tok_count, tok_count), bf16),
            pltpu.VMEM(gate_up.shape, bf16),
            pltpu.VMEM(down_proj.shape, bf16),
            pltpu.VMEM((count * CAP, 2 * half), jnp.float32),
            pltpu.VMEM((2, count * CAP, half), bf16),
            pltpu.VMEM((count, own * CAP, width), bf16),
            pltpu.VMEM((count, 2, chunk, 128), bf16),
            pltpu.VMEM((3, steps, 2, chunk, 128), bf16),
            pltpu.VMEM((count, qkv_proj.shape[0], 2 * kw + qw), bf16),
            pltpu.VMEM((steps, width, out_proj.shape[0]), bf16),
            pltpu.VMEM((2, count, tok_count, qkv_proj.shape[0]), bf16),
            pltpu.VMEM((2, tok_count, 2 * kw), bf16),
            pltpu.VMEM((2, tok_count, 2 * kw), bf16),
            pltpu.VMEM((2, tok_count, qw), bf16),
            pltpu.VMEM((2, tok_count, qw), bf16),
            pltpu.VMEM((width, tok_count), bf16),
            pltpu.VMEM((width, tok_count), bf16),
            pltpu.VMEM((tok_count, width), jnp.float32),
            pltpu.VMEM((width, tok_count), jnp.float32),
            pltpu.VMEM((tok_count, 2 * kw), bf16),
            dma((2 * own,)), dma((2 * own,)), dma((3,)), dma((1,)),
            dma((2, steps, 2)), dma((2, steps, 2)), dma((2, steps, 2)), dma((3, steps, 2)),
            dma((2, steps)), dma((2, steps)), dma((2, steps)), dma((2, steps)),
            dma((2, steps)), dma((2, steps)), dma((2, steps)), dma((2, steps)),
            dma((2,)), dma((1,)), dma((1,)), dma((1,)),
            dma((3,)), dma((3,)), dma((3,)), dma((3,)), dma((3,)), dma((3,)), dma((2,)), dma((2,)), dma((2,)), dma((2,)),
        ],
        compiler_params=pltpu.CompilerParams(
            collective_id=0, has_side_effects=True, vmem_limit_bytes=67043328),
    )(tokens[0].T, routes[0].T, route_weights[0].T, moe_gain, attn_gain, head_sink_logits,
      gate_up, down_proj, qkv_proj, out_proj.T)
    return out.T[None]


def solution(mesh):
    in_specs = (
        P("pipe", ("groups", "seq"), None),
        P("pipe", ("groups", "seq"), None),
        P("pipe", ("groups", "seq"), None),
        P(),
        P("seq", None, None),
        P("seq", None, None),
        P(),
        P("seq", None),
        P(),
        P("seq", None),
    )
    out_specs = P("pipe", ("groups", "seq"), None)
    seq_count, pipe_count, group_count = mesh.shape["seq"], mesh.shape["pipe"], mesh.shape["groups"]
    whole = (
        pipe_count == 2
        and group_count == 2
        and seq_count % 2 == 0
        and 2 * E // seq_count == 4
        and seq_count == 8
        and QUERY_HEADS % (2 * seq_count) == 0
    )
    return jax.shard_map(
        whole_layer if whole else body, mesh=mesh, in_specs=in_specs, out_specs=out_specs, check_vma=False
    )
```

```python
import functools

import jax
import jax.numpy as jnp
from jax import lax
from jax.experimental import pallas as pl
from jax.experimental.pallas import tpu as pltpu
from jax.sharding import PartitionSpec as P

MESH = pl.DeviceIdType.MESH
E = 16
TOP = 4
QUERY_HEADS = 32
KEY_VALUE_HEADS = 4
HEAD_SIZE = 64
WINDOW_SPAN = 128
HALF = 720
CAP = 48


eps = 1e-05


def from_partner(value, axis, distance):
    return lax.ppermute(value, axis, [(i, i ^ 1 << distance) for i in range(lax.axis_size(axis))])


def shifted(value, axis, steps):
    count = lax.axis_size(axis)
    pairs = [(source, (source + steps) % count) for source in range(count)]
    return lax.ppermute(value, axis, pairs)


def passed_along(value, axis, steps):
    count = lax.axis_size(axis)
    first, last = (max(0, -steps), min(count, count - steps))
    return lax.ppermute(value, axis, [(source, source + steps) for source in range(first, last)])


def rms_scale(value_matrix, gain):
    widened = value_matrix.astype(jnp.float32)
    mean_square = jnp.mean(widened * widened, axis=-1, keepdims=True)
    return (widened * lax.rsqrt(mean_square + eps) * gain).astype(jnp.bfloat16)


def slot_positions(route_rows):
    flat = route_rows.reshape(-1)
    onehot = (flat[:, None] == jnp.arange(E, dtype=jnp.int32)[None, :]).astype(jnp.int32)
    earlier = jnp.cumsum(onehot, axis=0) - onehot
    return flat * CAP + jnp.sum(earlier * onehot, axis=1)


def expert_layer(local, route_rows, route_scale, moe_gain, gate_up, down_proj):
    tok_count, width = local.shape
    seq_count = lax.axis_size("seq")
    per_device = gate_up.shape[0]
    normed = rms_scale(local, moe_gain)
    positions = slot_positions(route_rows)
    select = (positions[None, :] == jnp.arange(E * CAP, dtype=jnp.int32)[:, None]).astype(
        jnp.bfloat16
    )
    repeated = jnp.repeat(normed, TOP, axis=0)
    table = jnp.dot(select, repeated, preferred_element_type=jnp.float32).astype(jnp.bfloat16)
    by_expert = table.reshape(E, CAP, width)
    first = lax.axis_index("seq") % 2 == 0
    outgoing = jnp.repeat(by_expert, 2, axis=0).reshape(seq_count, per_device, CAP, width)
    received = lax.all_to_all(outgoing, "seq", split_axis=0, concat_axis=0, tiled=True)
    projected = jnp.einsum("spcd,pdh->spch", received, gate_up, preferred_element_type=jnp.float32)
    gate_part = projected[..., :HALF]
    up_part = projected[..., HALF:]
    hidden = (gate_part * jax.nn.sigmoid(1.702 * gate_part) * (up_part + 1.0)).astype(jnp.bfloat16)
    partial_value = jnp.einsum(
        "spch,phd->spcd", hidden, down_proj, preferred_element_type=jnp.float32
    )
    if per_device >= 2:
        finished = (
            partial_value.reshape(seq_count, per_device // 2, 2, CAP, width)
            .sum(axis=2)
            .astype(jnp.bfloat16)
        )
    else:
        lower_rows = partial_value[:, :, : CAP // 2]
        upper_rows = partial_value[:, :, CAP // 2 :]
        kept = jnp.where(first, lower_rows, upper_rows)
        given = jnp.where(first, upper_rows, lower_rows)
        partner_part = from_partner(given.astype(jnp.bfloat16), "seq", 0).astype(given.dtype)
        finished = (kept + partner_part).astype(jnp.bfloat16)
    summed = lax.all_to_all(finished, "seq", split_axis=0, concat_axis=0, tiled=True).reshape(
        E * CAP, width
    )
    picked = lax.dot_general(
        select, summed, (((0,), (0,)), ((), ())), preferred_element_type=jnp.float32
    )
    weighted = jnp.sum(picked.reshape(tok_count, TOP, width) * route_scale[:, :, None], axis=1)
    return (local.astype(jnp.float32) + weighted).astype(jnp.bfloat16)


def attend(query_matrix, keys_extended, values_extended, head_sink_logits, halo_valid):
    tok_count = query_matrix.shape[0]
    query_groups = QUERY_HEADS // KEY_VALUE_HEADS
    attention_block = min(tok_count, 512)
    scale = float(HEAD_SIZE) ** (-0.5)
    sink_mass_total = jnp.exp(head_sink_logits).reshape(KEY_VALUE_HEADS, query_groups, 1, 1)
    block_queries = query_matrix.reshape(attention_block, KEY_VALUE_HEADS, query_groups, HEAD_SIZE)
    block_keys = keys_extended.reshape(attention_block + WINDOW_SPAN, KEY_VALUE_HEADS, HEAD_SIZE)
    block_values = values_extended.reshape(
        attention_block + WINDOW_SPAN, KEY_VALUE_HEADS, HEAD_SIZE
    )
    scores = (
        jnp.einsum("qhgd,khd->hgqk", block_queries, block_keys, preferred_element_type=jnp.float32)
        * scale
    )
    query_pos = jnp.arange(attention_block, dtype=jnp.int32)[:, None] + WINDOW_SPAN
    key_pos = jnp.arange(attention_block + WINDOW_SPAN, dtype=jnp.int32)[None, :]
    distance = query_pos - key_pos
    allowed = (
        (distance >= 0) & (distance < WINDOW_SPAN) & ((key_pos + 0 >= WINDOW_SPAN) | halo_valid)
    )
    weights = jnp.where(allowed, jnp.exp(scores), 0.0)
    probs = (weights / (jnp.sum(weights, axis=-1, keepdims=True) + sink_mass_total)).astype(
        jnp.bfloat16
    )
    mixed = jnp.einsum("hgqk,khd->qhgd", probs, block_values, preferred_element_type=jnp.float32)
    outputs = mixed.reshape(attention_block, QUERY_HEADS * HEAD_SIZE).astype(jnp.bfloat16)
    return outputs


def body(
    tokens,
    routes,
    route_weights,
    moe_gain,
    gate_up,
    down_proj,
    attn_gain,
    qkv_proj,
    head_sink_logits,
    out_proj,
):
    hidden = expert_layer(tokens[0], routes[0], route_weights[0], moe_gain, gate_up, down_proj)
    tok_count, width = hidden.shape
    normed = rms_scale(hidden, attn_gain)
    seq_index = lax.axis_index("seq")
    pipe_index = lax.axis_index("pipe")
    halo_valid = (seq_index > 0) | (pipe_index > 0)
    query_width = QUERY_HEADS * HEAD_SIZE
    width_of_pair = KEY_VALUE_HEADS * HEAD_SIZE
    columns = normed
    packed_heads = jnp.dot(
        columns,
        lax.all_gather(qkv_proj, "seq", axis=0, tiled=True),
        preferred_element_type=jnp.float32,
    ).astype(jnp.bfloat16)
    from_left = shifted(packed_heads[tok_count - WINDOW_SPAN :, query_width:], "seq", 1)
    from_section = passed_along(from_left, "pipe", 1)
    halo_pairs = jnp.where(seq_index == 0, from_section, from_left)
    query_matrix = packed_heads[:, :query_width]
    pairs_ext = jnp.concatenate([halo_pairs, packed_heads[:, query_width:]], axis=0)
    keys_extended = pairs_ext[:, :width_of_pair]
    values_extended = pairs_ext[:, width_of_pair:]
    attended = attend(query_matrix, keys_extended, values_extended, head_sink_logits, halo_valid)
    columns = attended
    projected = jnp.dot(
        columns,
        lax.all_gather(out_proj, "seq", axis=0, tiled=True),
        preferred_element_type=jnp.float32,
    )
    return (hidden.astype(jnp.float32) + projected).astype(jnp.bfloat16)[None]


def ring_place(index, count, folded):
    if not folded:
        return index
    line, side = index // 2, index % 2
    return line + side * (count - 1 - 2 * line)

def ring_index(place, count, folded):
    if not folded:
        return place
    side = place // (count // 2)
    line = place + side * (count - 1 - 2 * place)
    return 2 * line + side


def copy_to(src, dst, send, recv, **device):
    return pltpu.make_async_remote_copy(src_ref=src, dst_ref=dst, send_sem=send, recv_sem=recv,
        device_id=device, device_id_type=MESH)


def dot(a, b, dims=((1,), (0,))):
    return lax.dot_general(a, b, (dims, ((), ())), preferred_element_type=jnp.float32)


def layer_kernel(
    tok_t_ref, routes_ref, weights_ref, gain_ref, attn_gain_ref, sink_ref,
    gate_up_ref, down_ref, qkv_ref, out_t_ref,
    out_ref,
    blocks, picked, combine, gu, dn, proj, act, done, parts, held, wq, wo,
    both, kv, halo, queries, mixed, given, back, hid, hid_t, passed,
    gu_sem, dn_sem, wq_sem, wo_sem, ag_s, ag_r, rs_s, rs_r, q_s, q_r, qx_s, qx_r,
    o_s, o_r, ox_s, ox_r, far_s, far_r, far_xs, far_xr, side_s, side_r, feed_s, feed_r, fx_s, fx_r, pair_s, pair_r, halo_s, halo_r,
):
    count = lax.axis_size("seq")
    steps = count // 2
    me = lax.axis_index("seq")
    core = lax.axis_index("pipe")
    group = lax.axis_index("groups")
    width, tok_count = tok_t_ref.shape
    own = picked.shape[0]
    slots = own * CAP
    place = ring_place(me, count, True)
    at = lambda offset: ring_index(lax.rem(place + offset + count, count), count, True)
    spot = lambda p: ring_index(lax.rem(p + count, count), count, True)
    peers = (at(1), at(-1))
    column = lax.rem(place, steps)
    inner = (column > 0) & (column < steps - 1)
    corner = jnp.logical_not(inner)
    low = column < steps // 2
    toward = jnp.where(low, 1, -1)
    outward = (jnp.logical_not(low), low)
    inner_out = [inner & outward[way] for way in (0, 1)]
    inner_in = [inner & jnp.logical_not(outward[way]) for way in (0, 1)]
    corner_fresh = [corner & outward[way] for way in (0, 1)]
    beside_place = count - 1 - place
    beside = spot(beside_place)
    following, preceding = lax.rem(me + 1, count), lax.rem(me + count - 1, count)
    other_core, other_group = 1 - core, 1 - group
    sends = []

    def launch(copy):
        copy.start()
        sends.append((None, copy))
        return copy

    barrier = pltpu.get_barrier_semaphore()
    for device in ({"seq": peers[0]}, {"seq": peers[1]}, {"seq": following}, {"seq": preceding},
                   {"pipe": other_core}, {"groups": other_group}, {"seq": beside}):
        pl.semaphore_signal(barrier, inc=1, device_id=device, device_id_type=MESH)
    qw, kw = queries.shape[2], kv.shape[2] // 2
    all_q = QUERY_HEADS * HEAD_SIZE
    all_k = KEY_VALUE_HEADS * HEAD_SIZE
    wo_slot = lax.rem(me, steps)
    holds = lambda origin: lax.div(origin, steps) == core
    wo_copy = pltpu.make_async_copy(out_t_ref, wo.at[wo_slot], wo_sem.at[0])

    @pl.when(holds(me))
    def _():
        wo_copy.start()

    wq_copies = []
    for i, (source, goal, size) in enumerate((
        (all_q + core * kw, 0, kw), (all_q + all_k + core * kw, kw, kw), (core * qw, 2 * kw, qw))):
        wq_copies.append(pltpu.make_async_copy(
            qkv_ref.at[:, pl.ds(pl.multiple_of(source, 128), size)],
            wq.at[me, :, pl.ds(goal, size)], wq_sem.at[i]))
    for copy in wq_copies:
        copy.start()
    gu_copies = [pltpu.make_async_copy(gate_up_ref.at[j], gu.at[j], gu_sem.at[j]) for j in range(2 * own)]
    dn_copies = [pltpu.make_async_copy(down_ref.at[j], dn.at[j], dn_sem.at[j]) for j in range(2 * own)]

    pl.semaphore_wait(barrier, 7)

    rows_all = blocks.shape[1]
    cut = (rows_all // 2 + 15) // 16 * 16
    pieces = (pl.ds(0, cut), pl.ds(cut, rows_all - cut))
    ag = {}

    def ag_send(way, step, piece):
        origin = at(-step if way == 0 else step)
        ref = blocks.at[origin, pieces[piece]]
        ag[way, step, piece] = launch(copy_to(ref, ref, ag_s.at[way, step, piece], ag_r.at[way, step, piece], seq=peers[way]))

    qcols = wq.shape[2] // 2
    q = {}
    qx = {}

    qpart = pl.ds(pl.multiple_of(group * qcols, 128), qcols)
    near = steps // 2

    def q_send(way, step):
        ref = wq.at[at(-step if way == 0 else step), :, qpart]
        q[way, step] = launch(copy_to(ref, ref, q_s.at[way, step], q_r.at[way, step], seq=peers[way]))

    def q_cross(way, step):
        q[way, step].wait_recv()
        ref = wq.at[at(-step - 1 if way == 0 else step + 1), :, qpart]
        qx[way, step] = launch(copy_to(ref, ref, qx_s.at[way, step], qx_r.at[way, step], groups=other_group))

    def q_begin():
        for way in (0, 1):
            q_send(way, 0)

    def q_step(step):
        for way in (0, 1):
            q_cross(way, step - 1)
            if step < steps - 1:
                q_send(way, step)

    far_sends = []

    def far_out(origin, kind, peer):
        ref = wq.at[origin, :, qpart]
        copy = copy_to(ref, ref, far_s.at[kind], far_r.at[0], seq=peer)

        @pl.when(inner)
        def _():
            copy.start()
        far_sends.append((inner, copy))

    def far_side():
        far_out(at(toward), 0, beside)

    def far_feed():
        far_out(at(3 * toward), 1, spot(place - toward))

    def far_copy():
        ref = wq.at[at(steps), :, qpart]
        return (copy_to(ref, ref, far_s.at[0], far_r.at[0], seq=beside),
            copy_to(ref, ref, far_xs.at[0], far_xr.at[0], groups=other_group))

    def far_cross(role):
        landed, crossing = far_copy()

        @pl.when(role)
        def _():
            landed.wait_recv()
            crossing.start()

    orows = wo.shape[1] // 2
    ocut = (orows // 2 + 15) // 16 * 16
    o_sends = []

    def o_part(way, step):
        base = pl.multiple_of(group * orows, 16)
        if step < steps - 1:
            return pl.ds(base, orows)
        return pl.ds(base, ocut) if way == 0 else pl.ds(pl.multiple_of(base + ocut, 16), orows - ocut)

    def o_copy(way, step):
        origin = at(-step if way == 0 else step)
        ref = wo.at[lax.rem(origin, steps), o_part(way, step)]
        return holds(origin), copy_to(ref, ref, o_s.at[way, step], o_r.at[way, step], seq=peers[way])

    def o_landed(way, step):
        origin = at(-step - 1 if way == 0 else step + 1)
        ref = wo.at[lax.rem(origin, steps), o_part(way, step)]
        return (holds(origin), copy_to(ref, ref, o_s.at[way, step], o_r.at[way, step], seq=peers[way]),
                copy_to(ref, ref, ox_s.at[way, step], ox_r.at[way, step], groups=other_group))

    def o_begin():
        @pl.when(holds(me))
        def _():
            wo_copy.wait()
        for way in (0, 1):
            cond, copy = o_copy(way, 0)

            @pl.when(cond)
            def _():
                copy.start()
            o_sends.append((cond, copy))

    def o_step(step):
        for way in (0, 1):
            cond, arrived, crossing = o_landed(way, step - 1)

            @pl.when(cond)
            def _():
                arrived.wait_recv()
                crossing.start()
            o_sends.append((cond, crossing))
            if step < near:
                onward, copy = o_copy(way, step)

                @pl.when(onward)
                def _():
                    copy.start()
                o_sends.append((onward, copy))

    def o_crossed(step):
        for way in (0, 1):
            cond, _, crossing = o_landed(way, step)

            @pl.when(cond)
            def _():
                crossing.wait_recv()

    def side_copy(origin, hop):
        ref = wo.at[lax.rem(origin, steps)]
        return inner & holds(origin), copy_to(ref, ref, side_s.at[hop], side_r.at[hop], seq=beside)

    def side_send(hop):
        cond, copy = side_copy(at(toward * hop), hop)

        @pl.when(cond)
        def _():
            copy.start()
        o_sends.append((cond, copy))

    def side_wait(hop):
        cond, copy = side_copy(spot(beside_place - toward * hop), hop)

        @pl.when(cond)
        def _():
            copy.wait_recv()

    feed_part = pl.ds(pl.multiple_of(group * orows, 16), orows)

    def feed_copy(origin, index):
        ref = wo.at[lax.rem(origin, steps), feed_part]
        return holds(origin), copy_to(ref, ref, feed_s.at[index], feed_r.at[index], seq=spot(place - toward))

    def feed_send(which):
        origins = (at(2 * toward), spot(beside_place - toward), spot(beside_place - 2 * toward))
        for index in which:
            origin = origins[index]
            cond, copy = feed_copy(origin, index)

            @pl.when(inner & cond)
            def _():
                copy.start()
            o_sends.append((inner & cond, copy))

    feed_crossings = []

    def feed_cross(index):
        origin = (spot(place + 3 * toward), spot(beside_place - 2 * toward), spot(beside_place - 3 * toward))[index]
        held_here, landed = feed_copy(origin, index)
        cond = corner & held_here
        ref = wo.at[lax.rem(origin, steps), feed_part]
        crossing = copy_to(ref, ref, fx_s.at[index], fx_r.at[index], groups=other_group)

        @pl.when(cond)
        def _():
            landed.wait_recv()
            crossing.start()
        o_sends.append((cond, crossing))
        feed_crossings.append((cond, crossing))

    lane_tok = lax.broadcasted_iota(jnp.int32, (tok_count, tok_count), 1)
    row_tok = lax.broadcasted_iota(jnp.int32, (tok_count, tok_count), 0)
    before = jnp.where(row_tok < lane_tok, 1.0, 0.0).astype(jnp.bfloat16)
    slot_row = lax.broadcasted_iota(jnp.int32, (tok_count, tok_count), 0).astype(jnp.float32)

    def process(n):
        table = blocks[n, width : width + E, :].astype(jnp.float32)
        present = table > 0.0
        earlier = dot(jnp.where(present, 1.0, 0.0).astype(jnp.bfloat16), before)
        slot = jnp.where(present, earlier, -1.0)
        comb = jnp.zeros((tok_count, tok_count), jnp.float32)
        for e in range(own):
            mine = expert_row == me * own + e
            slot_e = jnp.sum(jnp.where(mine, slot, 0.0), axis=0, keepdims=True)
            scale_e = jnp.sum(jnp.where(mine, table, 0.0), axis=0, keepdims=True)
            hit = (slot_row == slot_e + float(e * CAP)) & (slot_e >= 0.0)
            comb = jnp.where(hit, scale_e, comb)
        combine[n] = comb.T.astype(jnp.bfloat16)
        select = jnp.where(comb > 0.0, 1.0, 0.0).astype(jnp.bfloat16)[:slots]
        rows = dot(select, blocks[n, :width, :], ((1,), (1,))).astype(jnp.bfloat16)
        for e in range(own):
            picked[e, n] = rows[e * CAP : (e + 1) * CAP]

    o_begin()
    tall = tok_t_ref[...].astype(jnp.float32)
    scale = lax.rsqrt(jnp.sum(tall * tall, axis=0, keepdims=True) / width + eps)
    for i in range(0, width, 128):
        size = min(128, width - i)
        gain = jnp.broadcast_to(gain_ref[pl.ds(i, size)].reshape(1, size), (tok_count, size)).T
        blocks[me, i : i + size, :] = (
            tok_t_ref[i : i + size, :].astype(jnp.float32) * scale * gain
        ).astype(jnp.bfloat16)
    expert_row = lax.broadcasted_iota(jnp.int32, (E, tok_count), 0)
    dense = jnp.zeros((E, tok_count), jnp.float32)
    for j in range(TOP):
        dense = dense + jnp.where(expert_row == routes_ref[j : j + 1, :], weights_ref[j : j + 1, :], 0.0)
    blocks[me, width : width + E, :] = dense.astype(jnp.bfloat16)
    for piece in (0, 1):
        for way in (0, 1):
            ag_send(way, 0, piece ^ way)
    for copy in gu_copies[:2]:
        copy.start()
    side_send(0)
    for copy in wq_copies:
        copy.wait()
    process(me)
    for i in range(0, width, 128):
        size = min(128, width - i)
        hid[:, i : i + size] = tok_t_ref[i : i + size, :].astype(jnp.float32).T
    for step in range(1, steps):
        for piece in (0, 1):
            for way in (0, 1):
                ag[way, step - 1, piece ^ way].wait_recv()
                if step < steps - 1 or piece == 0:
                    ag_send(way, step, piece ^ way)
        if step <= near:
            o_step(step)
        else:
            q_begin()
            o_crossed(step - near - 1)
            side_send(1)
        for copy in (gu_copies[2:], dn_copies[:2], dn_copies[2:])[step - 1]:
            copy.start()
        process(at(-step))
        process(at(step))
    ag[0, steps - 1, 0].wait_recv()
    ag[1, steps - 1, 1].wait_recv()
    process(at(steps))

    o_crossed(1)
    side_send(2)
    pos = {0: 1, 1: 2, 2: 3, 3: 4}
    half = dn.shape[1]
    chunk = CAP
    for e in range(own):
        for j in (2 * e, 2 * e + 1):
            gu_copies[j].wait()
            x = picked[e].reshape(count * CAP, width)
            proj[...] = dot(x, gu[j])

            @pl.loop(0, count)
            def _(i):
                r = pl.ds(pl.multiple_of(i * chunk, 16), chunk)
                gate = proj[r, :half]
                up = proj[r, half:]
                act[j % 2, r, :] = (gate * jax.nn.sigmoid(1.702 * gate) * (up + 1.0)).astype(jnp.bfloat16)

            if j in (0, 2):
                q_step((0, 2).index(j) + 1)
                if j == 0:
                    far_side()
        dn_copies[2 * e].wait()
        dn_copies[2 * e + 1].wait()
        result = dot(act[0], dn[2 * e]) + dot(act[1], dn[2 * e + 1])
        done[:, e * CAP : (e + 1) * CAP, :] = result.astype(jnp.bfloat16).reshape(count, CAP, width)

    hrows = tok_count // 2
    tail = width % 128
    full = width - tail
    folds = 128 // tail
    trows = hrows // folds
    base = hrows * (full // 128)

    def part(n):
        value = dot(combine[n][:, :slots], done[n])
        for c in (0, 1):
            rows = value[c * hrows : (c + 1) * hrows]
            for i in range(0, full, 128):
                parts[n, c, i // 128 * hrows : (i // 128 + 1) * hrows, :] = rows[:, i : i + 128].astype(jnp.bfloat16)
            parts[n, c, base : base + trows, :] = jnp.concatenate(
                [rows[k * trows : (k + 1) * trows, full:] for k in range(folds)], axis=1
            ).astype(jnp.bfloat16)

    rs = {}

    def rs_add(goal, way, step, piece):
        here = held.at[way, step, piece]
        copy_to(here, here, rs_s.at[0, step, piece], rs_r.at[way, step, piece], seq=peers[0]).wait_recv()
        parts[goal, piece] = (
            parts[goal, piece].astype(jnp.float32) + held[way, step, piece].astype(jnp.float32)
        ).astype(jnp.bfloat16)

    def rs_send(way, step, piece):
        goal = at((steps - step) * (1 if way == 0 else -1))
        if (way, step - 1, piece) in rs:
            @pl.when(jnp.logical_not(corner_fresh[way]))
            def _():
                rs_add(goal, way, step - 1, piece)
        if step == steps - 1:
            @pl.when(inner_out[way])
            def _():
                rs_add(goal, 2, 2, piece)
            if piece == way:
                @pl.when(inner_in[way])
                def _():
                    rs_add(goal, 2, 0, piece)
        landing, peer = way, peers[way]
        if step < steps - 1:
            landing = jnp.where(inner_out[way], 2, way)
            peer = jnp.where(inner_out[way], beside, peer)
        rs[way, step, piece] = launch(copy_to(parts.at[goal, piece], held.at[landing, step, piece],
            rs_s.at[way, step, piece], rs_r.at[landing, step, piece], seq=peer))

    part(at(steps))
    rs_send(0, 0, 0)
    rs_send(1, 0, 1)
    q_step(3)
    far_cross(inner)
    far_feed()
    for way in (0, 1):
        part(at((steps - 1) * (1 if way == 0 else -1)))
        rs_send(way, 1, 1 - way)
    for offset in range(steps - 2, 0, -1):
        part(at(offset))
        part(at(-offset))
    part(me)
    for hop in range(3):
        side_wait(hop)
    feed_send((0, 1, 2))
    rs_send(0, 1, 0)
    rs_send(1, 1, 1)
    for step in range(2, steps):
        for piece in (0, 1):
            for way in (0, 1):
                rs_send(way, step, 1 ^ piece ^ way)
        if step == 2:
            far_cross(corner)
        feed_cross(step - 2)
    feed_cross(2)
    for c in (0, 1):
        @pl.when(inner)
        def _():
            rs_add(me, 2, 1, c)
        for way in (0, 1):
            copy_to(held.at[way, steps - 1, c], held.at[way, steps - 1, c], rs_s.at[way, steps - 1, c],
                rs_r.at[way, steps - 1, c], seq=peers[way]).wait_recv()
        rows = slice(c * hrows, (c + 1) * hrows)
        value = (parts[me, c].astype(jnp.float32) + held[0, steps - 1, c].astype(jnp.float32)
            + held[1, steps - 1, c].astype(jnp.float32))
        for i in range(0, full, 128):
            term = value[i // 128 * hrows : (i // 128 + 1) * hrows]
            hid[rows, i : i + 128] = (hid[rows, i : i + 128] + term).astype(jnp.bfloat16).astype(jnp.float32)
        term = jnp.concatenate(
            [value[base : base + trows, k * tail : (k + 1) * tail] for k in range(folds)], axis=0)
        hid[rows, full:] = (hid[rows, full:] + term).astype(jnp.bfloat16).astype(jnp.float32)
    hidden = hid[...]
    scale = lax.rsqrt(jnp.sum(hidden * hidden, axis=1, keepdims=True) / width + eps)
    normed = hidden * scale * attn_gain_ref[...].reshape(1, width)
    shard = wq.shape[1]
    for i in range(count):
        both[core, i] = normed[:, i * shard : (i + 1) * shard].astype(jnp.bfloat16)
    pair = launch(copy_to(both.at[core], both.at[core], pair_s.at[0], pair_r.at[0], pipe=other_core))

    for key in qx:
        qx[key].wait_recv()
    far_copy()[1].wait_recv()

    def project(m, columns):
        total = None
        for i in range(count):
            x = both[:, i].reshape(2 * tok_count, shard) if m is None else both[m, i]
            term = dot(x, wq[i, :, columns])
            total = term if total is None else total + term
        return total

    kv[core] = project(core, pl.ds(0, 2 * kw)).astype(jnp.bfloat16)
    along = [launch(copy_to(kv.at[core], halo.at[core], halo_s.at[0], halo_r.at[0], seq=following))]
    for i in range(0, width, 128):
        size = min(128, width - i)
        hid_t[i : i + size, :] = hid[:, i : i + size].T
    pair.wait_recv()
    kv[other_core] = project(other_core, pl.ds(0, 2 * kw)).astype(jnp.bfloat16)
    along.append(launch(copy_to(kv.at[other_core], halo.at[other_core], halo_s.at[1], halo_r.at[1], seq=following)))
    packed = project(None, pl.ds(2 * kw, qw)).astype(jnp.bfloat16)
    queries[...] = (packed * (float(HEAD_SIZE) ** -0.5)).reshape(2, tok_count, qw)

    wide = (4 * tok_count, 2 * tok_count)
    lane = lax.broadcasted_iota(jnp.int32, wide, 1)
    row = lax.rem(lax.broadcasted_iota(jnp.int32, wide, 0), tok_count)
    left = lane < tok_count
    past = jnp.where(left, lane, lane - tok_count) > row
    low = lax.broadcasted_iota(jnp.int32, (tok_count, 2 * HEAD_SIZE), 1) < HEAD_SIZE

    def stacked(tile, head):
        tile = tile.astype(jnp.float32)
        kept = jnp.where(low if head == 0 else ~low, tile, 0.0)
        turned = pltpu.roll(kept, HEAD_SIZE, 1)
        pair_of = (kept, turned) if head == 0 else (turned, kept)
        return jnp.concatenate(pair_of, axis=0).astype(jnp.bfloat16)

    tiles = qw // 128
    per_head = tiles // 2

    def attention(m, known):
        past_kv = passed[...]
        dropped = past & jnp.logical_not(known)
        for head in range(2):
            k_own = stacked(kv[m, :, :kw], head)
            v_own = stacked(kv[m, :, kw:], head)
            k_past = stacked(past_kv[:, :kw], head)
            v_past = stacked(past_kv[:, kw:], head)
            for first in range(head * per_head, (head + 1) * per_head, 4):
                some = range(first, first + 4)
                sinks = [jnp.exp(jnp.concatenate(
                    [jnp.full((tok_count, 1), sink_ref[core * 2 * tiles + 2 * t + side]) for t in some], axis=0))
                    for side in (0, 1)]
                x = jnp.concatenate([queries[m, :, t * 128 : (t + 1) * 128] for t in some], axis=0)
                score = jnp.where(past, dot(x, k_past, ((1,), (1,))), dot(x, k_own, ((1,), (1,))))
                weight = jnp.where(dropped, 0.0, jnp.exp(score))
                mass_a = jnp.sum(weight[:, :tok_count], axis=1, keepdims=True) + sinks[0]
                mass_b = jnp.sum(weight[:, tok_count:], axis=1, keepdims=True) + sinks[1]
                probs = weight * jnp.where(left, 1.0 / mass_a, 1.0 / mass_b)
                result = (
                    dot(jnp.where(past, 0.0, probs).astype(jnp.bfloat16), v_own)
                    + dot(jnp.where(past, probs, 0.0).astype(jnp.bfloat16), v_past)
                ).astype(jnp.bfloat16)
                for k, t in enumerate(some):
                    mixed[m, :, t * 128 : (t + 1) * 128] = result[k * tok_count : (k + 1) * tok_count]

    share = wo.shape[2]
    last = copy_to(given, back, pair_s.at[1], pair_r.at[1], pipe=other_core)

    def output(m):
        total = None
        for i in range(steps):
            term = dot(wo[i], mixed[m, :, i * share : (i + 1) * share], ((1,), (1,)))
            total = term if total is None else total + term

        @pl.when(m == other_core)
        def _():
            given[...] = total.astype(jnp.bfloat16)
            last.start()

        @pl.when(m == core)
        def _():
            hid_t[...] = hid_t[...] + total

    early = jnp.where(me == 0, 0, other_core)
    late = 1 - early

    @pl.when(me > 0)
    def _():
        for copy in along:
            copy.wait_recv()
        passed[...] = halo[other_core]

    @pl.when(me == 0)
    def _():
        passed[...] = jnp.zeros_like(passed)
    attention(early, me > 0)
    for cond, crossing in feed_crossings:
        @pl.when(cond)
        def _():
            crossing.wait_recv()
    output(early)

    @pl.when(me == 0)
    def _():
        for copy in along:
            copy.wait_recv()
    passed[...] = halo[jnp.where(me == 0, 0, core)]
    attention(late, me >= 0)
    output(late)
    last.wait_recv()
    out_ref[...] = (hid_t[...] + back[...].astype(jnp.float32)).astype(jnp.bfloat16)
    last.wait_send()
    for _, copy in sends:
        copy.wait_send()
    far_copy()[1].wait_send()
    for cond, copy in o_sends + far_sends:
        @pl.when(cond)
        def _():
            copy.wait_send()


def whole_layer(
    tokens, routes, route_weights, moe_gain, gate_up, down_proj, attn_gain, qkv_proj,
    head_sink_logits, out_proj,
):
    count = lax.axis_size("seq")
    steps = count // 2
    tok_count, width = tokens.shape[1:]
    own = gate_up.shape[0] // 2
    half = down_proj.shape[1]
    heads = QUERY_HEADS // 2
    qw = heads * HEAD_SIZE
    kw = KEY_VALUE_HEADS * HEAD_SIZE // 2
    chunk = tok_count // 2 * width // 128
    dma = pltpu.SemaphoreType.DMA
    bf16 = jnp.bfloat16
    vm = pl.BlockSpec(memory_space=pltpu.VMEM)
    hbm = pl.BlockSpec(memory_space=pl.ANY)
    out = pl.pallas_call(
        layer_kernel,
        out_shape=jax.ShapeDtypeStruct((width, tok_count), bf16),
        in_specs=[vm] * 5 + [pl.BlockSpec(memory_space=pltpu.SMEM)] + [hbm] * 4,
        out_specs=vm,
        scratch_shapes=[
            pltpu.VMEM((count, width + E, tok_count), bf16),
            pltpu.VMEM((own, count, CAP, width), bf16),
            pltpu.VMEM((count, tok_count, tok_count), bf16),
            pltpu.VMEM(gate_up.shape, bf16),
            pltpu.VMEM(down_proj.shape, bf16),
            pltpu.VMEM((count * CAP, 2 * half), jnp.float32),
            pltpu.VMEM((2, count * CAP, half), bf16),
            pltpu.VMEM((count, own * CAP, width), bf16),
            pltpu.VMEM((count, 2, chunk, 128), bf16),
            pltpu.VMEM((3, steps, 2, chunk, 128), bf16),
            pltpu.VMEM((count, qkv_proj.shape[0], 2 * kw + qw), bf16),
            pltpu.VMEM((steps, width, out_proj.shape[0]), bf16),
            pltpu.VMEM((2, count, tok_count, qkv_proj.shape[0]), bf16),
            pltpu.VMEM((2, tok_count, 2 * kw), bf16),
            pltpu.VMEM((2, tok_count, 2 * kw), bf16),
            pltpu.VMEM((2, tok_count, qw), bf16),
            pltpu.VMEM((2, tok_count, qw), bf16),
            pltpu.VMEM((width, tok_count), bf16),
            pltpu.VMEM((width, tok_count), bf16),
            pltpu.VMEM((tok_count, width), jnp.float32),
            pltpu.VMEM((width, tok_count), jnp.float32),
            pltpu.VMEM((tok_count, 2 * kw), bf16),
            dma((2 * own,)), dma((2 * own,)), dma((3,)), dma((1,)),
            dma((2, steps, 2)), dma((2, steps, 2)), dma((2, steps, 2)), dma((3, steps, 2)),
            dma((2, steps)), dma((2, steps)), dma((2, steps)), dma((2, steps)),
            dma((2, steps)), dma((2, steps)), dma((2, steps)), dma((2, steps)),
            dma((2,)), dma((1,)), dma((1,)), dma((1,)),
            dma((3,)), dma((3,)), dma((3,)), dma((3,)), dma((3,)), dma((3,)), dma((2,)), dma((2,)), dma((2,)), dma((2,)),
        ],
        compiler_params=pltpu.CompilerParams(
            collective_id=0, has_side_effects=True, vmem_limit_bytes=67043328),
    )(tokens[0].T, routes[0].T, route_weights[0].T, moe_gain, attn_gain, head_sink_logits,
      gate_up, down_proj, qkv_proj, out_proj.T)
    return out.T[None]


def solution(mesh):
    in_specs = (
        P("pipe", ("groups", "seq"), None),
        P("pipe", ("groups", "seq"), None),
        P("pipe", ("groups", "seq"), None),
        P(),
        P("seq", None, None),
        P("seq", None, None),
        P(),
        P("seq", None),
        P(),
        P("seq", None),
    )
    out_specs = P("pipe", ("groups", "seq"), None)
    seq_count, pipe_count, group_count = mesh.shape["seq"], mesh.shape["pipe"], mesh.shape["groups"]
    whole = (
        pipe_count == 2
        and group_count == 2
        and seq_count % 2 == 0
        and 2 * E // seq_count == 4
        and seq_count == 8
        and QUERY_HEADS % (2 * seq_count) == 0
    )
    return jax.shard_map(
        whole_layer if whole else body, mesh=mesh, in_specs=in_specs, out_specs=out_specs, check_vma=False
    )
```

```python
import functools

import jax
import jax.numpy as jnp
from jax import lax
from jax.experimental import pallas as pl
from jax.experimental.pallas import tpu as pltpu
from jax.sharding import PartitionSpec as P

MESH = pl.DeviceIdType.MESH
E = 16
TOP = 4
QUERY_HEADS = 32
KEY_VALUE_HEADS = 4
HEAD_SIZE = 64
WINDOW_SPAN = 128
HALF = 720
CAP = 48


eps = 1e-05


def from_partner(value, axis, distance):
    return lax.ppermute(value, axis, [(i, i ^ 1 << distance) for i in range(lax.axis_size(axis))])


def shifted(value, axis, steps):
    count = lax.axis_size(axis)
    pairs = [(source, (source + steps) % count) for source in range(count)]
    return lax.ppermute(value, axis, pairs)


def passed_along(value, axis, steps):
    count = lax.axis_size(axis)
    first, last = (max(0, -steps), min(count, count - steps))
    return lax.ppermute(value, axis, [(source, source + steps) for source in range(first, last)])


def rms_scale(value_matrix, gain):
    widened = value_matrix.astype(jnp.float32)
    mean_square = jnp.mean(widened * widened, axis=-1, keepdims=True)
    return (widened * lax.rsqrt(mean_square + eps) * gain).astype(jnp.bfloat16)


def slot_positions(route_rows):
    flat = route_rows.reshape(-1)
    onehot = (flat[:, None] == jnp.arange(E, dtype=jnp.int32)[None, :]).astype(jnp.int32)
    earlier = jnp.cumsum(onehot, axis=0) - onehot
    return flat * CAP + jnp.sum(earlier * onehot, axis=1)


def expert_layer(local, route_rows, route_scale, moe_gain, gate_up, down_proj):
    tok_count, width = local.shape
    seq_count = lax.axis_size("seq")
    per_device = gate_up.shape[0]
    normed = rms_scale(local, moe_gain)
    positions = slot_positions(route_rows)
    select = (positions[None, :] == jnp.arange(E * CAP, dtype=jnp.int32)[:, None]).astype(
        jnp.bfloat16
    )
    repeated = jnp.repeat(normed, TOP, axis=0)
    table = jnp.dot(select, repeated, preferred_element_type=jnp.float32).astype(jnp.bfloat16)
    by_expert = table.reshape(E, CAP, width)
    first = lax.axis_index("seq") % 2 == 0
    outgoing = jnp.repeat(by_expert, 2, axis=0).reshape(seq_count, per_device, CAP, width)
    received = lax.all_to_all(outgoing, "seq", split_axis=0, concat_axis=0, tiled=True)
    projected = jnp.einsum("spcd,pdh->spch", received, gate_up, preferred_element_type=jnp.float32)
    gate_part = projected[..., :HALF]
    up_part = projected[..., HALF:]
    hidden = (gate_part * jax.nn.sigmoid(1.702 * gate_part) * (up_part + 1.0)).astype(jnp.bfloat16)
    partial_value = jnp.einsum(
        "spch,phd->spcd", hidden, down_proj, preferred_element_type=jnp.float32
    )
    if per_device >= 2:
        finished = (
            partial_value.reshape(seq_count, per_device // 2, 2, CAP, width)
            .sum(axis=2)
            .astype(jnp.bfloat16)
        )
    else:
        lower_rows = partial_value[:, :, : CAP // 2]
        upper_rows = partial_value[:, :, CAP // 2 :]
        kept = jnp.where(first, lower_rows, upper_rows)
        given = jnp.where(first, upper_rows, lower_rows)
        partner_part = from_partner(given.astype(jnp.bfloat16), "seq", 0).astype(given.dtype)
        finished = (kept + partner_part).astype(jnp.bfloat16)
    summed = lax.all_to_all(finished, "seq", split_axis=0, concat_axis=0, tiled=True).reshape(
        E * CAP, width
    )
    picked = lax.dot_general(
        select, summed, (((0,), (0,)), ((), ())), preferred_element_type=jnp.float32
    )
    weighted = jnp.sum(picked.reshape(tok_count, TOP, width) * route_scale[:, :, None], axis=1)
    return (local.astype(jnp.float32) + weighted).astype(jnp.bfloat16)


def attend(query_matrix, keys_extended, values_extended, head_sink_logits, halo_valid):
    tok_count = query_matrix.shape[0]
    query_groups = QUERY_HEADS // KEY_VALUE_HEADS
    attention_block = min(tok_count, 512)
    scale = float(HEAD_SIZE) ** (-0.5)
    sink_mass_total = jnp.exp(head_sink_logits).reshape(KEY_VALUE_HEADS, query_groups, 1, 1)
    block_queries = query_matrix.reshape(attention_block, KEY_VALUE_HEADS, query_groups, HEAD_SIZE)
    block_keys = keys_extended.reshape(attention_block + WINDOW_SPAN, KEY_VALUE_HEADS, HEAD_SIZE)
    block_values = values_extended.reshape(
        attention_block + WINDOW_SPAN, KEY_VALUE_HEADS, HEAD_SIZE
    )
    scores = (
        jnp.einsum("qhgd,khd->hgqk", block_queries, block_keys, preferred_element_type=jnp.float32)
        * scale
    )
    query_pos = jnp.arange(attention_block, dtype=jnp.int32)[:, None] + WINDOW_SPAN
    key_pos = jnp.arange(attention_block + WINDOW_SPAN, dtype=jnp.int32)[None, :]
    distance = query_pos - key_pos
    allowed = (
        (distance >= 0) & (distance < WINDOW_SPAN) & ((key_pos + 0 >= WINDOW_SPAN) | halo_valid)
    )
    weights = jnp.where(allowed, jnp.exp(scores), 0.0)
    probs = (weights / (jnp.sum(weights, axis=-1, keepdims=True) + sink_mass_total)).astype(
        jnp.bfloat16
    )
    mixed = jnp.einsum("hgqk,khd->qhgd", probs, block_values, preferred_element_type=jnp.float32)
    outputs = mixed.reshape(attention_block, QUERY_HEADS * HEAD_SIZE).astype(jnp.bfloat16)
    return outputs


def body(
    tokens,
    routes,
    route_weights,
    moe_gain,
    gate_up,
    down_proj,
    attn_gain,
    qkv_proj,
    head_sink_logits,
    out_proj,
):
    hidden = expert_layer(tokens[0], routes[0], route_weights[0], moe_gain, gate_up, down_proj)
    tok_count, width = hidden.shape
    normed = rms_scale(hidden, attn_gain)
    seq_index = lax.axis_index("seq")
    pipe_index = lax.axis_index("pipe")
    halo_valid = (seq_index > 0) | (pipe_index > 0)
    query_width = QUERY_HEADS * HEAD_SIZE
    width_of_pair = KEY_VALUE_HEADS * HEAD_SIZE
    columns = normed
    packed_heads = jnp.dot(
        columns,
        lax.all_gather(qkv_proj, "seq", axis=0, tiled=True),
        preferred_element_type=jnp.float32,
    ).astype(jnp.bfloat16)
    from_left = shifted(packed_heads[tok_count - WINDOW_SPAN :, query_width:], "seq", 1)
    from_section = passed_along(from_left, "pipe", 1)
    halo_pairs = jnp.where(seq_index == 0, from_section, from_left)
    query_matrix = packed_heads[:, :query_width]
    pairs_ext = jnp.concatenate([halo_pairs, packed_heads[:, query_width:]], axis=0)
    keys_extended = pairs_ext[:, :width_of_pair]
    values_extended = pairs_ext[:, width_of_pair:]
    attended = attend(query_matrix, keys_extended, values_extended, head_sink_logits, halo_valid)
    columns = attended
    projected = jnp.dot(
        columns,
        lax.all_gather(out_proj, "seq", axis=0, tiled=True),
        preferred_element_type=jnp.float32,
    )
    return (hidden.astype(jnp.float32) + projected).astype(jnp.bfloat16)[None]


def ring_place(index, count, folded):
    if not folded:
        return index
    line, side = index // 2, index % 2
    return line + side * (count - 1 - 2 * line)

def ring_index(place, count, folded):
    if not folded:
        return place
    side = place // (count // 2)
    line = place + side * (count - 1 - 2 * place)
    return 2 * line + side


def copy_to(src, dst, send, recv, **device):
    return pltpu.make_async_remote_copy(src_ref=src, dst_ref=dst, send_sem=send, recv_sem=recv,
        device_id=device, device_id_type=MESH)


def dot(a, b, dims=((1,), (0,))):
    return lax.dot_general(a, b, (dims, ((), ())), preferred_element_type=jnp.float32)


def layer_kernel(
    tok_t_ref, routes_ref, weights_ref, gain_ref, attn_gain_ref, sink_ref,
    gate_up_ref, down_ref, qkv_ref, out_t_ref,
    out_ref,
    blocks, picked, combine, gu, dn, proj, act, done, parts, held, wq, wo,
    both, kv, halo, queries, mixed, given, back, hid, hid_t, passed,
    gu_sem, dn_sem, wq_sem, wo_sem, ag_s, ag_r, rs_s, rs_r, q_s, q_r, qx_s, qx_r,
    o_s, o_r, ox_s, ox_r, far_s, far_r, far_xs, far_xr, side_s, side_r, feed_s, feed_r, fx_s, fx_r, pair_s, pair_r, halo_s, halo_r,
):
    count = lax.axis_size("seq")
    steps = count // 2
    me = lax.axis_index("seq")
    core = lax.axis_index("pipe")
    group = lax.axis_index("groups")
    width, tok_count = tok_t_ref.shape
    own = picked.shape[0]
    slots = own * CAP
    place = ring_place(me, count, True)
    at = lambda offset: ring_index(lax.rem(place + offset + count, count), count, True)
    spot = lambda p: ring_index(lax.rem(p + count, count), count, True)
    peers = (at(1), at(-1))
    column = lax.rem(place, steps)
    inner = (column > 0) & (column < steps - 1)
    corner = jnp.logical_not(inner)
    low = column < steps // 2
    toward = jnp.where(low, 1, -1)
    outward = (jnp.logical_not(low), low)
    inner_out = [inner & outward[way] for way in (0, 1)]
    inner_in = [inner & jnp.logical_not(outward[way]) for way in (0, 1)]
    corner_fresh = [corner & outward[way] for way in (0, 1)]
    beside_place = count - 1 - place
    beside = spot(beside_place)
    following, preceding = lax.rem(me + 1, count), lax.rem(me + count - 1, count)
    other_core, other_group = 1 - core, 1 - group
    sends = []

    def launch(copy):
        copy.start()
        sends.append((None, copy))
        return copy

    barrier = pltpu.get_barrier_semaphore()
    for device in ({"seq": peers[0]}, {"seq": peers[1]}, {"seq": following}, {"seq": preceding},
                   {"pipe": other_core}, {"groups": other_group}, {"seq": beside}):
        pl.semaphore_signal(barrier, inc=1, device_id=device, device_id_type=MESH)
    qw, kw = queries.shape[2], kv.shape[2] // 2
    all_q = QUERY_HEADS * HEAD_SIZE
    all_k = KEY_VALUE_HEADS * HEAD_SIZE
    wo_slot = lax.rem(me, steps)
    holds = lambda origin: lax.div(origin, steps) == core
    wo_copy = pltpu.make_async_copy(out_t_ref, wo.at[wo_slot], wo_sem.at[0])

    @pl.when(holds(me))
    def _():
        wo_copy.start()

    wq_copies = []
    for i, (source, goal, size) in enumerate((
        (all_q + core * kw, 0, kw), (all_q + all_k + core * kw, kw, kw), (core * qw, 2 * kw, qw))):
        wq_copies.append(pltpu.make_async_copy(
            qkv_ref.at[:, pl.ds(pl.multiple_of(source, 128), size)],
            wq.at[me, :, pl.ds(goal, size)], wq_sem.at[i]))
    for copy in wq_copies:
        copy.start()
    gu_copies = [pltpu.make_async_copy(gate_up_ref.at[j], gu.at[j], gu_sem.at[j]) for j in range(2 * own)]
    dn_copies = [pltpu.make_async_copy(down_ref.at[j], dn.at[j], dn_sem.at[j]) for j in range(2 * own)]

    pl.semaphore_wait(barrier, 7)

    rows_all = blocks.shape[1]
    cut = (rows_all // 2 + 15) // 16 * 16
    pieces = (pl.ds(0, cut), pl.ds(cut, rows_all - cut))
    ag = {}

    def ag_send(way, step, piece):
        origin = at(-step if way == 0 else step)
        ref = blocks.at[origin, pieces[piece]]
        ag[way, step, piece] = launch(copy_to(ref, ref, ag_s.at[way, step, piece], ag_r.at[way, step, piece], seq=peers[way]))

    qcols = wq.shape[2] // 2
    q = {}
    qx = {}

    qpart = pl.ds(pl.multiple_of(group * qcols, 128), qcols)
    near = steps // 2

    def q_send(way, step):
        ref = wq.at[at(-step if way == 0 else step), :, qpart]
        q[way, step] = launch(copy_to(ref, ref, q_s.at[way, step], q_r.at[way, step], seq=peers[way]))

    def q_cross(way, step):
        q[way, step].wait_recv()
        ref = wq.at[at(-step - 1 if way == 0 else step + 1), :, qpart]
        qx[way, step] = launch(copy_to(ref, ref, qx_s.at[way, step], qx_r.at[way, step], groups=other_group))

    def q_begin():
        for way in (0, 1):
            q_send(way, 0)

    def q_step(step):
        for way in (0, 1):
            q_cross(way, step - 1)
            if step < steps - 1:
                q_send(way, step)

    far_sends = []

    def far_out(origin, kind, peer):
        ref = wq.at[origin, :, qpart]
        copy = copy_to(ref, ref, far_s.at[kind], far_r.at[0], seq=peer)

        @pl.when(inner)
        def _():
            copy.start()
        far_sends.append((inner, copy))

    def far_side():
        far_out(at(toward), 0, beside)

    def far_feed():
        far_out(at(3 * toward), 1, spot(place - toward))

    def far_copy():
        ref = wq.at[at(steps), :, qpart]
        return (copy_to(ref, ref, far_s.at[0], far_r.at[0], seq=beside),
            copy_to(ref, ref, far_xs.at[0], far_xr.at[0], groups=other_group))

    def far_cross(role):
        landed, crossing = far_copy()

        @pl.when(role)
        def _():
            landed.wait_recv()
            crossing.start()

    orows = wo.shape[1] // 2
    ocut = (orows // 2 + 15) // 16 * 16
    o_sends = []

    def o_part(way, step):
        base = pl.multiple_of(group * orows, 16)
        if step < steps - 1:
            return pl.ds(base, orows)
        return pl.ds(base, ocut) if way == 0 else pl.ds(pl.multiple_of(base + ocut, 16), orows - ocut)

    def o_copy(way, step):
        origin = at(-step if way == 0 else step)
        ref = wo.at[lax.rem(origin, steps), o_part(way, step)]
        return holds(origin), copy_to(ref, ref, o_s.at[way, step], o_r.at[way, step], seq=peers[way])

    def o_landed(way, step):
        origin = at(-step - 1 if way == 0 else step + 1)
        ref = wo.at[lax.rem(origin, steps), o_part(way, step)]
        return (holds(origin), copy_to(ref, ref, o_s.at[way, step], o_r.at[way, step], seq=peers[way]),
                copy_to(ref, ref, ox_s.at[way, step], ox_r.at[way, step], groups=other_group))

    def o_begin():
        @pl.when(holds(me))
        def _():
            wo_copy.wait()
        for way in (0, 1):
            cond, copy = o_copy(way, 0)

            @pl.when(cond)
            def _():
                copy.start()
            o_sends.append((cond, copy))

    def o_step(step):
        for way in (0, 1):
            cond, arrived, crossing = o_landed(way, step - 1)

            @pl.when(cond)
            def _():
                arrived.wait_recv()
                crossing.start()
            o_sends.append((cond, crossing))
            if step < near:
                onward, copy = o_copy(way, step)

                @pl.when(onward)
                def _():
                    copy.start()
                o_sends.append((onward, copy))

    def o_crossed(step):
        for way in (0, 1):
            cond, _, crossing = o_landed(way, step)

            @pl.when(cond)
            def _():
                crossing.wait_recv()

    def side_copy(origin, hop):
        ref = wo.at[lax.rem(origin, steps)]
        return inner & holds(origin), copy_to(ref, ref, side_s.at[hop], side_r.at[hop], seq=beside)

    def side_send(hop):
        cond, copy = side_copy(at(toward * hop), hop)

        @pl.when(cond)
        def _():
            copy.start()
        o_sends.append((cond, copy))

    def side_wait(hop):
        cond, copy = side_copy(spot(beside_place - toward * hop), hop)

        @pl.when(cond)
        def _():
            copy.wait_recv()

    feed_part = pl.ds(pl.multiple_of(group * orows, 16), orows)

    def feed_copy(origin, index):
        ref = wo.at[lax.rem(origin, steps), feed_part]
        return holds(origin), copy_to(ref, ref, feed_s.at[index], feed_r.at[index], seq=spot(place - toward))

    def feed_send(which):
        origins = (at(2 * toward), spot(beside_place - toward), spot(beside_place - 2 * toward))
        for index in which:
            origin = origins[index]
            cond, copy = feed_copy(origin, index)

            @pl.when(inner & cond)
            def _():
                copy.start()
            o_sends.append((inner & cond, copy))

    feed_crossings = []

    def feed_cross(index):
        origin = (spot(place + 3 * toward), spot(beside_place - 2 * toward), spot(beside_place - 3 * toward))[index]
        held_here, landed = feed_copy(origin, index)
        cond = corner & held_here
        ref = wo.at[lax.rem(origin, steps), feed_part]
        crossing = copy_to(ref, ref, fx_s.at[index], fx_r.at[index], groups=other_group)

        @pl.when(cond)
        def _():
            landed.wait_recv()
            crossing.start()
        o_sends.append((cond, crossing))
        feed_crossings.append((cond, crossing))

    lane_tok = lax.broadcasted_iota(jnp.int32, (tok_count, tok_count), 1)
    row_tok = lax.broadcasted_iota(jnp.int32, (tok_count, tok_count), 0)
    before = jnp.where(row_tok < lane_tok, 1.0, 0.0).astype(jnp.bfloat16)
    slot_row = lax.broadcasted_iota(jnp.int32, (tok_count, tok_count), 0).astype(jnp.float32)

    def process(n):
        table = blocks[n, width : width + E, :].astype(jnp.float32)
        present = table > 0.0
        earlier = dot(jnp.where(present, 1.0, 0.0).astype(jnp.bfloat16), before)
        slot = jnp.where(present, earlier, -1.0)
        comb = jnp.zeros((tok_count, tok_count), jnp.float32)
        for e in range(own):
            mine = expert_row == me * own + e
            slot_e = jnp.sum(jnp.where(mine, slot, 0.0), axis=0, keepdims=True)
            scale_e = jnp.sum(jnp.where(mine, table, 0.0), axis=0, keepdims=True)
            hit = (slot_row == slot_e + float(e * CAP)) & (slot_e >= 0.0)
            comb = jnp.where(hit, scale_e, comb)
        combine[n] = comb.T.astype(jnp.bfloat16)
        select = jnp.where(comb > 0.0, 1.0, 0.0).astype(jnp.bfloat16)[:slots]
        rows = dot(select, blocks[n, :width, :], ((1,), (1,))).astype(jnp.bfloat16)
        for e in range(own):
            picked[e, n] = rows[e * CAP : (e + 1) * CAP]

    o_begin()
    tall = tok_t_ref[...].astype(jnp.float32)
    scale = lax.rsqrt(jnp.sum(tall * tall, axis=0, keepdims=True) / width + eps)
    for i in range(0, width, 128):
        size = min(128, width - i)
        gain = jnp.broadcast_to(gain_ref[pl.ds(i, size)].reshape(1, size), (tok_count, size)).T
        blocks[me, i : i + size, :] = (
            tok_t_ref[i : i + size, :].astype(jnp.float32) * scale * gain
        ).astype(jnp.bfloat16)
    expert_row = lax.broadcasted_iota(jnp.int32, (E, tok_count), 0)
    dense = jnp.zeros((E, tok_count), jnp.float32)
    for j in range(TOP):
        dense = dense + jnp.where(expert_row == routes_ref[j : j + 1, :], weights_ref[j : j + 1, :], 0.0)
    blocks[me, width : width + E, :] = dense.astype(jnp.bfloat16)
    for piece in (0, 1):
        for way in (0, 1):
            ag_send(way, 0, piece ^ way)
    for copy in gu_copies[:2]:
        copy.start()
    side_send(0)
    for copy in wq_copies:
        copy.wait()
    process(me)
    for i in range(0, width, 128):
        size = min(128, width - i)
        hid[:, i : i + size] = tok_t_ref[i : i + size, :].astype(jnp.float32).T
    for step in range(1, steps):
        for piece in (0, 1):
            for way in (0, 1):
                ag[way, step - 1, piece ^ way].wait_recv()
                if step < steps - 1 or piece == 0:
                    ag_send(way, step, piece ^ way)
        if step <= near:
            o_step(step)
        else:
            q_begin()
            o_crossed(step - near - 1)
            side_send(1)
        for copy in (gu_copies[2:], dn_copies[:2], dn_copies[2:])[step - 1]:
            copy.start()
        process(at(-step))
        process(at(step))
    ag[0, steps - 1, 0].wait_recv()
    ag[1, steps - 1, 1].wait_recv()
    process(at(steps))

    o_crossed(1)
    side_send(2)
    pos = {0: 1, 1: 2, 2: 3, 3: 4}
    half = dn.shape[1]
    chunk = CAP
    for e in range(own):
        for j in (2 * e, 2 * e + 1):
            gu_copies[j].wait()
            x = picked[e].reshape(count * CAP, width)
            proj[...] = dot(x, gu[j])

            @pl.loop(0, count)
            def _(i):
                r = pl.ds(pl.multiple_of(i * chunk, 16), chunk)
                gate = proj[r, :half]
                up = proj[r, half:]
                act[j % 2, r, :] = (gate * jax.nn.sigmoid(1.702 * gate) * (up + 1.0)).astype(jnp.bfloat16)

            if j in (0, 2):
                q_step((0, 2).index(j) + 1)
                if j == 0:
                    far_side()
        dn_copies[2 * e].wait()
        dn_copies[2 * e + 1].wait()
        result = dot(act[0], dn[2 * e]) + dot(act[1], dn[2 * e + 1])
        done[:, e * CAP : (e + 1) * CAP, :] = result.astype(jnp.bfloat16).reshape(count, CAP, width)

    hrows = tok_count // 2
    tail = width % 128
    full = width - tail
    folds = 128 // tail
    trows = hrows // folds
    base = hrows * (full // 128)

    def part(n):
        value = dot(combine[n][:, :slots], done[n])
        for c in (0, 1):
            rows = value[c * hrows : (c + 1) * hrows]
            for i in range(0, full, 128):
                parts[n, c, i // 128 * hrows : (i // 128 + 1) * hrows, :] = rows[:, i : i + 128].astype(jnp.bfloat16)
            parts[n, c, base : base + trows, :] = jnp.concatenate(
                [rows[k * trows : (k + 1) * trows, full:] for k in range(folds)], axis=1
            ).astype(jnp.bfloat16)

    rs = {}

    def rs_add(goal, way, step, piece):
        here = held.at[way, step, piece]
        copy_to(here, here, rs_s.at[0, step, piece], rs_r.at[way, step, piece], seq=peers[0]).wait_recv()
        parts[goal, piece] = (
            parts[goal, piece].astype(jnp.float32) + held[way, step, piece].astype(jnp.float32)
        ).astype(jnp.bfloat16)

    def rs_send(way, step, piece):
        goal = at((steps - step) * (1 if way == 0 else -1))
        if (way, step - 1, piece) in rs:
            @pl.when(jnp.logical_not(corner_fresh[way]))
            def _():
                rs_add(goal, way, step - 1, piece)
        if step == steps - 1:
            @pl.when(inner_out[way])
            def _():
                rs_add(goal, 2, 2, piece)
            if piece == way:
                @pl.when(inner_in[way])
                def _():
                    rs_add(goal, 2, 0, piece)
        landing, peer = way, peers[way]
        if step < steps - 1:
            landing = jnp.where(inner_out[way], 2, way)
            peer = jnp.where(inner_out[way], beside, peer)
        rs[way, step, piece] = launch(copy_to(parts.at[goal, piece], held.at[landing, step, piece],
            rs_s.at[way, step, piece], rs_r.at[landing, step, piece], seq=peer))

    part(at(steps))
    rs_send(0, 0, 0)
    rs_send(1, 0, 1)
    q_step(3)
    far_cross(inner)
    far_feed()
    for way in (0, 1):
        part(at((steps - 1) * (1 if way == 0 else -1)))
        rs_send(way, 1, 1 - way)
    for offset in range(steps - 2, 0, -1):
        part(at(offset))
        part(at(-offset))
    part(me)
    for hop in range(3):
        side_wait(hop)
    feed_send((0, 1, 2))
    rs_send(0, 1, 0)
    rs_send(1, 1, 1)
    for step in range(2, steps):
        for piece in (0, 1):
            for way in (0, 1):
                rs_send(way, step, 1 ^ piece ^ way)
        if step == 2:
            far_cross(corner)
        feed_cross(step - 2)
    feed_cross(2)
    for c in (0, 1):
        @pl.when(inner)
        def _():
            rs_add(me, 2, 1, c)
        for way in (0, 1):
            copy_to(held.at[way, steps - 1, c], held.at[way, steps - 1, c], rs_s.at[way, steps - 1, c],
                rs_r.at[way, steps - 1, c], seq=peers[way]).wait_recv()
        rows = slice(c * hrows, (c + 1) * hrows)
        value = (parts[me, c].astype(jnp.float32) + held[0, steps - 1, c].astype(jnp.float32)
            + held[1, steps - 1, c].astype(jnp.float32))
        for i in range(0, full, 128):
            term = value[i // 128 * hrows : (i // 128 + 1) * hrows]
            hid[rows, i : i + 128] = (hid[rows, i : i + 128] + term).astype(jnp.bfloat16).astype(jnp.float32)
        term = jnp.concatenate(
            [value[base : base + trows, k * tail : (k + 1) * tail] for k in range(folds)], axis=0)
        hid[rows, full:] = (hid[rows, full:] + term).astype(jnp.bfloat16).astype(jnp.float32)
    hidden = hid[...]
    scale = lax.rsqrt(jnp.sum(hidden * hidden, axis=1, keepdims=True) / width + eps)
    normed = hidden * scale * attn_gain_ref[...].reshape(1, width)
    shard = wq.shape[1]
    for i in range(count):
        both[core, i] = normed[:, i * shard : (i + 1) * shard].astype(jnp.bfloat16)
    pair = launch(copy_to(both.at[core], both.at[core], pair_s.at[0], pair_r.at[0], pipe=other_core))

    for key in qx:
        qx[key].wait_recv()
    far_copy()[1].wait_recv()

    def project(m, columns):
        total = None
        for i in range(count):
            x = both[:, i].reshape(2 * tok_count, shard) if m is None else both[m, i]
            term = dot(x, wq[i, :, columns])
            total = term if total is None else total + term
        return total

    kv[core] = project(core, pl.ds(0, 2 * kw)).astype(jnp.bfloat16)
    along = [launch(copy_to(kv.at[core], halo.at[core], halo_s.at[0], halo_r.at[0], seq=following))]
    for i in range(0, width, 128):
        size = min(128, width - i)
        hid_t[i : i + size, :] = hid[:, i : i + size].T
    pair.wait_recv()
    kv[other_core] = project(other_core, pl.ds(0, 2 * kw)).astype(jnp.bfloat16)
    along.append(launch(copy_to(kv.at[other_core], halo.at[other_core], halo_s.at[1], halo_r.at[1], seq=following)))
    packed = project(None, pl.ds(2 * kw, qw)).astype(jnp.bfloat16)
    queries[...] = (packed * (float(HEAD_SIZE) ** -0.5)).reshape(2, tok_count, qw)

    wide = (4 * tok_count, 2 * tok_count)
    lane = lax.broadcasted_iota(jnp.int32, wide, 1)
    row = lax.rem(lax.broadcasted_iota(jnp.int32, wide, 0), tok_count)
    left = lane < tok_count
    past = jnp.where(left, lane, lane - tok_count) > row
    low = lax.broadcasted_iota(jnp.int32, (tok_count, 2 * HEAD_SIZE), 1) < HEAD_SIZE

    def stacked(tile, head):
        tile = tile.astype(jnp.float32)
        kept = jnp.where(low if head == 0 else ~low, tile, 0.0)
        turned = pltpu.roll(kept, HEAD_SIZE, 1)
        pair_of = (kept, turned) if head == 0 else (turned, kept)
        return jnp.concatenate(pair_of, axis=0).astype(jnp.bfloat16)

    tiles = qw // 128
    per_head = tiles // 2

    def attention(m, known):
        past_kv = passed[...]
        dropped = past & jnp.logical_not(known)
        for head in range(2):
            k_own = stacked(kv[m, :, :kw], head)
            v_own = stacked(kv[m, :, kw:], head)
            k_past = stacked(past_kv[:, :kw], head)
            v_past = stacked(past_kv[:, kw:], head)
            for first in range(head * per_head, (head + 1) * per_head, 4):
                some = range(first, first + 4)
                sinks = [jnp.exp(jnp.concatenate(
                    [jnp.full((tok_count, 1), sink_ref[core * 2 * tiles + 2 * t + side]) for t in some], axis=0))
                    for side in (0, 1)]
                x = jnp.concatenate([queries[m, :, t * 128 : (t + 1) * 128] for t in some], axis=0)
                score = jnp.where(past, dot(x, k_past, ((1,), (1,))), dot(x, k_own, ((1,), (1,))))
                weight = jnp.where(dropped, 0.0, jnp.exp(score))
                mass_a = jnp.sum(weight[:, :tok_count], axis=1, keepdims=True) + sinks[0]
                mass_b = jnp.sum(weight[:, tok_count:], axis=1, keepdims=True) + sinks[1]
                probs = (weight * 0.125) * jnp.where(left, 1.0 / (mass_a * 0.125), 1.0 / (mass_b * 0.125))
                result = (
                    dot(jnp.where(past, 0.0, probs).astype(jnp.bfloat16), v_own)
                    + dot(jnp.where(past, probs, 0.0).astype(jnp.bfloat16), v_past)
                ).astype(jnp.bfloat16)
                for k, t in enumerate(some):
                    mixed[m, :, t * 128 : (t + 1) * 128] = result[k * tok_count : (k + 1) * tok_count]

    share = wo.shape[2]
    last = copy_to(given, back, pair_s.at[1], pair_r.at[1], pipe=other_core)

    def output(m):
        total = None
        for i in range(steps):
            term = dot(wo[i], mixed[m, :, i * share : (i + 1) * share], ((1,), (1,)))
            total = term if total is None else total + term

        @pl.when(m == other_core)
        def _():
            given[...] = total.astype(jnp.bfloat16)
            last.start()

        @pl.when(m == core)
        def _():
            hid_t[...] = hid_t[...] + total

    early = jnp.where(me == 0, 0, other_core)
    late = 1 - early

    @pl.when(me > 0)
    def _():
        for copy in along:
            copy.wait_recv()
        passed[...] = halo[other_core]

    @pl.when(me == 0)
    def _():
        passed[...] = jnp.zeros_like(passed)
    attention(early, me > 0)
    for cond, crossing in feed_crossings:
        @pl.when(cond)
        def _():
            crossing.wait_recv()
    output(early)

    @pl.when(me == 0)
    def _():
        for copy in along:
            copy.wait_recv()
    passed[...] = halo[jnp.where(me == 0, 0, core)]
    attention(late, me >= 0)
    output(late)
    last.wait_recv()
    out_ref[...] = (hid_t[...] + back[...].astype(jnp.float32)).astype(jnp.bfloat16)
    last.wait_send()
    for _, copy in sends:
        copy.wait_send()
    far_copy()[1].wait_send()
    for cond, copy in o_sends + far_sends:
        @pl.when(cond)
        def _():
            copy.wait_send()


def whole_layer(
    tokens, routes, route_weights, moe_gain, gate_up, down_proj, attn_gain, qkv_proj,
    head_sink_logits, out_proj,
):
    count = lax.axis_size("seq")
    steps = count // 2
    tok_count, width = tokens.shape[1:]
    own = gate_up.shape[0] // 2
    half = down_proj.shape[1]
    heads = QUERY_HEADS // 2
    qw = heads * HEAD_SIZE
    kw = KEY_VALUE_HEADS * HEAD_SIZE // 2
    chunk = tok_count // 2 * width // 128
    dma = pltpu.SemaphoreType.DMA
    bf16 = jnp.bfloat16
    vm = pl.BlockSpec(memory_space=pltpu.VMEM)
    hbm = pl.BlockSpec(memory_space=pl.ANY)
    out = pl.pallas_call(
        layer_kernel,
        out_shape=jax.ShapeDtypeStruct((width, tok_count), bf16),
        in_specs=[vm] * 5 + [pl.BlockSpec(memory_space=pltpu.SMEM)] + [hbm] * 4,
        out_specs=vm,
        scratch_shapes=[
            pltpu.VMEM((count, width + E, tok_count), bf16),
            pltpu.VMEM((own, count, CAP, width), bf16),
            pltpu.VMEM((count, tok_count, tok_count), bf16),
            pltpu.VMEM(gate_up.shape, bf16),
            pltpu.VMEM(down_proj.shape, bf16),
            pltpu.VMEM((count * CAP, 2 * half), jnp.float32),
            pltpu.VMEM((2, count * CAP, half), bf16),
            pltpu.VMEM((count, own * CAP, width), bf16),
            pltpu.VMEM((count, 2, chunk, 128), bf16),
            pltpu.VMEM((3, steps, 2, chunk, 128), bf16),
            pltpu.VMEM((count, qkv_proj.shape[0], 2 * kw + qw), bf16),
            pltpu.VMEM((steps, width, out_proj.shape[0]), bf16),
            pltpu.VMEM((2, count, tok_count, qkv_proj.shape[0]), bf16),
            pltpu.VMEM((2, tok_count, 2 * kw), bf16),
            pltpu.VMEM((2, tok_count, 2 * kw), bf16),
            pltpu.VMEM((2, tok_count, qw), bf16),
            pltpu.VMEM((2, tok_count, qw), bf16),
            pltpu.VMEM((width, tok_count), bf16),
            pltpu.VMEM((width, tok_count), bf16),
            pltpu.VMEM((tok_count, width), jnp.float32),
            pltpu.VMEM((width, tok_count), jnp.float32),
            pltpu.VMEM((tok_count, 2 * kw), bf16),
            dma((2 * own,)), dma((2 * own,)), dma((3,)), dma((1,)),
            dma((2, steps, 2)), dma((2, steps, 2)), dma((2, steps, 2)), dma((3, steps, 2)),
            dma((2, steps)), dma((2, steps)), dma((2, steps)), dma((2, steps)),
            dma((2, steps)), dma((2, steps)), dma((2, steps)), dma((2, steps)),
            dma((2,)), dma((1,)), dma((1,)), dma((1,)),
            dma((3,)), dma((3,)), dma((3,)), dma((3,)), dma((3,)), dma((3,)), dma((2,)), dma((2,)), dma((2,)), dma((2,)),
        ],
        compiler_params=pltpu.CompilerParams(
            collective_id=0, has_side_effects=True, vmem_limit_bytes=67043328),
    )(tokens[0].T, routes[0].T, route_weights[0].T, moe_gain, attn_gain, head_sink_logits,
      gate_up, down_proj, qkv_proj, out_proj.T)
    return out.T[None]


def solution(mesh):
    in_specs = (
        P("pipe", ("groups", "seq"), None),
        P("pipe", ("groups", "seq"), None),
        P("pipe", ("groups", "seq"), None),
        P(),
        P("seq", None, None),
        P("seq", None, None),
        P(),
        P("seq", None),
        P(),
        P("seq", None),
    )
    out_specs = P("pipe", ("groups", "seq"), None)
    seq_count, pipe_count, group_count = mesh.shape["seq"], mesh.shape["pipe"], mesh.shape["groups"]
    whole = (
        pipe_count == 2
        and group_count == 2
        and seq_count % 2 == 0
        and 2 * E // seq_count == 4
        and seq_count == 8
        and QUERY_HEADS % (2 * seq_count) == 0
    )
    return jax.shard_map(
        whole_layer if whole else body, mesh=mesh, in_specs=in_specs, out_specs=out_specs, check_vma=False
    )
```

```python
import functools

import jax
import jax.numpy as jnp
from jax import lax
from jax.experimental import pallas as pl
from jax.experimental.pallas import tpu as pltpu
from jax.sharding import PartitionSpec as P

MESH = pl.DeviceIdType.MESH
E = 16
TOP = 4
QUERY_HEADS = 32
KEY_VALUE_HEADS = 4
HEAD_SIZE = 64
WINDOW_SPAN = 128
HALF = 720
CAP = 48


eps = 1e-05


def from_partner(value, axis, distance):
    return lax.ppermute(value, axis, [(i, i ^ 1 << distance) for i in range(lax.axis_size(axis))])


def shifted(value, axis, steps):
    count = lax.axis_size(axis)
    pairs = [(source, (source + steps) % count) for source in range(count)]
    return lax.ppermute(value, axis, pairs)


def passed_along(value, axis, steps):
    count = lax.axis_size(axis)
    first, last = (max(0, -steps), min(count, count - steps))
    return lax.ppermute(value, axis, [(source, source + steps) for source in range(first, last)])


def rms_scale(value_matrix, gain):
    widened = value_matrix.astype(jnp.float32)
    mean_square = jnp.mean(widened * widened, axis=-1, keepdims=True)
    return (widened * lax.rsqrt(mean_square + eps) * gain).astype(jnp.bfloat16)


def slot_positions(route_rows):
    flat = route_rows.reshape(-1)
    onehot = (flat[:, None] == jnp.arange(E, dtype=jnp.int32)[None, :]).astype(jnp.int32)
    earlier = jnp.cumsum(onehot, axis=0) - onehot
    return flat * CAP + jnp.sum(earlier * onehot, axis=1)


def expert_layer(local, route_rows, route_scale, moe_gain, gate_up, down_proj):
    tok_count, width = local.shape
    seq_count = lax.axis_size("seq")
    per_device = gate_up.shape[0]
    normed = rms_scale(local, moe_gain)
    positions = slot_positions(route_rows)
    select = (positions[None, :] == jnp.arange(E * CAP, dtype=jnp.int32)[:, None]).astype(
        jnp.bfloat16
    )
    repeated = jnp.repeat(normed, TOP, axis=0)
    table = jnp.dot(select, repeated, preferred_element_type=jnp.float32).astype(jnp.bfloat16)
    by_expert = table.reshape(E, CAP, width)
    first = lax.axis_index("seq") % 2 == 0
    outgoing = jnp.repeat(by_expert, 2, axis=0).reshape(seq_count, per_device, CAP, width)
    received = lax.all_to_all(outgoing, "seq", split_axis=0, concat_axis=0, tiled=True)
    projected = jnp.einsum("spcd,pdh->spch", received, gate_up, preferred_element_type=jnp.float32)
    gate_part = projected[..., :HALF]
    up_part = projected[..., HALF:]
    hidden = (gate_part * jax.nn.sigmoid(1.702 * gate_part) * (up_part + 1.0)).astype(jnp.bfloat16)
    partial_value = jnp.einsum(
        "spch,phd->spcd", hidden, down_proj, preferred_element_type=jnp.float32
    )
    if per_device >= 2:
        finished = (
            partial_value.reshape(seq_count, per_device // 2, 2, CAP, width)
            .sum(axis=2)
            .astype(jnp.bfloat16)
        )
    else:
        lower_rows = partial_value[:, :, : CAP // 2]
        upper_rows = partial_value[:, :, CAP // 2 :]
        kept = jnp.where(first, lower_rows, upper_rows)
        given = jnp.where(first, upper_rows, lower_rows)
        partner_part = from_partner(given.astype(jnp.bfloat16), "seq", 0).astype(given.dtype)
        finished = (kept + partner_part).astype(jnp.bfloat16)
    summed = lax.all_to_all(finished, "seq", split_axis=0, concat_axis=0, tiled=True).reshape(
        E * CAP, width
    )
    picked = lax.dot_general(
        select, summed, (((0,), (0,)), ((), ())), preferred_element_type=jnp.float32
    )
    weighted = jnp.sum(picked.reshape(tok_count, TOP, width) * route_scale[:, :, None], axis=1)
    return (local.astype(jnp.float32) + weighted).astype(jnp.bfloat16)


def attend(query_matrix, keys_extended, values_extended, head_sink_logits, halo_valid):
    tok_count = query_matrix.shape[0]
    query_groups = QUERY_HEADS // KEY_VALUE_HEADS
    attention_block = min(tok_count, 512)
    scale = float(HEAD_SIZE) ** (-0.5)
    sink_mass_total = jnp.exp(head_sink_logits).reshape(KEY_VALUE_HEADS, query_groups, 1, 1)
    block_queries = query_matrix.reshape(attention_block, KEY_VALUE_HEADS, query_groups, HEAD_SIZE)
    block_keys = keys_extended.reshape(attention_block + WINDOW_SPAN, KEY_VALUE_HEADS, HEAD_SIZE)
    block_values = values_extended.reshape(
        attention_block + WINDOW_SPAN, KEY_VALUE_HEADS, HEAD_SIZE
    )
    scores = (
        jnp.einsum("qhgd,khd->hgqk", block_queries, block_keys, preferred_element_type=jnp.float32)
        * scale
    )
    query_pos = jnp.arange(attention_block, dtype=jnp.int32)[:, None] + WINDOW_SPAN
    key_pos = jnp.arange(attention_block + WINDOW_SPAN, dtype=jnp.int32)[None, :]
    distance = query_pos - key_pos
    allowed = (
        (distance >= 0) & (distance < WINDOW_SPAN) & ((key_pos + 0 >= WINDOW_SPAN) | halo_valid)
    )
    weights = jnp.where(allowed, jnp.exp(scores), 0.0)
    probs = (weights / (jnp.sum(weights, axis=-1, keepdims=True) + sink_mass_total)).astype(
        jnp.bfloat16
    )
    mixed = jnp.einsum("hgqk,khd->qhgd", probs, block_values, preferred_element_type=jnp.float32)
    outputs = mixed.reshape(attention_block, QUERY_HEADS * HEAD_SIZE).astype(jnp.bfloat16)
    return outputs


def body(
    tokens,
    routes,
    route_weights,
    moe_gain,
    gate_up,
    down_proj,
    attn_gain,
    qkv_proj,
    head_sink_logits,
    out_proj,
):
    hidden = expert_layer(tokens[0], routes[0], route_weights[0], moe_gain, gate_up, down_proj)
    tok_count, width = hidden.shape
    normed = rms_scale(hidden, attn_gain)
    seq_index = lax.axis_index("seq")
    pipe_index = lax.axis_index("pipe")
    halo_valid = (seq_index > 0) | (pipe_index > 0)
    query_width = QUERY_HEADS * HEAD_SIZE
    width_of_pair = KEY_VALUE_HEADS * HEAD_SIZE
    columns = normed
    packed_heads = jnp.dot(
        columns,
        lax.all_gather(qkv_proj, "seq", axis=0, tiled=True),
        preferred_element_type=jnp.float32,
    ).astype(jnp.bfloat16)
    from_left = shifted(packed_heads[tok_count - WINDOW_SPAN :, query_width:], "seq", 1)
    from_section = passed_along(from_left, "pipe", 1)
    halo_pairs = jnp.where(seq_index == 0, from_section, from_left)
    query_matrix = packed_heads[:, :query_width]
    pairs_ext = jnp.concatenate([halo_pairs, packed_heads[:, query_width:]], axis=0)
    keys_extended = pairs_ext[:, :width_of_pair]
    values_extended = pairs_ext[:, width_of_pair:]
    attended = attend(query_matrix, keys_extended, values_extended, head_sink_logits, halo_valid)
    columns = attended
    projected = jnp.dot(
        columns,
        lax.all_gather(out_proj, "seq", axis=0, tiled=True),
        preferred_element_type=jnp.float32,
    )
    return (hidden.astype(jnp.float32) + projected).astype(jnp.bfloat16)[None]


def ring_place(index, count, folded):
    if not folded:
        return index
    line, side = index // 2, index % 2
    return line + side * (count - 1 - 2 * line)

def ring_index(place, count, folded):
    if not folded:
        return place
    side = place // (count // 2)
    line = place + side * (count - 1 - 2 * place)
    return 2 * line + side


def copy_to(src, dst, send, recv, **device):
    return pltpu.make_async_remote_copy(src_ref=src, dst_ref=dst, send_sem=send, recv_sem=recv,
        device_id=device, device_id_type=MESH)


def dot(a, b, dims=((1,), (0,))):
    return lax.dot_general(a, b, (dims, ((), ())), preferred_element_type=jnp.float32)


def layer_kernel(
    tok_t_ref, routes_ref, weights_ref, gain_ref, attn_gain_ref, sink_ref,
    gate_up_ref, down_ref, qkv_ref, out_t_ref,
    out_ref,
    blocks, picked, combine, gu, dn, proj, act, done, parts, held, wq, wo,
    both, kv, halo, queries, mixed, given, back, hid, hid_t, passed,
    gu_sem, dn_sem, wq_sem, wo_sem, ag_s, ag_r, rs_s, rs_r, q_s, q_r, qx_s, qx_r,
    o_s, o_r, ox_s, ox_r, far_s, far_r, far_xs, far_xr, side_s, side_r, feed_s, feed_r, fx_s, fx_r, pair_s, pair_r, halo_s, halo_r,
):
    count = lax.axis_size("seq")
    steps = count // 2
    me = lax.axis_index("seq")
    core = lax.axis_index("pipe")
    group = lax.axis_index("groups")
    width, tok_count = tok_t_ref.shape
    own = picked.shape[0]
    slots = own * CAP
    place = ring_place(me, count, True)
    at = lambda offset: ring_index(lax.rem(place + offset + count, count), count, True)
    spot = lambda p: ring_index(lax.rem(p + count, count), count, True)
    peers = (at(1), at(-1))
    column = lax.rem(place, steps)
    inner = (column > 0) & (column < steps - 1)
    corner = jnp.logical_not(inner)
    low = column < steps // 2
    toward = jnp.where(low, 1, -1)
    outward = (jnp.logical_not(low), low)
    inner_out = [inner & outward[way] for way in (0, 1)]
    inner_in = [inner & jnp.logical_not(outward[way]) for way in (0, 1)]
    corner_fresh = [corner & outward[way] for way in (0, 1)]
    beside_place = count - 1 - place
    beside = spot(beside_place)
    following, preceding = lax.rem(me + 1, count), lax.rem(me + count - 1, count)
    other_core, other_group = 1 - core, 1 - group
    sends = []

    def launch(copy):
        copy.start()
        sends.append((None, copy))
        return copy

    barrier = pltpu.get_barrier_semaphore()
    for device in ({"seq": peers[0]}, {"seq": peers[1]}, {"seq": following}, {"seq": preceding},
                   {"pipe": other_core}, {"groups": other_group}, {"seq": beside}):
        pl.semaphore_signal(barrier, inc=1, device_id=device, device_id_type=MESH)
    qw, kw = queries.shape[2], kv.shape[2] // 2
    all_q = QUERY_HEADS * HEAD_SIZE
    all_k = KEY_VALUE_HEADS * HEAD_SIZE
    wo_slot = lax.rem(me, steps)
    holds = lambda origin: lax.div(origin, steps) == core
    wo_copy = pltpu.make_async_copy(out_t_ref, wo.at[wo_slot], wo_sem.at[0])

    @pl.when(holds(me))
    def _():
        wo_copy.start()

    wq_copies = []
    for i, (source, goal, size) in enumerate((
        (all_q + core * kw, 0, kw), (all_q + all_k + core * kw, kw, kw), (core * qw, 2 * kw, qw))):
        wq_copies.append(pltpu.make_async_copy(
            qkv_ref.at[:, pl.ds(pl.multiple_of(source, 128), size)],
            wq.at[me, :, pl.ds(goal, size)], wq_sem.at[i]))
    for copy in wq_copies:
        copy.start()
    gu_copies = [pltpu.make_async_copy(gate_up_ref.at[j], gu.at[j], gu_sem.at[j]) for j in range(2 * own)]
    dn_copies = [pltpu.make_async_copy(down_ref.at[j], dn.at[j], dn_sem.at[j]) for j in range(2 * own)]

    pl.semaphore_wait(barrier, 7)

    rows_all = blocks.shape[1]
    cut = (rows_all // 2 + 15) // 16 * 16
    pieces = (pl.ds(0, cut), pl.ds(cut, rows_all - cut))
    ag = {}

    def ag_send(way, step, piece):
        origin = at(-step if way == 0 else step)
        ref = blocks.at[origin, pieces[piece]]
        ag[way, step, piece] = launch(copy_to(ref, ref, ag_s.at[way, step, piece], ag_r.at[way, step, piece], seq=peers[way]))

    qcols = wq.shape[2] // 2
    q = {}
    qx = {}

    qpart = pl.ds(pl.multiple_of(group * qcols, 128), qcols)
    near = steps // 2

    def q_send(way, step):
        ref = wq.at[at(-step if way == 0 else step), :, qpart]
        q[way, step] = launch(copy_to(ref, ref, q_s.at[way, step], q_r.at[way, step], seq=peers[way]))

    def q_cross(way, step):
        q[way, step].wait_recv()
        ref = wq.at[at(-step - 1 if way == 0 else step + 1), :, qpart]
        qx[way, step] = launch(copy_to(ref, ref, qx_s.at[way, step], qx_r.at[way, step], groups=other_group))

    def q_begin():
        for way in (0, 1):
            q_send(way, 0)

    def q_step(step):
        for way in (0, 1):
            q_cross(way, step - 1)
            if step < steps - 1:
                q_send(way, step)

    far_sends = []

    def far_out(origin, kind, peer):
        ref = wq.at[origin, :, qpart]
        copy = copy_to(ref, ref, far_s.at[kind], far_r.at[0], seq=peer)

        @pl.when(inner)
        def _():
            copy.start()
        far_sends.append((inner, copy))

    def far_side():
        far_out(at(toward), 0, beside)

    def far_feed():
        far_out(at(3 * toward), 1, spot(place - toward))

    def far_copy():
        ref = wq.at[at(steps), :, qpart]
        return (copy_to(ref, ref, far_s.at[0], far_r.at[0], seq=beside),
            copy_to(ref, ref, far_xs.at[0], far_xr.at[0], groups=other_group))

    def far_cross(role):
        landed, crossing = far_copy()

        @pl.when(role)
        def _():
            landed.wait_recv()
            crossing.start()

    orows = wo.shape[1] // 2
    ocut = (orows // 2 + 15) // 16 * 16
    o_sends = []

    def o_part(way, step):
        base = pl.multiple_of(group * orows, 16)
        if step < steps - 1:
            return pl.ds(base, orows)
        return pl.ds(base, ocut) if way == 0 else pl.ds(pl.multiple_of(base + ocut, 16), orows - ocut)

    def o_copy(way, step):
        origin = at(-step if way == 0 else step)
        ref = wo.at[lax.rem(origin, steps), o_part(way, step)]
        return holds(origin), copy_to(ref, ref, o_s.at[way, step], o_r.at[way, step], seq=peers[way])

    def o_landed(way, step):
        origin = at(-step - 1 if way == 0 else step + 1)
        ref = wo.at[lax.rem(origin, steps), o_part(way, step)]
        return (holds(origin), copy_to(ref, ref, o_s.at[way, step], o_r.at[way, step], seq=peers[way]),
                copy_to(ref, ref, ox_s.at[way, step], ox_r.at[way, step], groups=other_group))

    def o_begin():
        @pl.when(holds(me))
        def _():
            wo_copy.wait()
        for way in (0, 1):
            cond, copy = o_copy(way, 0)

            @pl.when(cond)
            def _():
                copy.start()
            o_sends.append((cond, copy))

    def o_step(step):
        for way in (0, 1):
            cond, arrived, crossing = o_landed(way, step - 1)

            @pl.when(cond)
            def _():
                arrived.wait_recv()
                crossing.start()
            o_sends.append((cond, crossing))
            if step < near:
                onward, copy = o_copy(way, step)

                @pl.when(onward)
                def _():
                    copy.start()
                o_sends.append((onward, copy))

    def o_crossed(step):
        for way in (0, 1):
            cond, _, crossing = o_landed(way, step)

            @pl.when(cond)
            def _():
                crossing.wait_recv()

    def side_copy(origin, hop):
        ref = wo.at[lax.rem(origin, steps)]
        return inner & holds(origin), copy_to(ref, ref, side_s.at[hop], side_r.at[hop], seq=beside)

    def side_send(hop):
        cond, copy = side_copy(at(toward * hop), hop)

        @pl.when(cond)
        def _():
            copy.start()
        o_sends.append((cond, copy))

    def side_wait(hop):
        cond, copy = side_copy(spot(beside_place - toward * hop), hop)

        @pl.when(cond)
        def _():
            copy.wait_recv()

    feed_part = pl.ds(pl.multiple_of(group * orows, 16), orows)

    def feed_copy(origin, index):
        ref = wo.at[lax.rem(origin, steps), feed_part]
        return holds(origin), copy_to(ref, ref, feed_s.at[index], feed_r.at[index], seq=spot(place - toward))

    def feed_send(which):
        origins = (at(2 * toward), spot(beside_place - toward), spot(beside_place - 2 * toward))
        for index in which:
            origin = origins[index]
            cond, copy = feed_copy(origin, index)

            @pl.when(inner & cond)
            def _():
                copy.start()
            o_sends.append((inner & cond, copy))

    feed_crossings = []

    def feed_cross(index):
        origin = (spot(place + 3 * toward), spot(beside_place - 2 * toward), spot(beside_place - 3 * toward))[index]
        held_here, landed = feed_copy(origin, index)
        cond = corner & held_here
        ref = wo.at[lax.rem(origin, steps), feed_part]
        crossing = copy_to(ref, ref, fx_s.at[index], fx_r.at[index], groups=other_group)

        @pl.when(cond)
        def _():
            landed.wait_recv()
            crossing.start()
        o_sends.append((cond, crossing))
        feed_crossings.append((cond, crossing))

    lane_tok = lax.broadcasted_iota(jnp.int32, (tok_count, tok_count), 1)
    row_tok = lax.broadcasted_iota(jnp.int32, (tok_count, tok_count), 0)
    before = jnp.where(row_tok < lane_tok, 1.0, 0.0).astype(jnp.bfloat16)
    slot_row = lax.broadcasted_iota(jnp.int32, (tok_count, tok_count), 0).astype(jnp.float32)

    def process(n):
        table = blocks[n, width : width + E, :].astype(jnp.float32)
        present = table > 0.0
        earlier = dot(jnp.where(present, 1.0, 0.0).astype(jnp.bfloat16), before)
        slot = jnp.where(present, earlier, -1.0)
        comb = jnp.zeros((tok_count, tok_count), jnp.float32)
        for e in range(own):
            mine = expert_row == me * own + e
            slot_e = jnp.sum(jnp.where(mine, slot, 0.0), axis=0, keepdims=True)
            scale_e = jnp.sum(jnp.where(mine, table, 0.0), axis=0, keepdims=True)
            hit = (slot_row == slot_e + float(e * CAP)) & (slot_e >= 0.0)
            comb = jnp.where(hit, scale_e, comb)
        combine[n] = comb.T.astype(jnp.bfloat16)
        select = jnp.where(comb > 0.0, 1.0, 0.0).astype(jnp.bfloat16)[:slots]
        rows = dot(select, blocks[n, :width, :], ((1,), (1,))).astype(jnp.bfloat16)
        for e in range(own):
            picked[e, n] = rows[e * CAP : (e + 1) * CAP]

    o_begin()
    tall = tok_t_ref[...].astype(jnp.float32)
    scale = lax.rsqrt(jnp.sum(tall * tall, axis=0, keepdims=True) / width + eps)
    for i in range(0, width, 128):
        size = min(128, width - i)
        gain = jnp.broadcast_to(gain_ref[pl.ds(i, size)].reshape(1, size), (tok_count, size)).T
        blocks[me, i : i + size, :] = (
            tok_t_ref[i : i + size, :].astype(jnp.float32) * scale * gain
        ).astype(jnp.bfloat16)
    expert_row = lax.broadcasted_iota(jnp.int32, (E, tok_count), 0)
    dense = jnp.zeros((E, tok_count), jnp.float32)
    for j in range(TOP):
        dense = dense + jnp.where(expert_row == routes_ref[j : j + 1, :], weights_ref[j : j + 1, :], 0.0)
    blocks[me, width : width + E, :] = dense.astype(jnp.bfloat16)
    for piece in (0, 1):
        for way in (0, 1):
            ag_send(way, 0, piece ^ way)
    for copy in gu_copies[:2]:
        copy.start()
    side_send(0)
    for copy in wq_copies:
        copy.wait()
    process(me)
    for i in range(0, width, 128):
        size = min(128, width - i)
        hid[:, i : i + size] = tok_t_ref[i : i + size, :].astype(jnp.float32).T
    for step in range(1, steps):
        for piece in (0, 1):
            for way in (0, 1):
                ag[way, step - 1, piece ^ way].wait_recv()
                if step < steps - 1 or piece == 0:
                    ag_send(way, step, piece ^ way)
        if step <= near:
            o_step(step)
        else:
            q_begin()
            o_crossed(step - near - 1)
            side_send(1)
        for copy in (gu_copies[2:], dn_copies[:2], dn_copies[2:])[step - 1]:
            copy.start()
        process(at(-step))
        process(at(step))
    ag[0, steps - 1, 0].wait_recv()
    ag[1, steps - 1, 1].wait_recv()
    process(at(steps))

    o_crossed(1)
    side_send(2)
    pos = {0: 1, 1: 2, 2: 3, 3: 4}
    half = dn.shape[1]
    chunk = CAP
    for e in range(own):
        for j in (2 * e, 2 * e + 1):
            gu_copies[j].wait()
            x = picked[e].reshape(count * CAP, width)
            proj[...] = dot(x, gu[j])

            @pl.loop(0, count)
            def _(i):
                r = pl.ds(pl.multiple_of(i * chunk, 16), chunk)
                gate = proj[r, :half]
                up = proj[r, half:]
                act[j % 2, r, :] = (gate * jax.nn.sigmoid(1.702 * gate) * (up + 1.0)).astype(jnp.bfloat16)

            if j in (0, 2):
                q_step((0, 2).index(j) + 1)
                if j == 0:
                    far_side()
        dn_copies[2 * e].wait()
        dn_copies[2 * e + 1].wait()
        result = dot(act[0], dn[2 * e]) + dot(act[1], dn[2 * e + 1])
        done[:, e * CAP : (e + 1) * CAP, :] = result.astype(jnp.bfloat16).reshape(count, CAP, width)

    hrows = tok_count // 2
    tail = width % 128
    full = width - tail
    folds = 128 // tail
    trows = hrows // folds
    base = hrows * (full // 128)

    def part(n):
        value = dot(combine[n][:, :slots], done[n])
        for c in (0, 1):
            rows = value[c * hrows : (c + 1) * hrows]
            for i in range(0, full, 128):
                parts[n, c, i // 128 * hrows : (i // 128 + 1) * hrows, :] = rows[:, i : i + 128].astype(jnp.bfloat16)
            parts[n, c, base : base + trows, :] = jnp.concatenate(
                [rows[k * trows : (k + 1) * trows, full:] for k in range(folds)], axis=1
            ).astype(jnp.bfloat16)

    rs = {}

    def rs_add(goal, way, step, piece):
        here = held.at[way, step, piece]
        copy_to(here, here, rs_s.at[0, step, piece], rs_r.at[way, step, piece], seq=peers[0]).wait_recv()
        parts[goal, piece] = (
            parts[goal, piece].astype(jnp.float32) + held[way, step, piece].astype(jnp.float32)
        ).astype(jnp.bfloat16)

    def rs_send(way, step, piece):
        goal = at((steps - step) * (1 if way == 0 else -1))
        if (way, step - 1, piece) in rs:
            @pl.when(jnp.logical_not(corner_fresh[way]))
            def _():
                rs_add(goal, way, step - 1, piece)
        if step == steps - 1:
            @pl.when(inner_out[way])
            def _():
                rs_add(goal, 2, 2, piece)
            if piece == way:
                @pl.when(inner_in[way])
                def _():
                    rs_add(goal, 2, 0, piece)
        landing, peer = way, peers[way]
        if step < steps - 1:
            landing = jnp.where(inner_out[way], 2, way)
            peer = jnp.where(inner_out[way], beside, peer)
        rs[way, step, piece] = launch(copy_to(parts.at[goal, piece], held.at[landing, step, piece],
            rs_s.at[way, step, piece], rs_r.at[landing, step, piece], seq=peer))

    part(at(steps))
    rs_send(0, 0, 0)
    rs_send(1, 0, 1)
    q_step(3)
    far_cross(inner)
    far_feed()
    for hop in range(3):
        side_wait(hop)
    feed_send((0, 1, 2))
    for way in (0, 1):
        part(at((steps - 1) * (1 if way == 0 else -1)))
        rs_send(way, 1, 1 - way)
    for offset in range(steps - 2, 0, -1):
        part(at(offset))
        part(at(-offset))
    part(me)
    rs_send(0, 1, 0)
    rs_send(1, 1, 1)
    for step in range(2, steps):
        for piece in (0, 1):
            for way in (0, 1):
                rs_send(way, step, 1 ^ piece ^ way)
        if step == 2:
            far_cross(corner)
        feed_cross(step - 2)
    feed_cross(2)
    for c in (0, 1):
        @pl.when(inner)
        def _():
            rs_add(me, 2, 1, c)
        for way in (0, 1):
            copy_to(held.at[way, steps - 1, c], held.at[way, steps - 1, c], rs_s.at[way, steps - 1, c],
                rs_r.at[way, steps - 1, c], seq=peers[way]).wait_recv()
        rows = slice(c * hrows, (c + 1) * hrows)
        value = (parts[me, c].astype(jnp.float32) + held[0, steps - 1, c].astype(jnp.float32)
            + held[1, steps - 1, c].astype(jnp.float32))
        for i in range(0, full, 128):
            term = value[i // 128 * hrows : (i // 128 + 1) * hrows]
            hid[rows, i : i + 128] = (hid[rows, i : i + 128] + term).astype(jnp.bfloat16).astype(jnp.float32)
        term = jnp.concatenate(
            [value[base : base + trows, k * tail : (k + 1) * tail] for k in range(folds)], axis=0)
        hid[rows, full:] = (hid[rows, full:] + term).astype(jnp.bfloat16).astype(jnp.float32)
    hidden = hid[...]
    scale = lax.rsqrt(jnp.sum(hidden * hidden, axis=1, keepdims=True) / width + eps)
    normed = hidden * scale * attn_gain_ref[...].reshape(1, width)
    shard = wq.shape[1]
    for i in range(count):
        both[core, i] = normed[:, i * shard : (i + 1) * shard].astype(jnp.bfloat16)
    pair = launch(copy_to(both.at[core], both.at[core], pair_s.at[0], pair_r.at[0], pipe=other_core))

    for key in qx:
        qx[key].wait_recv()
    far_copy()[1].wait_recv()

    def project(m, columns):
        total = None
        for i in range(count):
            x = both[:, i].reshape(2 * tok_count, shard) if m is None else both[m, i]
            term = dot(x, wq[i, :, columns])
            total = term if total is None else total + term
        return total

    kv[core] = project(core, pl.ds(0, 2 * kw)).astype(jnp.bfloat16)
    along = [launch(copy_to(kv.at[core], halo.at[core], halo_s.at[0], halo_r.at[0], seq=following))]
    for i in range(0, width, 128):
        size = min(128, width - i)
        hid_t[i : i + size, :] = hid[:, i : i + size].T
    pair.wait_recv()
    kv[other_core] = project(other_core, pl.ds(0, 2 * kw)).astype(jnp.bfloat16)
    along.append(launch(copy_to(kv.at[other_core], halo.at[other_core], halo_s.at[1], halo_r.at[1], seq=following)))
    packed = project(None, pl.ds(2 * kw, qw)).astype(jnp.bfloat16)
    queries[...] = (packed * (float(HEAD_SIZE) ** -0.5)).reshape(2, tok_count, qw)

    wide = (4 * tok_count, 2 * tok_count)
    lane = lax.broadcasted_iota(jnp.int32, wide, 1)
    row = lax.rem(lax.broadcasted_iota(jnp.int32, wide, 0), tok_count)
    left = lane < tok_count
    past = jnp.where(left, lane, lane - tok_count) > row
    low = lax.broadcasted_iota(jnp.int32, (tok_count, 2 * HEAD_SIZE), 1) < HEAD_SIZE

    def stacked(tile, head):
        tile = tile.astype(jnp.float32)
        kept = jnp.where(low if head == 0 else ~low, tile, 0.0)
        turned = pltpu.roll(kept, HEAD_SIZE, 1)
        pair_of = (kept, turned) if head == 0 else (turned, kept)
        return jnp.concatenate(pair_of, axis=0).astype(jnp.bfloat16)

    tiles = qw // 128
    per_head = tiles // 2

    def attention(m, known):
        past_kv = passed[...]
        dropped = past & jnp.logical_not(known)
        for head in range(2):
            k_own = stacked(kv[m, :, :kw], head)
            v_own = stacked(kv[m, :, kw:], head)
            k_past = stacked(past_kv[:, :kw], head)
            v_past = stacked(past_kv[:, kw:], head)
            for first in range(head * per_head, (head + 1) * per_head, 4):
                some = range(first, first + 4)
                sinks = [jnp.exp(jnp.concatenate(
                    [jnp.full((tok_count, 1), sink_ref[core * 2 * tiles + 2 * t + side]) for t in some], axis=0))
                    for side in (0, 1)]
                x = jnp.concatenate([queries[m, :, t * 128 : (t + 1) * 128] for t in some], axis=0)
                score = jnp.where(past, dot(x, k_past, ((1,), (1,))), dot(x, k_own, ((1,), (1,))))
                weight = jnp.where(dropped, 0.0, jnp.exp(score))
                mass_a = jnp.sum(weight[:, :tok_count], axis=1, keepdims=True) + sinks[0]
                mass_b = jnp.sum(weight[:, tok_count:], axis=1, keepdims=True) + sinks[1]
                probs = (weight * 0.125) * jnp.where(left, 1.0 / (mass_a * 0.125), 1.0 / (mass_b * 0.125))
                result = (
                    dot(jnp.where(past, 0.0, probs).astype(jnp.bfloat16), v_own)
                    + dot(jnp.where(past, probs, 0.0).astype(jnp.bfloat16), v_past)
                ).astype(jnp.bfloat16)
                for k, t in enumerate(some):
                    mixed[m, :, t * 128 : (t + 1) * 128] = result[k * tok_count : (k + 1) * tok_count]

    share = wo.shape[2]
    last = copy_to(given, back, pair_s.at[1], pair_r.at[1], pipe=other_core)

    def output(m):
        total = None
        for i in range(steps):
            term = dot(wo[i], mixed[m, :, i * share : (i + 1) * share], ((1,), (1,)))
            total = term if total is None else total + term

        @pl.when(m == other_core)
        def _():
            given[...] = total.astype(jnp.bfloat16)
            last.start()

        @pl.when(m == core)
        def _():
            hid_t[...] = hid_t[...] + total

    early = jnp.where(me == 0, 0, other_core)
    late = 1 - early

    @pl.when(me > 0)
    def _():
        for copy in along:
            copy.wait_recv()
        passed[...] = halo[other_core]

    @pl.when(me == 0)
    def _():
        passed[...] = jnp.zeros_like(passed)
    attention(early, me > 0)
    for cond, crossing in feed_crossings:
        @pl.when(cond)
        def _():
            crossing.wait_recv()
    output(early)

    @pl.when(me == 0)
    def _():
        for copy in along:
            copy.wait_recv()
    passed[...] = halo[jnp.where(me == 0, 0, core)]
    attention(late, me >= 0)
    output(late)
    last.wait_recv()
    out_ref[...] = (hid_t[...] + back[...].astype(jnp.float32)).astype(jnp.bfloat16)
    last.wait_send()
    for _, copy in sends:
        copy.wait_send()
    far_copy()[1].wait_send()
    for cond, copy in o_sends + far_sends:
        @pl.when(cond)
        def _():
            copy.wait_send()


def whole_layer(
    tokens, routes, route_weights, moe_gain, gate_up, down_proj, attn_gain, qkv_proj,
    head_sink_logits, out_proj,
):
    count = lax.axis_size("seq")
    steps = count // 2
    tok_count, width = tokens.shape[1:]
    own = gate_up.shape[0] // 2
    half = down_proj.shape[1]
    heads = QUERY_HEADS // 2
    qw = heads * HEAD_SIZE
    kw = KEY_VALUE_HEADS * HEAD_SIZE // 2
    chunk = tok_count // 2 * width // 128
    dma = pltpu.SemaphoreType.DMA
    bf16 = jnp.bfloat16
    vm = pl.BlockSpec(memory_space=pltpu.VMEM)
    hbm = pl.BlockSpec(memory_space=pl.ANY)
    out = pl.pallas_call(
        layer_kernel,
        out_shape=jax.ShapeDtypeStruct((width, tok_count), bf16),
        in_specs=[vm] * 5 + [pl.BlockSpec(memory_space=pltpu.SMEM)] + [hbm] * 4,
        out_specs=vm,
        scratch_shapes=[
            pltpu.VMEM((count, width + E, tok_count), bf16),
            pltpu.VMEM((own, count, CAP, width), bf16),
            pltpu.VMEM((count, tok_count, tok_count), bf16),
            pltpu.VMEM(gate_up.shape, bf16),
            pltpu.VMEM(down_proj.shape, bf16),
            pltpu.VMEM((count * CAP, 2 * half), jnp.float32),
            pltpu.VMEM((2, count * CAP, half), bf16),
            pltpu.VMEM((count, own * CAP, width), bf16),
            pltpu.VMEM((count, 2, chunk, 128), bf16),
            pltpu.VMEM((3, steps, 2, chunk, 128), bf16),
            pltpu.VMEM((count, qkv_proj.shape[0], 2 * kw + qw), bf16),
            pltpu.VMEM((steps, width, out_proj.shape[0]), bf16),
            pltpu.VMEM((2, count, tok_count, qkv_proj.shape[0]), bf16),
            pltpu.VMEM((2, tok_count, 2 * kw), bf16),
            pltpu.VMEM((2, tok_count, 2 * kw), bf16),
            pltpu.VMEM((2, tok_count, qw), bf16),
            pltpu.VMEM((2, tok_count, qw), bf16),
            pltpu.VMEM((width, tok_count), bf16),
            pltpu.VMEM((width, tok_count), bf16),
            pltpu.VMEM((tok_count, width), jnp.float32),
            pltpu.VMEM((width, tok_count), jnp.float32),
            pltpu.VMEM((tok_count, 2 * kw), bf16),
            dma((2 * own,)), dma((2 * own,)), dma((3,)), dma((1,)),
            dma((2, steps, 2)), dma((2, steps, 2)), dma((2, steps, 2)), dma((3, steps, 2)),
            dma((2, steps)), dma((2, steps)), dma((2, steps)), dma((2, steps)),
            dma((2, steps)), dma((2, steps)), dma((2, steps)), dma((2, steps)),
            dma((2,)), dma((1,)), dma((1,)), dma((1,)),
            dma((3,)), dma((3,)), dma((3,)), dma((3,)), dma((3,)), dma((3,)), dma((2,)), dma((2,)), dma((2,)), dma((2,)),
        ],
        compiler_params=pltpu.CompilerParams(
            collective_id=0, has_side_effects=True, vmem_limit_bytes=67043328),
    )(tokens[0].T, routes[0].T, route_weights[0].T, moe_gain, attn_gain, head_sink_logits,
      gate_up, down_proj, qkv_proj, out_proj.T)
    return out.T[None]


def solution(mesh):
    in_specs = (
        P("pipe", ("groups", "seq"), None),
        P("pipe", ("groups", "seq"), None),
        P("pipe", ("groups", "seq"), None),
        P(),
        P("seq", None, None),
        P("seq", None, None),
        P(),
        P("seq", None),
        P(),
        P("seq", None),
    )
    out_specs = P("pipe", ("groups", "seq"), None)
    seq_count, pipe_count, group_count = mesh.shape["seq"], mesh.shape["pipe"], mesh.shape["groups"]
    whole = (
        pipe_count == 2
        and group_count == 2
        and seq_count % 2 == 0
        and 2 * E // seq_count == 4
        and seq_count == 8
        and QUERY_HEADS % (2 * seq_count) == 0
    )
    return jax.shard_map(
        whole_layer if whole else body, mesh=mesh, in_specs=in_specs, out_specs=out_specs, check_vma=False
    )
```
